32 devices in a mesh: groups: 2 (over y), shot: 4 (over z), rcv: 2 (over x), rep: 2 (over core).
Axes of the slice: x: 2, y: 2, z: 4, core: 2. Of those that a mesh axis runs over, the one named last changes fastest.
Arguments:
- records: float32 [64, 131072], P(('groups', 'rcv'), ('shot', 'rep')), parts along dimension 0, may hold values from -6 to 6
- offsets: int32 [16, 32], P(('groups', 'shot', 'rep')), parts along dimension 0, may hold values from 0 to 130560, as said below
- filter_index: int32 [16, 32], P(('groups', 'shot', 'rep')), parts along dimension 0, may hold values from 0 to 7
- signatures: bfloat16 [8, 128], replicated, may hold values from -0.5 to 0.5
- thresholds: float32 [2, 256], replicated, may hold values from 0.3 to 2
Outputs:
- model_field: float32 [16, 32, 32, 512], P(('groups', 'shot', 'rep'), 'rcv'), parts along dimension 0
- residual: float32 [64, 131072], P(('groups', 'rcv'), ('shot', 'rep')), parts along dimension 0
The draws below stay inside these ranges and needn't reach their ends.
There are 2 independent parts, one for each index of `groups`. The reference program is written for one: setup_inputs(seed, part) draws one part's arguments, and reference() takes and returns one part's arrays. A program takes and returns all parts, laid end to end along the dimension named above; an argument that names none is the same for every part. Nothing has to cross between parts.
Inputs may be any that keep to these rules, and one draw needn't show every extreme that they name: Every offset is a multiple of 128. Shot (x,y) starts in slab offsets[x,y] // 16384; within one row x of the shot grid at most 8 shots start in any one slab, and this bound is reached in every row. Every shot ends inside the record.
All inputs are finite; a program needn't handle non-finite values.
Results may differ from the reference program's by a relative error of at most 0.024.
Values may be sent and summed in bfloat16 or wider, within the bound.
A program may use at most 64 MiB of HBM per device.

```python
import math
import jax
import jax.numpy as jnp
from jax import lax

NR = 32
SY = 32
NT = 512
BLOCK = 128
NSIG = 8
ITERS = 2
SLABB = 128
NSLAB = 8
SX = 8
CAP = 8
L = 131072
FB = 256


def draw_offsets(key, part):
    hot_owners = jax.random.permutation(jax.random.fold_in(key, 101), NSLAB)[:2]
    slot_owner = jnp.arange(NSLAB * CAP, dtype=jnp.int32) // CAP
    is_hot = jnp.any(slot_owner[:, None] == hot_owners[None, :], axis=1)

    def one_row(row_number):
        row_key = jax.random.fold_in(key, row_number)
        scores = jax.random.permutation(jax.random.fold_in(row_key, 1), NSLAB * CAP)
        scores = scores + jnp.where(is_hot, 0, NSLAB * CAP)
        chosen = slot_owner[jnp.argsort(scores)[:SY]]
        owners = chosen[jax.random.permutation(jax.random.fold_in(row_key, 2), SY)]
        within = jax.random.randint(jax.random.fold_in(row_key, 3), (SY,), 0, SLABB)
        within = jnp.where(owners == NSLAB - 1, within % (SLABB - NT // BLOCK + 1), within)
        return ((owners * SLABB + within) * BLOCK).astype(jnp.int32)
    return jax.vmap(one_row)(jnp.arange(SX))


def set_ends(drawn, stream_key, least, largest):
    index_at = [jax.random.randint(jax.random.fold_in(stream_key, axis), (), 0, length) for axis, length in enumerate(drawn.shape)]
    widest = drawn.shape.index(max(drawn.shape))
    neighbour = index_at[:widest] + [(index_at[widest] + 1) % drawn.shape[widest]] + index_at[widest + 1:]
    return drawn.at[tuple(index_at)].set(least).at[tuple(neighbour)].set(largest)


def level_of(own_key, dims, cuts, smallest, largest):
    def one(dim, parts):
        steps = jax.random.uniform(jax.random.fold_in(jax.random.fold_in(own_key, 6), dim), (parts,), jnp.float32, smallest / len(cuts), largest / len(cuts))
        return jnp.repeat(jnp.exp(steps), dims[dim] // parts).reshape((-1,) + (1,) * (len(dims) - dim - 1))

    factor_of = one(*cuts[0])
    for cut in cuts[1:]:
        factor_of = factor_of * one(*cut)
    return factor_of


def gaussian(own_key, extent, scale, bound, cuts=(), held_as=jnp.bfloat16):
    entries = scale * jax.random.normal(own_key, extent, jnp.float32)
    if cuts:
        entries = entries * level_of(own_key, extent, cuts, -0.22, 0.18)
    return jnp.clip(entries, -bound, bound).astype(held_as)


def setup_inputs(seed: int = 0, part: int = 0) -> dict:
    key_of = jax.random.split(jax.random.key(seed), 6)
    part_splits = jax.random.split(jax.random.fold_in(key_of[5], part), 6)
    return {
        "records": gaussian(part_splits[0], (NR, L), 1.0, 6.0, ((0, 2), (1, 8)), jnp.float32),
        "offsets": draw_offsets(jax.random.fold_in(jax.random.fold_in(key_of[5], part), 71), part),
        "filter_index": set_ends(jax.random.randint(part_splits[2], (SX, SY), 0, NSIG), jax.random.fold_in(part_splits[2], 1), 0, NSIG - 1).astype(jnp.int32),
        "signatures": gaussian(key_of[3], (NSIG, BLOCK), BLOCK ** -0.5, 0.5),
        "thresholds": jnp.clip(jnp.exp(jax.random.uniform(key_of[4], (ITERS, FB), jnp.float32, math.log(0.3), math.log(2.0))), 0.3, 2.0),
    }


def time_table(count):
    samples = jnp.arange(count)
    bin_index = jnp.arange(count // 2)[:, None]
    angles = 2.0 * math.pi / count * (bin_index * samples[None, :] % count).astype(jnp.float32)
    parity = jnp.where(samples % 2 == 0, 1.0, -1.0).astype(jnp.float32)
    cosine = jnp.where(bin_index == 0, math.sqrt(1.0 / count), math.sqrt(2.0 / count)) * jnp.cos(angles)
    sine_part = jnp.where(bin_index == 0, math.sqrt(1.0 / count) * parity[None, :], -math.sqrt(2.0 / count) * jnp.sin(angles))
    return jnp.stack([cosine, sine_part]).astype(jnp.bfloat16)

def shot_table(count):
    positions = jnp.arange(count)
    angles = 2.0 * math.pi / count * (positions[:, None] * positions[None, :] % count).astype(jnp.float32)
    scaling = 1.0 / math.sqrt(count)
    cosine = scaling * jnp.cos(angles)
    sine_part = scaling * jnp.sin(angles)
    upper_half = jnp.stack([cosine, sine_part], axis=1)
    lower_half = jnp.stack([-sine_part, cosine], axis=1)
    return jnp.stack([upper_half, lower_half]).astype(jnp.bfloat16)

def toeplitz_pair(shot_taps):
    tap_count = shot_taps.shape[1]
    row_index = jnp.arange(tap_count)[:, None]
    col_index = jnp.arange(tap_count)[None, :]
    full_table = shot_taps[:, (row_index - col_index) % tap_count]
    zero_table = jnp.zeros_like(full_table)
    return (jnp.where(row_index >= col_index, full_table, zero_table), jnp.where(row_index < col_index, full_table, zero_table))

def rounded(values):
    return lax.optimization_barrier(values.astype(jnp.bfloat16)).astype(jnp.float32)

def filter_forward(traces, shot_taps):
    lower_part, upper_part = toeplitz_pair(shot_taps)
    tap_count = shot_taps.shape[1]
    blocks = traces.reshape(traces.shape[0], traces.shape[1], -1, tap_count).astype(jnp.float32)
    earlier = jnp.concatenate([jnp.zeros_like(blocks[:, :, :1]), blocks[:, :, :-1]], axis=2)
    high = lax.Precision.HIGHEST
    result = jnp.einsum('spq,rsbq->rsbp', lower_part.astype(jnp.float32), blocks, precision=high)
    result = result + jnp.einsum('spq,rsbq->rsbp', upper_part.astype(jnp.float32), earlier, precision=high)
    return result.reshape(traces.shape)

def filter_adjoint(traces, shot_taps):
    lower_part, upper_part = toeplitz_pair(shot_taps)
    tap_count = shot_taps.shape[1]
    blocks = traces.reshape(traces.shape[0], traces.shape[1], -1, tap_count).astype(jnp.float32)
    later_blocks = jnp.concatenate([blocks[:, :, 1:], jnp.zeros_like(blocks[:, :, :1])], axis=2)
    high = lax.Precision.HIGHEST
    result = jnp.einsum('spq,rsbp->rsbq', lower_part.astype(jnp.float32), blocks, precision=high)
    result = result + jnp.einsum('spq,rsbp->rsbq', upper_part.astype(jnp.float32), later_blocks, precision=high)
    return result.reshape(traces.shape)

def reference(records, offsets, filter_index, signatures, thresholds):
    high = lax.Precision.HIGHEST
    shot_taps = signatures[filter_index]
    sample_range = jnp.arange(NT, dtype=jnp.int32)
    table_time = time_table(NT).astype(jnp.float32)
    table_x = shot_table(SX).astype(jnp.float32)
    table_y = shot_table(SY).astype(jnp.float32)
    table_r = shot_table(NR).astype(jnp.float32)

    def correlate(record_field):
        record_low = record_field.astype(jnp.bfloat16)

        def one_row(inputs):
            row_offsets, row_taps = inputs
            window = record_low[:, row_offsets[:, None] + sample_range[None, :]]
            return filter_adjoint(window, row_taps)
        return lax.map(one_row, (offsets, shot_taps))

    def blend(field_data):
        field_low = field_data.astype(jnp.bfloat16)

        def one_row(record_total, inputs):
            row_field, row_offsets, row_taps = inputs
            shots = rounded(filter_forward(row_field, row_taps))
            record_total = record_total.at[:, row_offsets[:, None] + sample_range[None, :]].add(shots)
            return (record_total, None)
        record_total, _ = lax.scan(one_row, jnp.zeros((NR, L), jnp.float32), (field_low, offsets, shot_taps))
        return record_total

    def shrink(field_data, level_index):
        section_data = rounded(jnp.einsum('ckt,xryt->ckxry', table_time, rounded(field_data), precision=high))
        section_data = rounded(jnp.einsum('akbx,bfxry->afkry', table_x, section_data, precision=high))
        section_data = rounded(jnp.einsum('ajby,bfkry->afkrj', table_y, section_data, precision=high))
        coefficients = jnp.einsum('aqbr,bfkrj->afkqj', table_r, section_data, precision=high)
        magnitude = jnp.sqrt(coefficients[0] * coefficients[0] + coefficients[1] * coefficients[1])
        threshold_row = thresholds[level_index][:, None, None, None]
        factor = 1.0 - threshold_row / jnp.maximum(magnitude, threshold_row)
        section_data = rounded(coefficients * factor[None])
        section_data = rounded(jnp.einsum('aqbr,afkqj->bfkrj', table_r, section_data, precision=high))
        section_data = rounded(jnp.einsum('ajby,afkrj->bfkry', table_y, section_data, precision=high))
        section_data = rounded(jnp.einsum('akbx,afkry->bfxry', table_x, section_data, precision=high))
        return jnp.einsum('ckt,ckxry->xryt', table_time, section_data, precision=high)
    model_field = shrink(correlate(records), 0)
    residual = records
    for level_index in range(1, ITERS):
        residual = records - blend(model_field)
        model_field = shrink(model_field + correlate(residual), level_index)
    return (model_field, residual)
```

```python
import functools
import math

import jax
import jax.numpy as jnp
import numpy as np
from jax import lax
from jax.experimental import pallas as pl
from jax.experimental.pallas import tpu as pltpu
from jax.sharding import PartitionSpec as P

NT = 512


def from_behind(value, axis, steps):
    count = lax.axis_size(axis)
    first, last = (max(0, -steps), min(count, count - steps))
    return lax.ppermute(value, axis, [(source, source + steps) for source in range(first, last)])


def time_table(count):
    samples = jnp.arange(count)
    bin_index = jnp.arange(count // 2)[:, None]
    angles = 2.0 * math.pi / count * (bin_index * samples[None, :] % count).astype(jnp.float32)
    parity = jnp.where(samples % 2 == 0, 1.0, -1.0).astype(jnp.float32)
    cosine = jnp.where(bin_index == 0, math.sqrt(1.0 / count), math.sqrt(2.0 / count)) * jnp.cos(
        angles
    )
    sine_part = jnp.where(
        bin_index == 0,
        math.sqrt(1.0 / count) * parity[None, :],
        -math.sqrt(2.0 / count) * jnp.sin(angles),
    )
    return jnp.stack([cosine, sine_part]).astype(jnp.bfloat16)


def shot_table(count):
    positions = jnp.arange(count)
    angles = (
        2.0
        * math.pi
        / count
        * (positions[:, None] * positions[None, :] % count).astype(jnp.float32)
    )
    scaling = 1.0 / math.sqrt(count)
    cosine = scaling * jnp.cos(angles)
    sine_part = scaling * jnp.sin(angles)
    upper_half = jnp.stack([cosine, sine_part], axis=1)
    lower_half = jnp.stack([-sine_part, cosine], axis=1)
    return jnp.stack([upper_half, lower_half]).astype(jnp.bfloat16)


def toeplitz_kernel(adjoint, taps_ref, out_ref):
    tap_count = taps_ref.shape[1]
    row_index = lax.broadcasted_iota(jnp.int32, (tap_count, tap_count), 0)
    col_index = lax.broadcasted_iota(jnp.int32, (tap_count, tap_count), 1)
    taps = taps_ref[...].astype(jnp.float32)
    for index in range(taps_ref.shape[0]):
        row = jnp.broadcast_to(taps[index : index + 1, :], (tap_count, tap_count))
        turned = pltpu.roll(row, 0, 1, stride=1, stride_axis=0)
        zeros = jnp.zeros_like(turned)
        near = jnp.where(col_index >= row_index, turned, zeros)
        far = jnp.where(col_index < row_index, turned, zeros)
        near, far = (near.T, far.T) if adjoint else (near, far)
        out_ref[index, :tap_count, :] = near.astype(jnp.bfloat16)
        out_ref[index, tap_count:, :] = far.astype(jnp.bfloat16)


def toeplitz_table(signatures, adjoint):
    count, tap_count = signatures.shape
    return pl.pallas_call(
        functools.partial(toeplitz_kernel, adjoint),
        out_shape=jax.ShapeDtypeStruct((count, 2 * tap_count, tap_count), jnp.bfloat16),
        in_specs=[pl.BlockSpec(memory_space=pltpu.VMEM)],
        out_specs=pl.BlockSpec(memory_space=pltpu.VMEM),
    )(signatures)


def apply_filter(traces, table, adjoint):
    empty = jnp.zeros_like(traces[:, :1])
    if adjoint:
        other = jnp.concatenate([traces[:, 1:], empty], axis=1)
    else:
        other = jnp.concatenate([empty, traces[:, :-1]], axis=1)
    return jnp.einsum(
        "sbrp,spq->sbrq",
        jnp.concatenate([traces, other], axis=3),
        table,
        preferred_element_type=jnp.float32,
    )


def rank_in_row(owners):
    shot_count = owners.shape[1]
    same_owner = owners[:, :, None] == owners[:, None, :]
    earlier = jnp.arange(shot_count)[None, :] < jnp.arange(shot_count)[:, None]
    return jnp.sum(same_owner & earlier[None], axis=2)


def to_slabs(payload):
    return lax.all_to_all(payload, ("shot", "rep"), split_axis=0, concat_axis=0, tiled=True)


def to_shots(payload):
    return lax.all_to_all(payload, ("shot", "rep"), split_axis=0, concat_axis=0, tiled=True)


def soft_limit(coefficients, threshold_row):
    magnitude = jnp.sqrt(coefficients[0] * coefficients[0] + coefficients[1] * coefficients[1])
    threshold_view = threshold_row[None, :, None, None]
    factor = 1.0 - threshold_view / jnp.maximum(magnitude, threshold_view)
    return (coefficients * factor[None]).astype(jnp.bfloat16)


def shrink(field_data, threshold_row, tables):
    table_time, table_x, table_y, table_r = tables
    rows_here, local_rcv, shot_count, sample_count = field_data.shape
    spectrum = jnp.einsum(
        "ckt,xryt->xckry",
        table_time,
        field_data.astype(jnp.bfloat16),
        preferred_element_type=jnp.float32,
    ).astype(jnp.bfloat16)
    bin_count = spectrum.shape[2]
    spectrum = spectrum.reshape(rows_here, 2, bin_count, local_rcv * shot_count)
    section_data = jnp.einsum(
        "akbx,xbfz->akfz",
        table_x,
        lax.all_to_all(spectrum, ("shot", "rep"), split_axis=2, concat_axis=0, tiled=True),
        preferred_element_type=jnp.float32,
    ).astype(jnp.bfloat16)
    all_rows, row_bins = (section_data.shape[1], section_data.shape[2])
    section_data = section_data.reshape(2, all_rows, row_bins, local_rcv, shot_count)
    section_data = lax.all_to_all(section_data, "rcv", split_axis=2, concat_axis=3, tiled=True)
    section_data = jnp.einsum(
        "ajby,bkfry->akfrj", table_y, section_data, preferred_element_type=jnp.float32
    ).astype(jnp.bfloat16)
    coefficients = jnp.einsum(
        "aqbr,bkfrj->akfqj", table_r, section_data, preferred_element_type=jnp.float32
    )
    shrunk = soft_limit(coefficients, threshold_row)
    section_data = jnp.einsum(
        "aqbr,akfqj->bkfrj", table_r, shrunk, preferred_element_type=jnp.float32
    ).astype(jnp.bfloat16)
    section_data = jnp.einsum(
        "ajby,akfrj->bkfry", table_y, section_data, preferred_element_type=jnp.float32
    ).astype(jnp.bfloat16)
    section_data = lax.all_to_all(section_data, "rcv", split_axis=3, concat_axis=2, tiled=True)
    section_data = section_data.reshape(2, all_rows, row_bins, local_rcv * shot_count)
    section_data = jnp.einsum(
        "akbx,akfz->bxfz", table_x, section_data, preferred_element_type=jnp.float32
    ).astype(jnp.bfloat16)
    result = jnp.einsum(
        "ckt,cxkz->xzt",
        table_time,
        lax.all_to_all(section_data, ("shot", "rep"), split_axis=1, concat_axis=2, tiled=True),
        preferred_element_type=jnp.float32,
    )
    return result.reshape(rows_here, local_rcv, shot_count, sample_count)


def body_by_rows(records, offsets, filter_index, signatures, thresholds):
    rows_here, shot_count = offsets.shape
    local_rcv, slab_len = records.shape
    slab_count = lax.axis_size(("shot", "rep"))
    rcv_count = lax.axis_size("rcv")
    tap_count = signatures.shape[1]
    sample_count = NT
    slab_blocks = slab_len // tap_count
    trace_blocks = sample_count // tap_count
    capacity = max(2, 2 * shot_count // slab_count)
    slot_count = slab_count * rows_here * capacity
    forward_tables = toeplitz_table(signatures, False)
    adjoint_tables = toeplitz_table(signatures, True)
    flat_index = filter_index.reshape(-1)
    forward_table = forward_tables[flat_index]
    adjoint_table = adjoint_tables[flat_index]
    owners = offsets // slab_len
    row_ids = jnp.arange(rows_here, dtype=jnp.int32)[:, None]
    slot_index = (
        owners * (rows_here * capacity) + row_ids * capacity + rank_in_row(owners)
    ).reshape(-1)
    every_offset = lax.all_gather(offsets, ("shot", "rep"), axis=0, tiled=True)
    every_owner = every_offset // slab_len
    every_start = every_offset // tap_count % slab_blocks
    every_rank = rank_in_row(every_owner)
    mine_mask = every_owner == lax.axis_index(("shot", "rep"))
    levels = jnp.arange(capacity, dtype=jnp.int32)
    picked = mine_mask[:, :, None] & (every_rank[:, :, None] == levels[None, None, :])
    table_in = jnp.sum(jnp.where(picked, every_start[:, :, None] + 1, 0), axis=1).reshape(-1)
    filled = table_in > 0
    block_steps = jnp.arange(trace_blocks, dtype=jnp.int32)
    target = jnp.where(
        filled[:, None],
        table_in[:, None] - 1 + block_steps[None, :],
        slab_blocks + trace_blocks - 1,
    )

    def correlate(record_field):
        record_low = (
            record_field.astype(jnp.bfloat16)
            .reshape(local_rcv, slab_blocks, tap_count)
            .transpose(1, 0, 2)
        )
        rim_blocks = from_behind(record_low[: trace_blocks - 1], ("shot", "rep"), -1)
        extended = jnp.concatenate(
            [record_low, rim_blocks, jnp.zeros((1, local_rcv, tap_count), jnp.bfloat16)], axis=0
        )
        windows = extended[target.reshape(-1)].reshape(
            slot_count, trace_blocks, local_rcv, tap_count
        )
        returned = to_shots(windows)
        traces = returned[slot_index]
        terms = apply_filter(traces, adjoint_table, True)
        terms = terms.reshape(rows_here, shot_count, trace_blocks, local_rcv, tap_count).transpose(
            0, 3, 1, 2, 4
        )
        return terms.reshape(rows_here, local_rcv, shot_count, sample_count)

    tables = (
        time_table(sample_count),
        shot_table(slab_count * rows_here),
        shot_table(shot_count),
        shot_table(local_rcv * rcv_count),
    )
    row_bins = sample_count // 2 // slab_count
    rcv_bins = row_bins // rcv_count
    bin_start = lax.axis_index(("shot", "rep")) * row_bins + lax.axis_index("rcv") * rcv_bins

    def threshold_for(level_index):
        return lax.dynamic_slice_in_dim(thresholds[level_index], bin_start, rcv_bins)

    model_field = shrink(correlate(records), threshold_for(0), tables)
    level_index = 1
    traces = model_field.astype(jnp.bfloat16).reshape(
        rows_here, local_rcv, shot_count, trace_blocks, tap_count
    )
    traces = traces.transpose(0, 2, 3, 1, 4).reshape(
        rows_here * shot_count, trace_blocks, local_rcv, tap_count
    )
    shots = apply_filter(traces, forward_table, False).astype(jnp.bfloat16)
    outgoing = (
        jnp.zeros((slot_count, trace_blocks, local_rcv, tap_count), jnp.bfloat16)
        .at[slot_index]
        .set(shots)
    )
    arrived = to_slabs(outgoing)
    slab_total = jnp.zeros((slab_blocks + trace_blocks, local_rcv, tap_count), jnp.float32)
    for block_step in range(trace_blocks):
        slab_total = slab_total.at[target[:, block_step]].add(
            arrived[:, block_step].astype(jnp.float32)
        )
    spill_over = slab_total[slab_blocks : slab_blocks + trace_blocks - 1]
    carried = from_behind(spill_over, ("shot", "rep"), 1)
    blended = slab_total[:slab_blocks].at[: trace_blocks - 1].add(carried)
    residual = records - blended.transpose(1, 0, 2).reshape(local_rcv, slab_len)
    model_field = shrink(model_field + correlate(residual), threshold_for(level_index), tables)
    return (model_field, residual)


def dot(left, right, left_dim=1, right_dim=0):
    return lax.dot_general(
        left, right, (((left_dim,), (right_dim,)), ((), ())), preferred_element_type=jnp.float32
    )


def fixed_time_table(count):
    samples = np.arange(count)
    bins = np.arange(count // 2)[:, None]
    angles = 2.0 * np.pi / count * (bins * samples[None, :] % count)
    scale = math.sqrt(2.0 / count)
    cosine = scale * np.cos(angles)
    sine = -scale * np.sin(angles)
    cosine[0] = math.sqrt(1.0 / count)
    sine[0] = math.sqrt(1.0 / count) * np.where(samples % 2 == 0, 1.0, -1.0)
    return np.stack([cosine, sine]).astype(jnp.bfloat16)


def fixed_shot_table(count):
    positions = np.arange(count)
    angles = 2.0 * np.pi / count * (positions[:, None] * positions[None, :] % count)
    cosine = np.cos(angles) / math.sqrt(count)
    sine = np.sin(angles) / math.sqrt(count)
    table = np.stack([np.stack([cosine, sine], 1), np.stack([-sine, cosine], 1)])
    return table.astype(jnp.bfloat16).astype(np.float32)


MESH = pl.DeviceIdType.MESH
AXES = ("shot", "rcv", "rep")


def neighbours(sizes):
    every = [(a, b, c) for a in range(sizes[0]) for b in range(sizes[1]) for c in range(sizes[2])]
    far = sizes[0] // 2
    return sorted(every[1:], key=lambda step: (abs(step[0] - far), -step[1], -step[2]))


def device_at(sizes, step):
    spot = [lax.rem(lax.axis_index(axis) + hop, size) for axis, hop, size in zip(AXES, step, sizes)]
    index = (spot[0] * sizes[1] + spot[1]) * sizes[2] + spot[2]
    return dict(zip(AXES, spot)), index


def greet(sizes):
    barrier = pltpu.get_barrier_semaphore()
    steps = neighbours(sizes)
    for step in steps:
        pl.semaphore_signal(barrier, inc=1, device_id=device_at(sizes, step)[0], device_id_type=MESH)
    pl.semaphore_wait(barrier, len(steps))


def copies(sizes, source, target, send_sem, recv_sem):
    mine = device_at(sizes, (0, 0, 0))[1]
    made = []
    for number, step in enumerate(neighbours(sizes)):
        device, index = device_at(sizes, step)
        made.append(
            pltpu.make_async_remote_copy(
                src_ref=source.at[index],
                dst_ref=target.at[mine],
                send_sem=send_sem.at[number],
                recv_sem=recv_sem.at[number],
                device_id=device,
                device_id_type=MESH,
            )
        )
    return made


def correlate_slots(starts_ref, picks_ref, blocks_ref, taps_ref, model_ref, held_ref):
    rcv, taps = blocks_ref.shape[1:]
    slots = starts_ref.shape[0]
    rows = held_ref.shape[0] // slots
    steps = rows // rcv

    def one(slot, carry):
        window = blocks_ref[pl.ds(starts_ref[slot], steps)].reshape(rows, taps)
        later = jnp.concatenate([window[rcv:], jnp.zeros((rcv, taps), window.dtype)], axis=0)
        pair = jnp.concatenate([window, later], axis=1)
        terms = dot(pair, taps_ref[picks_ref[slot]])
        where = pl.ds(pl.multiple_of(slot * rows, rows), rows)
        if model_ref is not None:
            terms = terms + model_ref[where]
        held_ref[where] = terms
        return carry

    lax.fori_loop(0, slots, one, 0, unroll=8)


def gather_traces(held_ref, traces_ref, rcv, slots):
    rows = held_ref.shape[0] // slots
    steps = rows // rcv
    for line in range(rcv):
        traces_ref[line * slots : (line + 1) * slots] = jnp.concatenate(
            [
                held_ref[pl.ds(step * rcv + line, slots, stride=rows), :].astype(jnp.bfloat16)
                for step in range(steps)
            ],
            axis=1,
        )


def spectra_chunk(table, traces_ref, out_ref, rcv, slots):
    parts, rows, lanes = out_ref.shape
    bins = rows // rcv
    half = parts * bins
    pack = max(1, 16 // bins)
    together = math.gcd(rcv, 4)
    for first in range(0, rcv, together):
        both = dot(table, traces_ref[first * slots : (first + together) * slots], 1, 1)
        for low in range(0, together, pack):
            pieces = []
            for line in range(low, low + pack):
                piece = both[:, line * slots : (line + 1) * slots]
                joined = jnp.concatenate([piece[:half], piece[half:]], axis=1)
                pieces.append(joined.reshape(parts, bins, lanes))
            out_ref[:, (first + low) * bins : (first + low + pack) * bins] = jnp.concatenate(
                pieces, axis=1
            ).astype(jnp.bfloat16)


def bins_chunk(place, halves, spectra_ref, go_ref, back_ref, cosine, sine, level, out_ref):
    _, rows, _ = spectra_ref.shape
    rcv_count, slab_count = place.shape
    joined = jnp.concatenate(
        [
            jnp.concatenate([spectra_ref[int(index)] for index in line], axis=1)
            for line in place
        ],
        axis=0,
    )
    section = dot(joined, go_ref[...]).astype(jnp.bfloat16)
    half = section.shape[1] // 2
    near = dot(cosine, section)
    far = dot(sine, section)
    real = near[:, :half] + far[:, half:]
    imag = near[:, half:] - far[:, :half]
    factor = 1.0 - level / jnp.maximum(jnp.sqrt(real * real + imag * imag), level)
    shrunk = jnp.concatenate([real * factor, imag * factor], axis=1).astype(jnp.bfloat16)
    near = dot(cosine, shrunk)
    far = dot(sine, shrunk)
    section = jnp.concatenate(
        [near[:, :half] - far[:, half:], far[:, :half] + near[:, half:]], axis=1
    ).astype(jnp.bfloat16)
    result = dot(section, back_ref[...], 1, 1).astype(jnp.bfloat16)
    width = result.shape[1] // slab_count
    for line in range(rcv_count):
        for slab in range(slab_count):
            piece = result[line * rows : (line + 1) * rows, slab * width : (slab + 1) * width]
            if halves == 2:
                piece = jnp.concatenate([piece[: rows // 2], piece[rows // 2 :]], axis=1)
            out_ref[int(place[line, slab])] = piece


def round_trip(sizes, place, halves, with_model, starts_ref, picks_ref, blocks_ref, taps_ref, table_ref, go_ref, back_ref, cosine_ref, sine_ref, level_ref, *rest):
    model_ref = rest[0] if with_model else None
    out_ref, held_ref, traces_ref, sent_ref, got_ref, answer_ref = rest[-10:-4]
    send_sems, recv_sems, back_sems, home_sems = rest[-4:]
    rcv = blocks_ref.shape[1]
    slots = starts_ref.shape[0]
    chunks = table_ref.shape[0]
    greet(sizes)
    mine = device_at(sizes, (0, 0, 0))[1]
    correlate_slots(starts_ref, picks_ref, blocks_ref, taps_ref, model_ref, held_ref)
    gather_traces(held_ref, traces_ref, rcv, slots)
    going = []
    for chunk in range(chunks):
        spectra_chunk(table_ref[chunk], traces_ref, sent_ref.at[chunk], rcv, slots)
        made = copies(
            sizes, sent_ref.at[chunk], got_ref.at[chunk], send_sems.at[chunk], recv_sems.at[chunk]
        )
        for copy in made:
            copy.start()
        got_ref[chunk, mine] = sent_ref[chunk, mine]
        going.append(made)
    coming = []
    for chunk in range(chunks):
        for copy in going[chunk]:
            copy.wait_recv()
        bins_chunk(
            place, halves, got_ref.at[chunk], go_ref, back_ref, cosine_ref[...], sine_ref[...], level_ref[chunk], answer_ref.at[chunk]
        )
        made = copies(
            sizes, answer_ref.at[chunk], out_ref.at[chunk], back_sems.at[chunk], home_sems.at[chunk]
        )
        for copy in made:
            copy.start()
        out_ref[chunk, mine] = answer_ref[chunk, mine]
        coming.append(made)
    for made in going:
        for copy in made:
            copy.wait_send()
    for made in coming:
        for copy in made:
            copy.wait()


def slots_round_trip(sizes, number, starts, picks, blocks, taps, table, go, back, cosine, sine, level, model, place, halves):
    rcv, width = blocks.shape[1:]
    chunks, _, samples = table.shape
    slots = starts.shape[0]
    parts = place.size
    bins = samples // 2 // parts // chunks
    rows = rcv * bins
    vmem = pl.BlockSpec(memory_space=pltpu.VMEM)
    smem = pl.BlockSpec(memory_space=pltpu.SMEM)
    extra = () if model is None else (model,)
    lanes = 2 * slots
    back_lanes = halves * back.shape[0] // place.shape[1]
    back_shape = (chunks, parts, rows // halves, back_lanes)
    peers = parts - 1
    return pl.pallas_call(
        functools.partial(round_trip, sizes, place, halves, model is not None),
        out_shape=jax.ShapeDtypeStruct(back_shape, jnp.bfloat16),
        in_specs=[smem, smem] + [vmem] * (8 + len(extra)),
        out_specs=vmem,
        scratch_shapes=[
            pltpu.VMEM((slots * rcv * samples // width, width), jnp.float32),
            pltpu.VMEM((rcv * slots, samples), jnp.bfloat16),
            pltpu.VMEM((chunks, parts, rows, lanes), jnp.bfloat16),
            pltpu.VMEM((chunks, parts, rows, lanes), jnp.bfloat16),
            pltpu.VMEM(back_shape, jnp.bfloat16),
        ]
        + [pltpu.SemaphoreType.DMA((chunks, peers))] * 4,
        compiler_params=pltpu.CompilerParams(collective_id=number, has_side_effects=True),
    )(starts, picks, blocks, taps, table, go, back, cosine, sine, level, *extra)


def upright(spectra_ref, chunk, lines, bins, group_lanes):
    parts = spectra_ref.shape[1]
    pack = max(1, 16 // bins)
    count = group_lanes // 2
    pieces = []
    for low_line in range(lines[0], lines[-1] + 1, pack):
        block = spectra_ref[chunk, :, low_line * bins : (low_line + pack) * bins].astype(jnp.float32)
        for line in range(pack):
            turned = block[:, line * bins : (line + 1) * bins].reshape(parts * bins, -1).T
            turned = turned.astype(jnp.bfloat16)
            for low in range(0, turned.shape[0], group_lanes):
                pieces.append(
                    jnp.concatenate(
                        [turned[low : low + count], turned[low + count : low + 2 * count]], axis=1
                    )
                )
    return jnp.concatenate(pieces, axis=0)


def synthesise(starts_ref, picks_ref, spectra_ref, taps_ref, table_ref, model_ref, total_ref):
    chunks, parts, lines_bins, lanes = spectra_ref.shape
    rcv = total_ref.shape[1]
    bins = lines_bins // rcv
    slots = lanes // 2
    taps = model_ref.shape[1]
    rows = model_ref.shape[0] // slots
    steps = rows // rcv
    together = math.gcd(rcv, 4)
    for first in range(0, rcv, together):
        lines = range(first, first + together)
        fields = sum(
            dot(upright(spectra_ref, chunk, lines, bins, lanes), table_ref[chunk])
            for chunk in range(chunks)
        )
        for line in lines:
            low = (line - first) * slots
            for step in range(steps):
                model_ref[pl.ds(step * rcv + line, slots, stride=rows), :] = fields[
                    low : low + slots, step * taps : (step + 1) * taps
                ]
    total_ref[...] = jnp.zeros_like(total_ref)

    def one(slot, carry):
        trace = model_ref[pl.ds(pl.multiple_of(slot * rows, rows), rows)].astype(jnp.bfloat16)
        earlier = jnp.concatenate([jnp.zeros((rcv, taps), trace.dtype), trace[:-rcv]], axis=0)
        pair = jnp.concatenate([trace, earlier], axis=1)
        shot = dot(pair, taps_ref[picks_ref[slot]]).astype(jnp.bfloat16).astype(jnp.float32)
        where = pl.ds(starts_ref[slot], steps)
        total_ref[where] = total_ref[where] + shot.reshape(steps, rcv, taps)
        return carry

    lax.fori_loop(0, slots, one, 0, unroll=8)


def spectra_to_slab(starts, picks, spectra, taps, table, slab_blocks, rcv):
    lanes = spectra.shape[3]
    width = taps.shape[2]
    steps = table.shape[2] // width
    vmem = pl.BlockSpec(memory_space=pltpu.VMEM)
    smem = pl.BlockSpec(memory_space=pltpu.SMEM)
    return pl.pallas_call(
        synthesise,
        out_shape=(
            jax.ShapeDtypeStruct((lanes // 2 * rcv * steps, width), jnp.float32),
            jax.ShapeDtypeStruct((slab_blocks + steps, rcv, width), jnp.float32),
        ),
        in_specs=[smem, smem, vmem, vmem, vmem],
        out_specs=(vmem, vmem),
    )(starts, picks, spectra, taps, table)


def record_kernel(groups, bins, spectra_ref, table_ref, out_ref):
    chunks, parts, rows, lanes = spectra_ref.shape
    count = out_ref.shape[2]
    together = rows // bins
    fields = sum(
        dot(upright(spectra_ref, chunk, range(together), bins, 2 * count), table_ref[chunk])
        for chunk in range(chunks)
    )
    for line in range(together):
        for group in range(groups):
            low = (line * groups + group) * count
            out_ref[group, line] = fields[low : low + count]


def records_of(spectra, table, groups, rcv):
    chunks, parts, rows, lanes = spectra.shape
    samples = table.shape[2]
    bins = rows // rcv
    count = lanes // 2 // groups
    together = math.gcd(rcv, 4)
    return pl.pallas_call(
        functools.partial(record_kernel, groups, bins),
        grid=(rcv // together,),
        out_shape=jax.ShapeDtypeStruct((groups, rcv, count, samples), jnp.float32),
        in_specs=[
            pl.BlockSpec((chunks, parts, together * bins, lanes), lambda i: (0, 0, i, 0)),
            pl.BlockSpec(table.shape, lambda i: (0, 0, 0)),
        ],
        out_specs=pl.BlockSpec((groups, together, count, samples), lambda i: (0, i, 0, 0)),
    )(spectra, table)


CHUNKS = 2


def body_by_slots(records, offsets, filter_index, signatures, thresholds):
    rows_here, shot_count = offsets.shape
    local_rcv, slab_len = records.shape
    slab_count = lax.axis_size(("shot", "rep"))
    rep_count = lax.axis_size("rep")
    rcv_count = lax.axis_size("rcv")
    sizes = tuple(lax.axis_size(axis) for axis in AXES)
    parts = slab_count * rcv_count
    tap_count = signatures.shape[1]
    slab_blocks = slab_len // tap_count
    steps = NT // tap_count
    capacity = max(2, 2 * shot_count // slab_count)
    row_count = rows_here * slab_count
    slots = row_count * capacity
    bins = NT // 2 // parts
    chunks = CHUNKS
    few = bins // chunks
    place = np.array(
        [
            [((slab // rep_count) * rcv_count + line) * rep_count + slab % rep_count for slab in range(slab_count)]
            for line in range(rcv_count)
        ]
    )

    time_table_fixed = fixed_time_table(NT).reshape(2, parts, chunks, few, NT)
    time_table_fixed = jnp.asarray(
        np.ascontiguousarray(time_table_fixed.transpose(2, 0, 1, 3, 4)).reshape(chunks, NT // chunks, NT)
    )
    table_x, table_y, table_r = (
        fixed_shot_table(count) for count in (row_count, shot_count, local_rcv * rcv_count)
    )
    grid_table = np.einsum("ajby,bkcx->cxyakj", table_y, table_x).astype(jnp.bfloat16)
    row_table = np.ascontiguousarray(grid_table.transpose(1, 0, 2, 3, 4, 5))
    points = 2 * row_count * shot_count
    grid_table = jnp.asarray(grid_table.reshape(points, points))
    row_table = jnp.asarray(row_table.reshape(points, points))
    same = np.eye(few, dtype=np.float32)
    cosine = jnp.asarray(np.kron(table_r[0, :, 0], same).astype(jnp.bfloat16))
    sine = jnp.asarray(np.kron(table_r[0, :, 1], same).astype(jnp.bfloat16))

    shots = jnp.stack([offsets, filter_index])
    every = lax.all_to_all(
        jnp.broadcast_to(shots[None], (slab_count,) + shots.shape), ("shot", "rep"), 0, 0, tiled=True
    )
    every_offset = every[:, 0].reshape(row_count, shot_count)
    every_pick = every[:, 1].reshape(row_count, shot_count)
    every_owner = every_offset // slab_len
    every_rank = rank_in_row(every_owner)
    slabs = jnp.arange(slab_count, dtype=jnp.int32)
    ranks = jnp.arange(capacity, dtype=jnp.int32)
    taken = (every_owner[None, :, None, :] == slabs[:, None, None, None]) & (
        every_rank[None, :, None, :] == ranks[None, None, :, None]
    )
    point_of = jnp.arange(row_count * shot_count, dtype=jnp.int32).reshape(row_count, shot_count)
    code = jnp.sum(jnp.where(taken, point_of[None, :, None, :] + 1, 0), axis=3).reshape(
        slab_count, 1, slots
    )
    code = jnp.where(
        code > 0, code - 1 + row_count * shot_count * jnp.arange(2, dtype=jnp.int32)[None, :, None], -1
    ).reshape(-1)
    chosen = (code[:, None] == jnp.arange(points, dtype=jnp.int32)[None, :]).astype(jnp.bfloat16)
    slot_table = dot(chosen, grid_table).astype(jnp.bfloat16)
    mine = (every_owner == lax.axis_index(("shot", "rep")))[:, None, :] & (
        every_rank[:, None, :] == ranks[None, :, None]
    )
    every_start = every_offset // tap_count % slab_blocks
    starts = jnp.sum(jnp.where(mine, every_start[:, None, :], 0), axis=2).reshape(-1)
    picks = jnp.sum(jnp.where(mine, every_pick[:, None, :], 0), axis=2).reshape(-1)
    adjoint_tables = toeplitz_table(signatures, True)
    bin_start = lax.axis_index(AXES) * bins

    def trip(number, blocks, rim, model, back, halves):
        low = blocks.astype(jnp.bfloat16)
        extended = jnp.concatenate([low, rim, jnp.zeros_like(low[:1])], axis=0)
        level = lax.dynamic_slice_in_dim(thresholds[number], bin_start, bins).reshape(chunks, 1, few)
        level = jnp.broadcast_to(level, (chunks, local_rcv * rcv_count, few)).reshape(chunks, -1, 1)
        return slots_round_trip(
            sizes, number, starts, picks, extended, adjoint_tables, time_table_fixed, slot_table, back, cosine, sine, level, model, place, halves
        )

    record_blocks = records.reshape(local_rcv, slab_blocks, tap_count).transpose(1, 0, 2)
    rim = from_behind(record_blocks[: steps - 1].astype(jnp.bfloat16), ("shot", "rep"), -1)
    spectra = trip(0, record_blocks, rim, None, slot_table, 1)
    forward_tables = toeplitz_table(signatures, False)
    model, total = spectra_to_slab(
        starts, picks, spectra, forward_tables, time_table_fixed, slab_blocks, local_rcv
    )
    spill = total[slab_blocks : slab_blocks + steps - 1]
    left = record_blocks - total[:slab_blocks]
    carried = from_behind(spill, ("shot", "rep"), 1)
    ahead = from_behind(left[: steps - 1], ("shot", "rep"), -1)
    left = left.at[: steps - 1].add(-carried)
    rim = (ahead - spill).astype(jnp.bfloat16)
    residual = left.transpose(1, 0, 2).reshape(local_rcv, slab_len)
    spectra = trip(1, left, rim, model, row_table, 2)
    model = records_of(spectra, time_table_fixed, 2, local_rcv // 2)
    return (model.reshape(rows_here, local_rcv, shot_count, NT), residual)


def body(records, offsets, filter_index, signatures, thresholds):
    rows_here, shot_count = offsets.shape
    slab_count = lax.axis_size(("shot", "rep"))
    parts = slab_count * lax.axis_size("rcv")
    slots = rows_here * slab_count * max(2, 2 * shot_count // slab_count)
    table_rows = 2 * rows_here * slab_count * shot_count
    fits = table_rows <= 1024 and rows_here == 1 and slots == 64 and 4 * shot_count == 128
    fits = fits and records.shape[0] == 16 and NT // 2 // parts == 16
    run = body_by_slots if fits else body_by_rows
    return run(records, offsets, filter_index, signatures, thresholds)


def solution(mesh):
    in_specs = (
        P(("groups", "rcv"), ("shot", "rep")),
        P(("groups", "shot", "rep"), None),
        P(("groups", "shot", "rep"), None),
        P(),
        P(),
    )
    out_specs = (
        P(("groups", "shot", "rep"), "rcv", None, None),
        P(("groups", "rcv"), ("shot", "rep")),
    )
    return jax.shard_map(body, mesh=mesh, in_specs=in_specs, out_specs=out_specs, check_vma=False)
```

```python
import functools
import math

import jax
import jax.numpy as jnp
import numpy as np
from jax import lax
from jax.experimental import pallas as pl
from jax.experimental.pallas import tpu as pltpu
from jax.sharding import PartitionSpec as P

NT = 512


def from_behind(value, axis, steps):
    count = lax.axis_size(axis)
    first, last = (max(0, -steps), min(count, count - steps))
    return lax.ppermute(value, axis, [(source, source + steps) for source in range(first, last)])


def time_table(count):
    samples = jnp.arange(count)
    bin_index = jnp.arange(count // 2)[:, None]
    angles = 2.0 * math.pi / count * (bin_index * samples[None, :] % count).astype(jnp.float32)
    parity = jnp.where(samples % 2 == 0, 1.0, -1.0).astype(jnp.float32)
    cosine = jnp.where(bin_index == 0, math.sqrt(1.0 / count), math.sqrt(2.0 / count)) * jnp.cos(
        angles
    )
    sine_part = jnp.where(
        bin_index == 0,
        math.sqrt(1.0 / count) * parity[None, :],
        -math.sqrt(2.0 / count) * jnp.sin(angles),
    )
    return jnp.stack([cosine, sine_part]).astype(jnp.bfloat16)


def shot_table(count):
    positions = jnp.arange(count)
    angles = (
        2.0
        * math.pi
        / count
        * (positions[:, None] * positions[None, :] % count).astype(jnp.float32)
    )
    scaling = 1.0 / math.sqrt(count)
    cosine = scaling * jnp.cos(angles)
    sine_part = scaling * jnp.sin(angles)
    upper_half = jnp.stack([cosine, sine_part], axis=1)
    lower_half = jnp.stack([-sine_part, cosine], axis=1)
    return jnp.stack([upper_half, lower_half]).astype(jnp.bfloat16)


def toeplitz_kernel(adjoint, taps_ref, out_ref):
    tap_count = taps_ref.shape[1]
    row_index = lax.broadcasted_iota(jnp.int32, (tap_count, tap_count), 0)
    col_index = lax.broadcasted_iota(jnp.int32, (tap_count, tap_count), 1)
    taps = taps_ref[...].astype(jnp.float32)
    for index in range(taps_ref.shape[0]):
        row = jnp.broadcast_to(taps[index : index + 1, :], (tap_count, tap_count))
        turned = pltpu.roll(row, 0, 1, stride=1, stride_axis=0)
        zeros = jnp.zeros_like(turned)
        near = jnp.where(col_index >= row_index, turned, zeros)
        far = jnp.where(col_index < row_index, turned, zeros)
        near, far = (near.T, far.T) if adjoint else (near, far)
        out_ref[index, :tap_count, :] = near.astype(jnp.bfloat16)
        out_ref[index, tap_count:, :] = far.astype(jnp.bfloat16)


def toeplitz_table(signatures, adjoint):
    count, tap_count = signatures.shape
    return pl.pallas_call(
        functools.partial(toeplitz_kernel, adjoint),
        out_shape=jax.ShapeDtypeStruct((count, 2 * tap_count, tap_count), jnp.bfloat16),
        in_specs=[pl.BlockSpec(memory_space=pltpu.VMEM)],
        out_specs=pl.BlockSpec(memory_space=pltpu.VMEM),
    )(signatures)


def apply_filter(traces, table, adjoint):
    empty = jnp.zeros_like(traces[:, :1])
    if adjoint:
        other = jnp.concatenate([traces[:, 1:], empty], axis=1)
    else:
        other = jnp.concatenate([empty, traces[:, :-1]], axis=1)
    return jnp.einsum(
        "sbrp,spq->sbrq",
        jnp.concatenate([traces, other], axis=3),
        table,
        preferred_element_type=jnp.float32,
    )


def rank_in_row(owners):
    shot_count = owners.shape[1]
    same_owner = owners[:, :, None] == owners[:, None, :]
    earlier = jnp.arange(shot_count)[None, :] < jnp.arange(shot_count)[:, None]
    return jnp.sum(same_owner & earlier[None], axis=2)


def to_slabs(payload):
    return lax.all_to_all(payload, ("shot", "rep"), split_axis=0, concat_axis=0, tiled=True)


def to_shots(payload):
    return lax.all_to_all(payload, ("shot", "rep"), split_axis=0, concat_axis=0, tiled=True)


def soft_limit(coefficients, threshold_row):
    magnitude = jnp.sqrt(coefficients[0] * coefficients[0] + coefficients[1] * coefficients[1])
    threshold_view = threshold_row[None, :, None, None]
    factor = 1.0 - threshold_view / jnp.maximum(magnitude, threshold_view)
    return (coefficients * factor[None]).astype(jnp.bfloat16)


def shrink(field_data, threshold_row, tables):
    table_time, table_x, table_y, table_r = tables
    rows_here, local_rcv, shot_count, sample_count = field_data.shape
    spectrum = jnp.einsum(
        "ckt,xryt->xckry",
        table_time,
        field_data.astype(jnp.bfloat16),
        preferred_element_type=jnp.float32,
    ).astype(jnp.bfloat16)
    bin_count = spectrum.shape[2]
    spectrum = spectrum.reshape(rows_here, 2, bin_count, local_rcv * shot_count)
    section_data = jnp.einsum(
        "akbx,xbfz->akfz",
        table_x,
        lax.all_to_all(spectrum, ("shot", "rep"), split_axis=2, concat_axis=0, tiled=True),
        preferred_element_type=jnp.float32,
    ).astype(jnp.bfloat16)
    all_rows, row_bins = (section_data.shape[1], section_data.shape[2])
    section_data = section_data.reshape(2, all_rows, row_bins, local_rcv, shot_count)
    section_data = lax.all_to_all(section_data, "rcv", split_axis=2, concat_axis=3, tiled=True)
    section_data = jnp.einsum(
        "ajby,bkfry->akfrj", table_y, section_data, preferred_element_type=jnp.float32
    ).astype(jnp.bfloat16)
    coefficients = jnp.einsum(
        "aqbr,bkfrj->akfqj", table_r, section_data, preferred_element_type=jnp.float32
    )
    shrunk = soft_limit(coefficients, threshold_row)
    section_data = jnp.einsum(
        "aqbr,akfqj->bkfrj", table_r, shrunk, preferred_element_type=jnp.float32
    ).astype(jnp.bfloat16)
    section_data = jnp.einsum(
        "ajby,akfrj->bkfry", table_y, section_data, preferred_element_type=jnp.float32
    ).astype(jnp.bfloat16)
    section_data = lax.all_to_all(section_data, "rcv", split_axis=3, concat_axis=2, tiled=True)
    section_data = section_data.reshape(2, all_rows, row_bins, local_rcv * shot_count)
    section_data = jnp.einsum(
        "akbx,akfz->bxfz", table_x, section_data, preferred_element_type=jnp.float32
    ).astype(jnp.bfloat16)
    result = jnp.einsum(
        "ckt,cxkz->xzt",
        table_time,
        lax.all_to_all(section_data, ("shot", "rep"), split_axis=1, concat_axis=2, tiled=True),
        preferred_element_type=jnp.float32,
    )
    return result.reshape(rows_here, local_rcv, shot_count, sample_count)


def body_by_rows(records, offsets, filter_index, signatures, thresholds):
    rows_here, shot_count = offsets.shape
    local_rcv, slab_len = records.shape
    slab_count = lax.axis_size(("shot", "rep"))
    rcv_count = lax.axis_size("rcv")
    tap_count = signatures.shape[1]
    sample_count = NT
    slab_blocks = slab_len // tap_count
    trace_blocks = sample_count // tap_count
    capacity = max(2, 2 * shot_count // slab_count)
    slot_count = slab_count * rows_here * capacity
    forward_tables = toeplitz_table(signatures, False)
    adjoint_tables = toeplitz_table(signatures, True)
    flat_index = filter_index.reshape(-1)
    forward_table = forward_tables[flat_index]
    adjoint_table = adjoint_tables[flat_index]
    owners = offsets // slab_len
    row_ids = jnp.arange(rows_here, dtype=jnp.int32)[:, None]
    slot_index = (
        owners * (rows_here * capacity) + row_ids * capacity + rank_in_row(owners)
    ).reshape(-1)
    every_offset = lax.all_gather(offsets, ("shot", "rep"), axis=0, tiled=True)
    every_owner = every_offset // slab_len
    every_start = every_offset // tap_count % slab_blocks
    every_rank = rank_in_row(every_owner)
    mine_mask = every_owner == lax.axis_index(("shot", "rep"))
    levels = jnp.arange(capacity, dtype=jnp.int32)
    picked = mine_mask[:, :, None] & (every_rank[:, :, None] == levels[None, None, :])
    table_in = jnp.sum(jnp.where(picked, every_start[:, :, None] + 1, 0), axis=1).reshape(-1)
    filled = table_in > 0
    block_steps = jnp.arange(trace_blocks, dtype=jnp.int32)
    target = jnp.where(
        filled[:, None],
        table_in[:, None] - 1 + block_steps[None, :],
        slab_blocks + trace_blocks - 1,
    )

    def correlate(record_field):
        record_low = (
            record_field.astype(jnp.bfloat16)
            .reshape(local_rcv, slab_blocks, tap_count)
            .transpose(1, 0, 2)
        )
        rim_blocks = from_behind(record_low[: trace_blocks - 1], ("shot", "rep"), -1)
        extended = jnp.concatenate(
            [record_low, rim_blocks, jnp.zeros((1, local_rcv, tap_count), jnp.bfloat16)], axis=0
        )
        windows = extended[target.reshape(-1)].reshape(
            slot_count, trace_blocks, local_rcv, tap_count
        )
        returned = to_shots(windows)
        traces = returned[slot_index]
        terms = apply_filter(traces, adjoint_table, True)
        terms = terms.reshape(rows_here, shot_count, trace_blocks, local_rcv, tap_count).transpose(
            0, 3, 1, 2, 4
        )
        return terms.reshape(rows_here, local_rcv, shot_count, sample_count)

    tables = (
        time_table(sample_count),
        shot_table(slab_count * rows_here),
        shot_table(shot_count),
        shot_table(local_rcv * rcv_count),
    )
    row_bins = sample_count // 2 // slab_count
    rcv_bins = row_bins // rcv_count
    bin_start = lax.axis_index(("shot", "rep")) * row_bins + lax.axis_index("rcv") * rcv_bins

    def threshold_for(level_index):
        return lax.dynamic_slice_in_dim(thresholds[level_index], bin_start, rcv_bins)

    model_field = shrink(correlate(records), threshold_for(0), tables)
    level_index = 1
    traces = model_field.astype(jnp.bfloat16).reshape(
        rows_here, local_rcv, shot_count, trace_blocks, tap_count
    )
    traces = traces.transpose(0, 2, 3, 1, 4).reshape(
        rows_here * shot_count, trace_blocks, local_rcv, tap_count
    )
    shots = apply_filter(traces, forward_table, False).astype(jnp.bfloat16)
    outgoing = (
        jnp.zeros((slot_count, trace_blocks, local_rcv, tap_count), jnp.bfloat16)
        .at[slot_index]
        .set(shots)
    )
    arrived = to_slabs(outgoing)
    slab_total = jnp.zeros((slab_blocks + trace_blocks, local_rcv, tap_count), jnp.float32)
    for block_step in range(trace_blocks):
        slab_total = slab_total.at[target[:, block_step]].add(
            arrived[:, block_step].astype(jnp.float32)
        )
    spill_over = slab_total[slab_blocks : slab_blocks + trace_blocks - 1]
    carried = from_behind(spill_over, ("shot", "rep"), 1)
    blended = slab_total[:slab_blocks].at[: trace_blocks - 1].add(carried)
    residual = records - blended.transpose(1, 0, 2).reshape(local_rcv, slab_len)
    model_field = shrink(model_field + correlate(residual), threshold_for(level_index), tables)
    return (model_field, residual)


def dot(left, right, left_dim=1, right_dim=0):
    return lax.dot_general(
        left, right, (((left_dim,), (right_dim,)), ((), ())), preferred_element_type=jnp.float32
    )


def fixed_time_table(count):
    samples = np.arange(count)
    bins = np.arange(count // 2)[:, None]
    angles = 2.0 * np.pi / count * (bins * samples[None, :] % count)
    scale = math.sqrt(2.0 / count)
    cosine = scale * np.cos(angles)
    sine = -scale * np.sin(angles)
    cosine[0] = math.sqrt(1.0 / count)
    sine[0] = math.sqrt(1.0 / count) * np.where(samples % 2 == 0, 1.0, -1.0)
    return np.stack([cosine, sine]).astype(jnp.bfloat16)


def fixed_shot_table(count):
    positions = np.arange(count)
    angles = 2.0 * np.pi / count * (positions[:, None] * positions[None, :] % count)
    cosine = np.cos(angles) / math.sqrt(count)
    sine = np.sin(angles) / math.sqrt(count)
    table = np.stack([np.stack([cosine, sine], 1), np.stack([-sine, cosine], 1)])
    return table.astype(jnp.bfloat16).astype(np.float32)


MESH = pl.DeviceIdType.MESH
AXES = ("shot", "rcv", "rep")


def neighbours(sizes):
    every = [(a, b, c) for a in range(sizes[0]) for b in range(sizes[1]) for c in range(sizes[2])]
    far = sizes[0] // 2
    return sorted(every[1:], key=lambda step: (abs(step[0] - far), -step[1], -step[2]))


def device_at(sizes, step):
    spot = [lax.rem(lax.axis_index(axis) + hop, size) for axis, hop, size in zip(AXES, step, sizes)]
    index = (spot[0] * sizes[1] + spot[1]) * sizes[2] + spot[2]
    return dict(zip(AXES, spot)), index


def build_taps(signature_ref, adjoint, out_ref):
    count, taps = signature_ref.shape
    row_index = lax.broadcasted_iota(jnp.int32, (taps, taps), 0)
    col_index = lax.broadcasted_iota(jnp.int32, (taps, taps), 1)
    values = signature_ref[...].astype(jnp.float32)
    for index in range(count):
        row = jnp.broadcast_to(values[index : index + 1, :], (taps, taps))
        turned = pltpu.roll(row, 0, 1, stride=1, stride_axis=0)
        zeros = jnp.zeros_like(turned)
        near = jnp.where(col_index >= row_index, turned, zeros)
        far = jnp.where(col_index < row_index, turned, zeros)
        near, far = (near.T, far.T) if adjoint else (near, far)
        where = slice(index * taps, (index + 1) * taps)
        out_ref[:taps, where] = near.astype(jnp.bfloat16)
        out_ref[taps:, where] = far.astype(jnp.bfloat16)


def pick_signature(every, picks_ref):
    slots, width = picks_ref.shape
    picks = jnp.concatenate([picks_ref[...]] * (every.shape[0] // slots), axis=0)
    chosen = every[:, :width]
    for index in range(1, every.shape[1] // width):
        chosen = jnp.where(picks == index, every[:, index * width : (index + 1) * width], chosen)
    return chosen


def correlate_line(line, select_ref, blocks_ref, taps_ref, picks_ref, field_ref, traces_ref):
    slots, width = picks_ref.shape
    window = dot(select_ref[...], blocks_ref[line]).astype(jnp.bfloat16)
    later = jnp.concatenate([window[slots:], jnp.zeros((slots, width), window.dtype)], axis=0)
    terms = pick_signature(dot(jnp.concatenate([window, later], axis=1), taps_ref[...]), picks_ref)
    steps = terms.shape[0] // slots
    terms = jnp.concatenate(
        [terms[step * slots : (step + 1) * slots] for step in range(steps)], axis=1
    )
    where = pl.ds(pl.multiple_of(line * slots, slots), slots)
    if field_ref is not None:
        terms = terms + field_ref[where]
    traces_ref[where] = terms.astype(jnp.bfloat16)


def blend_line(line, place_ref, field_ref, taps_ref, picks_ref):
    slots, width = picks_ref.shape
    trace = field_ref[pl.ds(pl.multiple_of(line * slots, slots), slots)].astype(jnp.bfloat16)
    steps = trace.shape[1] // width
    stacked = jnp.concatenate(
        [trace[:, step * width : (step + 1) * width] for step in range(steps)], axis=0
    )
    earlier = jnp.concatenate([jnp.zeros((slots, width), trace.dtype), stacked[:-slots]], axis=0)
    shots = pick_signature(dot(jnp.concatenate([stacked, earlier], axis=1), taps_ref[...]), picks_ref)
    return dot(place_ref[...], shots.astype(jnp.bfloat16))


def spectra_chunk(table, traces_ref, out_ref, lines, rcv, slots):
    parts, rows, lanes = out_ref.shape
    bins = rows // rcv
    half = parts * bins
    pack = max(1, 16 // bins)
    together = math.gcd(len(lines), 4)
    for first in range(lines[0], lines[-1] + 1, together):
        both = dot(table, traces_ref[first * slots : (first + together) * slots], 1, 1)
        for low in range(0, together, pack):
            pieces = []
            for line in range(low, low + pack):
                piece = both[:, line * slots : (line + 1) * slots]
                joined = jnp.concatenate([piece[:half], piece[half:]], axis=1)
                pieces.append(joined.reshape(parts, bins, lanes))
            out_ref[:, (first + low) * bins : (first + low + pack) * bins] = jnp.concatenate(
                pieces, axis=1
            ).astype(jnp.bfloat16)


def bins_chunk(place, halves, spectra_ref, go_ref, back_ref, cosine, sine, level, out_ref):
    _, rows, _ = spectra_ref.shape
    rcv_count, slab_count = place.shape
    joined = jnp.concatenate(
        [
            jnp.concatenate([spectra_ref[int(index)] for index in line], axis=1)
            for line in place
        ],
        axis=0,
    )
    section = dot(joined, go_ref[...]).astype(jnp.bfloat16)
    half = section.shape[1] // 2
    near = dot(cosine, section)
    far = dot(sine, section)
    real = near[:, :half] + far[:, half:]
    imag = near[:, half:] - far[:, :half]
    factor = 1.0 - level / jnp.maximum(jnp.sqrt(real * real + imag * imag), level)
    shrunk = jnp.concatenate([real * factor, imag * factor], axis=1).astype(jnp.bfloat16)
    near = dot(cosine, shrunk)
    far = dot(sine, shrunk)
    section = jnp.concatenate(
        [near[:, :half] - far[:, half:], far[:, :half] + near[:, half:]], axis=1
    ).astype(jnp.bfloat16)
    result = dot(section, back_ref[...], 1, 1).astype(jnp.bfloat16)
    width = result.shape[1] // slab_count
    for line in range(rcv_count):
        for slab in range(slab_count):
            piece = result[line * rows : (line + 1) * rows, slab * width : (slab + 1) * width]
            if halves == 2:
                piece = jnp.concatenate([piece[: rows // 2], piece[rows // 2 :]], axis=1)
            out_ref[int(place[line, slab])] = piece


def level_of(levels_ref, index, first, bins, copies_of):
    width = levels_ref.shape[1]
    lane = lax.broadcasted_iota(jnp.int32, (bins, width), 1)
    row = lax.broadcasted_iota(jnp.int32, (bins, width), 0)
    values = jnp.broadcast_to(levels_ref[index : index + 1, :], (bins, width))
    column = jnp.sum(jnp.where(lane == row + first, values, 0.0), axis=1, keepdims=True)
    return jnp.concatenate([column] * copies_of, axis=0)


def upright(spectra_ref, chunk, lines, bins, group_lanes):
    parts = spectra_ref.shape[1]
    pack = max(1, 16 // bins)
    count = group_lanes // 2
    pieces = []
    for low_line in range(lines[0], lines[-1] + 1, pack):
        block = spectra_ref[chunk, :, low_line * bins : (low_line + pack) * bins].astype(jnp.float32)
        for line in range(pack):
            turned = block[:, line * bins : (line + 1) * bins].reshape(parts * bins, -1).T
            turned = turned.astype(jnp.bfloat16)
            for low in range(0, turned.shape[0], group_lanes):
                pieces.append(
                    jnp.concatenate(
                        [turned[low : low + count], turned[low + count : low + 2 * count]], axis=1
                    )
                )
    return jnp.concatenate(pieces, axis=0)


HALVES = 2
CHUNKS = 2


def whole_kernel(
    sizes,
    place,
    starts_ref,
    picks_ref,
    records_ref,
    blocks_ref,
    signatures_ref,
    levels_ref,
    table_ref,
    slot_table_ref,
    row_table_ref,
    cosine_ref,
    sine_ref,
    model_ref,
    left_ref,
    adjoint_ref,
    forward_ref,
    select_ref,
    place_ref,
    traces_ref,
    field_ref,
    rest_ref,
    head_ref,
    spill_ref,
    carried_ref,
    ahead_ref,
    sent_ref,
    got_ref,
    answer_ref,
    home_ref,
    reply_ref,
    final_ref,
    go_sends,
    go_recvs,
    back_sends,
    back_recvs,
    rim_sends,
    rim_recvs,
):
    slots, width = picks_ref.shape
    rcv, padded, _ = blocks_ref.shape
    blocks = records_ref.shape[1]
    chunks = table_ref.shape[0]
    samples = table_ref.shape[2]
    steps = samples // width
    parts = place.size
    few = samples // 2 // parts // chunks
    lines_in_half = rcv // HALVES
    rows_in_half = lines_in_half * few
    edge = head_ref.shape[1]
    all_rcv = rcv * place.shape[0]
    halves = [range(half * lines_in_half, (half + 1) * lines_in_half) for half in range(HALVES)]

    barrier = pltpu.get_barrier_semaphore()
    hops = neighbours(sizes)
    for hop in hops:
        pl.semaphore_signal(barrier, inc=1, device_id=device_at(sizes, hop)[0], device_id_type=MESH)
    mine = device_at(sizes, (0, 0, 0))[1]
    slab = lax.axis_index("shot") * sizes[2] + lax.axis_index("rep")
    last_slab = sizes[0] * sizes[2] - 1

    def slab_device(shift):
        other = lax.rem(slab + shift + last_slab + 1, last_slab + 1)
        return {
            "shot": other // sizes[2],
            "rcv": lax.axis_index("rcv"),
            "rep": lax.rem(other, sizes[2]),
        }

    build_taps(signatures_ref, True, adjoint_ref)
    block_index = lax.broadcasted_iota(jnp.int32, (slots, padded), 1)
    first_block = jnp.broadcast_to(starts_ref[:, :1], (slots, padded))
    select = jnp.concatenate(
        [(block_index == first_block + step).astype(jnp.float32) for step in range(steps)], axis=0
    )
    select_ref[...] = select.astype(jnp.bfloat16)
    place_ref[...] = select.T.astype(jnp.bfloat16)
    pl.semaphore_wait(barrier, len(hops))

    def exchange(source, target, send_sems, recv_sems, low, rows):
        made = []
        where = pl.ds(low, rows)
        for number, hop in enumerate(hops):
            device, index = device_at(sizes, hop)
            copy = pltpu.make_async_remote_copy(
                src_ref=source.at[index, where],
                dst_ref=target.at[mine, where],
                send_sem=send_sems.at[number],
                recv_sem=recv_sems.at[number],
                device_id=device,
                device_id_type=MESH,
            )
            copy.start()
            made.append(copy)
        target[mine, where] = source[mine, where]
        return made

    def send_half(half, from_ref, model):
        def one(line, carry):
            correlate_line(line, select_ref, from_ref, adjoint_ref, picks_ref, model, traces_ref)
            return carry

        lax.fori_loop(half * lines_in_half, (half + 1) * lines_in_half, one, 0)
        made = []
        for chunk in range(chunks):
            spectra_chunk(
                table_ref[chunk], traces_ref, sent_ref.at[chunk], halves[half], rcv, slots
            )
            made.append(
                exchange(
                    sent_ref.at[chunk],
                    got_ref.at[chunk],
                    go_sends.at[half, chunk],
                    go_recvs.at[half, chunk],
                    half * rows_in_half,
                    rows_in_half,
                )
            )
        return made

    def level(index, chunk):
        return level_of(levels_ref, index, (mine * chunks + chunk) * few, few, all_rcv)

    going = [send_half(half, blocks_ref, None) for half in range(HALVES)]
    build_taps(signatures_ref, False, forward_ref)
    coming = {}
    for chunk in range(chunks):
        for half in range(HALVES):
            for copy in going[half][chunk]:
                copy.wait_recv()
        bins_chunk(
            place, 1, got_ref.at[chunk], slot_table_ref, slot_table_ref, cosine_ref[...], sine_ref[...], level(0, chunk), answer_ref.at[chunk]
        )
        coming[0, chunk] = exchange(
            answer_ref.at[chunk], home_ref.at[chunk], back_sends.at[0, chunk], back_recvs.at[0, chunk], 0, rows_in_half
        )
    for half in range(1, HALVES):
        for chunk in range(chunks):
            coming[half, chunk] = exchange(
                answer_ref.at[chunk],
                home_ref.at[chunk],
                back_sends.at[half, chunk],
                back_recvs.at[half, chunk],
                half * rows_in_half,
                rows_in_half,
            )
    for made in going:
        for chunk in made:
            for copy in chunk:
                copy.wait_send()

    again = []
    for half in range(HALVES):
        low, high = half * lines_in_half, (half + 1) * lines_in_half
        for chunk in range(chunks):
            for copy in coming[half, chunk]:
                copy.wait_recv()
        together = math.gcd(lines_in_half, 4)
        for first in range(low, high, together):
            lines = range(first, first + together)
            field_ref[first * slots : (first + together) * slots] = sum(
                dot(upright(home_ref, chunk, lines, few, 2 * slots), table_ref[chunk])
                for chunk in range(chunks)
            )

        def one(line, carry):
            blended = blend_line(line, place_ref, field_ref, forward_ref, picks_ref)
            left = records_ref[line] - blended[:blocks]
            left_ref[line] = left
            head_ref[line] = left[:edge]
            spill_ref[line] = blended[blocks : blocks + edge]
            return carry

        lax.fori_loop(low, high, one, 0)
        where = pl.ds(low, lines_in_half)
        onward = pltpu.make_async_remote_copy(
            src_ref=spill_ref.at[where],
            dst_ref=carried_ref.at[where],
            send_sem=rim_sends.at[half, 0],
            recv_sem=rim_recvs.at[half, 0],
            device_id=slab_device(1),
            device_id_type=MESH,
        )
        backward = pltpu.make_async_remote_copy(
            src_ref=head_ref.at[where],
            dst_ref=ahead_ref.at[where],
            send_sem=rim_sends.at[half, 1],
            recv_sem=rim_recvs.at[half, 1],
            device_id=slab_device(-1),
            device_id_type=MESH,
        )

        @pl.when(slab < last_slab)
        def _():
            onward.start()

        @pl.when(slab > 0)
        def _():
            backward.start()
            onward.wait_recv()
            left_ref[where, :edge] = left_ref[where, :edge] - carried_ref[where]

        rest_ref[where, :blocks] = left_ref[where].astype(jnp.bfloat16)
        rest_ref[where, blocks:] = jnp.zeros(
            (lines_in_half, padded - blocks, width), jnp.bfloat16
        )

        @pl.when(slab < last_slab)
        def _():
            backward.wait_recv()
            rim = ahead_ref[where] - spill_ref[where]
            rim = jnp.concatenate(
                [rim, jnp.zeros((lines_in_half, padded - blocks - edge, width), jnp.float32)], axis=1
            )
            rest_ref[where, blocks:] = rim.astype(jnp.bfloat16)
            onward.wait_send()

        @pl.when(slab > 0)
        def _():
            backward.wait_send()

        again.append(send_half(half, rest_ref, field_ref))

    for half in range(HALVES):
        for chunk in range(chunks):
            for copy in coming[half, chunk]:
                copy.wait_send()
    final = []
    for chunk in range(chunks):
        for half in range(HALVES):
            for copy in again[half][chunk]:
                copy.wait_recv()
        bins_chunk(
            place, 2, got_ref.at[chunk], slot_table_ref, row_table_ref, cosine_ref[...], sine_ref[...], level(1, chunk), reply_ref.at[chunk]
        )
        final.append(
            exchange(
                reply_ref.at[chunk], final_ref.at[chunk], back_sends.at[0, chunk], back_recvs.at[0, chunk], 0, reply_ref.shape[2]
            )
        )
    for made in again:
        for chunk in made:
            for copy in chunk:
                copy.wait_send()
    groups, lines_there, count, _ = model_ref.shape
    together = math.gcd(lines_there, 4)
    for chunk in range(chunks):
        for copy in final[chunk]:
            copy.wait()
        for first in range(0, lines_there, together):
            fields = dot(
                upright(final_ref, chunk, range(first, first + together), few, 2 * count),
                table_ref[chunk],
            )
            for line in range(together):
                for group in range(groups):
                    low = (line * groups + group) * count
                    piece = fields[low : low + count]
                    if chunk:
                        piece = piece + model_ref[group, first + line]
                    model_ref[group, first + line] = piece


def body_by_slots(records, offsets, filter_index, signatures, thresholds):
    rows_here, shot_count = offsets.shape
    local_rcv, slab_len = records.shape
    slab_count = lax.axis_size(("shot", "rep"))
    rep_count = lax.axis_size("rep")
    rcv_count = lax.axis_size("rcv")
    sizes = tuple(lax.axis_size(axis) for axis in AXES)
    parts = slab_count * rcv_count
    tap_count = signatures.shape[1]
    slab_blocks = slab_len // tap_count
    steps = NT // tap_count
    capacity = max(2, 2 * shot_count // slab_count)
    row_count = rows_here * slab_count
    slots = row_count * capacity
    bins = NT // 2 // parts
    chunks = CHUNKS
    few = bins // chunks
    place = np.array(
        [
            [((slab // rep_count) * rcv_count + line) * rep_count + slab % rep_count for slab in range(slab_count)]
            for line in range(rcv_count)
        ]
    )

    time_table_fixed = fixed_time_table(NT).reshape(2, parts, chunks, few, NT)
    time_table_fixed = jnp.asarray(
        np.ascontiguousarray(time_table_fixed.transpose(2, 0, 1, 3, 4)).reshape(chunks, NT // chunks, NT)
    )
    table_x, table_y, table_r = (
        fixed_shot_table(count) for count in (row_count, shot_count, local_rcv * rcv_count)
    )
    grid_table = np.einsum("ajby,bkcx->cxyakj", table_y, table_x).astype(jnp.bfloat16)
    row_table = np.ascontiguousarray(grid_table.transpose(1, 0, 2, 3, 4, 5))
    points = 2 * row_count * shot_count
    grid_table = jnp.asarray(grid_table.reshape(points, points))
    row_table = jnp.asarray(row_table.reshape(points, points))
    same = np.eye(few, dtype=np.float32)
    cosine = jnp.asarray(np.kron(table_r[0, :, 0], same).astype(jnp.bfloat16))
    sine = jnp.asarray(np.kron(table_r[0, :, 1], same).astype(jnp.bfloat16))

    shots = jnp.stack([offsets, filter_index])
    every = lax.all_to_all(
        jnp.broadcast_to(shots[None], (slab_count,) + shots.shape), ("shot", "rep"), 0, 0, tiled=True
    )
    every_offset = every[:, 0].reshape(row_count, shot_count)
    every_pick = every[:, 1].reshape(row_count, shot_count)
    every_owner = every_offset // slab_len
    every_rank = rank_in_row(every_owner)
    slabs = jnp.arange(slab_count, dtype=jnp.int32)
    ranks = jnp.arange(capacity, dtype=jnp.int32)
    taken = (every_owner[None, :, None, :] == slabs[:, None, None, None]) & (
        every_rank[None, :, None, :] == ranks[None, None, :, None]
    )
    point_of = jnp.arange(row_count * shot_count, dtype=jnp.int32).reshape(row_count, shot_count)
    code = jnp.sum(jnp.where(taken, point_of[None, :, None, :] + 1, 0), axis=3).reshape(
        slab_count, 1, slots
    )
    code = jnp.where(
        code > 0, code - 1 + row_count * shot_count * jnp.arange(2, dtype=jnp.int32)[None, :, None], -1
    ).reshape(-1)
    chosen = (code[:, None] == jnp.arange(points, dtype=jnp.int32)[None, :]).astype(jnp.bfloat16)
    slot_table = dot(chosen, grid_table).astype(jnp.bfloat16)
    mine = (every_owner == lax.axis_index(("shot", "rep")))[:, None, :] & (
        every_rank[:, None, :] == ranks[None, :, None]
    )
    every_start = every_offset // tap_count % slab_blocks
    starts = jnp.sum(jnp.where(mine, every_start[:, None, :] + 1, 0), axis=2).reshape(-1)
    starts = jnp.where(starts > 0, starts - 1, -NT)
    picks = jnp.sum(jnp.where(mine, every_pick[:, None, :], 0), axis=2).reshape(-1)
    starts = jnp.broadcast_to(starts[:, None], (slots, tap_count))
    picks = jnp.broadcast_to(picks[:, None], (slots, tap_count))

    edge = 8
    padded = slab_blocks + 2 * edge
    record_blocks = records.reshape(local_rcv, slab_blocks, tap_count)
    rim = from_behind(
        record_blocks[:, :edge].astype(jnp.bfloat16), ("shot", "rep"), -1
    )
    extended = jnp.concatenate(
        [record_blocks.astype(jnp.bfloat16), rim, jnp.zeros_like(rim)], axis=1
    )
    vmem = pl.BlockSpec(memory_space=pltpu.VMEM)
    rows = local_rcv * few
    table_width = tap_count * signatures.shape[0]
    low, wide = jnp.bfloat16, jnp.float32
    model, residual = pl.pallas_call(
        functools.partial(whole_kernel, sizes, place),
        out_shape=(
            jax.ShapeDtypeStruct((2, local_rcv // 2, shot_count, NT), wide),
            jax.ShapeDtypeStruct(record_blocks.shape, wide),
        ),
        in_specs=[vmem] * 11,
        out_specs=(vmem, vmem),
        scratch_shapes=[
            pltpu.VMEM((2 * tap_count, table_width), low),
            pltpu.VMEM((2 * tap_count, table_width), low),
            pltpu.VMEM((slots * steps, padded), low),
            pltpu.VMEM((padded, slots * steps), low),
            pltpu.VMEM((local_rcv * slots, NT), low),
            pltpu.VMEM((local_rcv * slots, NT), wide),
            pltpu.VMEM(extended.shape, low),
        ]
        + [pltpu.VMEM((local_rcv, edge, tap_count), wide)] * 4
        + [pltpu.VMEM((chunks, parts, rows, 2 * slots), low)] * 4
        + [pltpu.VMEM((chunks, parts, rows // 2, 4 * shot_count), low)] * 2
        + [pltpu.SemaphoreType.DMA((HALVES, chunks, parts - 1))] * 4
        + [pltpu.SemaphoreType.DMA((HALVES, 2))] * 2,
        compiler_params=pltpu.CompilerParams(collective_id=0, has_side_effects=True),
    )(
        starts, picks, record_blocks, extended, signatures, thresholds, time_table_fixed, slot_table, row_table, cosine, sine
    )
    return (
        model.reshape(rows_here, local_rcv, shot_count, NT),
        residual.reshape(local_rcv, slab_len),
    )


def body(records, offsets, filter_index, signatures, thresholds):
    rows_here, shot_count = offsets.shape
    slab_count = lax.axis_size(("shot", "rep"))
    parts = slab_count * lax.axis_size("rcv")
    slots = rows_here * slab_count * max(2, 2 * shot_count // slab_count)
    table_rows = 2 * rows_here * slab_count * shot_count
    fits = table_rows <= 1024 and rows_here == 1 and slots == 64 and 4 * shot_count == 128
    fits = fits and records.shape[0] == 16 and NT // 2 // parts == 16
    run = body_by_slots if fits else body_by_rows
    return run(records, offsets, filter_index, signatures, thresholds)


def solution(mesh):
    in_specs = (
        P(("groups", "rcv"), ("shot", "rep")),
        P(("groups", "shot", "rep"), None),
        P(("groups", "shot", "rep"), None),
        P(),
        P(),
    )
    out_specs = (
        P(("groups", "shot", "rep"), "rcv", None, None),
        P(("groups", "rcv"), ("shot", "rep")),
    )
    return jax.shard_map(body, mesh=mesh, in_specs=in_specs, out_specs=out_specs, check_vma=False)
```

```python
import functools
import math

import jax
import jax.numpy as jnp
import numpy as np
from jax import lax
from jax.experimental import pallas as pl
from jax.experimental.pallas import tpu as pltpu
from jax.sharding import PartitionSpec as P

NT = 512


def from_behind(value, axis, steps):
    count = lax.axis_size(axis)
    first, last = (max(0, -steps), min(count, count - steps))
    return lax.ppermute(value, axis, [(source, source + steps) for source in range(first, last)])


def time_table(count):
    samples = jnp.arange(count)
    bin_index = jnp.arange(count // 2)[:, None]
    angles = 2.0 * math.pi / count * (bin_index * samples[None, :] % count).astype(jnp.float32)
    parity = jnp.where(samples % 2 == 0, 1.0, -1.0).astype(jnp.float32)
    cosine = jnp.where(bin_index == 0, math.sqrt(1.0 / count), math.sqrt(2.0 / count)) * jnp.cos(
        angles
    )
    sine_part = jnp.where(
        bin_index == 0,
        math.sqrt(1.0 / count) * parity[None, :],
        -math.sqrt(2.0 / count) * jnp.sin(angles),
    )
    return jnp.stack([cosine, sine_part]).astype(jnp.bfloat16)


def shot_table(count):
    positions = jnp.arange(count)
    angles = (
        2.0
        * math.pi
        / count
        * (positions[:, None] * positions[None, :] % count).astype(jnp.float32)
    )
    scaling = 1.0 / math.sqrt(count)
    cosine = scaling * jnp.cos(angles)
    sine_part = scaling * jnp.sin(angles)
    upper_half = jnp.stack([cosine, sine_part], axis=1)
    lower_half = jnp.stack([-sine_part, cosine], axis=1)
    return jnp.stack([upper_half, lower_half]).astype(jnp.bfloat16)


def toeplitz_kernel(adjoint, taps_ref, out_ref):
    tap_count = taps_ref.shape[1]
    row_index = lax.broadcasted_iota(jnp.int32, (tap_count, tap_count), 0)
    col_index = lax.broadcasted_iota(jnp.int32, (tap_count, tap_count), 1)
    taps = taps_ref[...].astype(jnp.float32)
    for index in range(taps_ref.shape[0]):
        row = jnp.broadcast_to(taps[index : index + 1, :], (tap_count, tap_count))
        turned = pltpu.roll(row, 0, 1, stride=1, stride_axis=0)
        zeros = jnp.zeros_like(turned)
        near = jnp.where(col_index >= row_index, turned, zeros)
        far = jnp.where(col_index < row_index, turned, zeros)
        near, far = (near.T, far.T) if adjoint else (near, far)
        out_ref[index, :tap_count, :] = near.astype(jnp.bfloat16)
        out_ref[index, tap_count:, :] = far.astype(jnp.bfloat16)


def toeplitz_table(signatures, adjoint):
    count, tap_count = signatures.shape
    return pl.pallas_call(
        functools.partial(toeplitz_kernel, adjoint),
        out_shape=jax.ShapeDtypeStruct((count, 2 * tap_count, tap_count), jnp.bfloat16),
        in_specs=[pl.BlockSpec(memory_space=pltpu.VMEM)],
        out_specs=pl.BlockSpec(memory_space=pltpu.VMEM),
    )(signatures)


def apply_filter(traces, table, adjoint):
    empty = jnp.zeros_like(traces[:, :1])
    if adjoint:
        other = jnp.concatenate([traces[:, 1:], empty], axis=1)
    else:
        other = jnp.concatenate([empty, traces[:, :-1]], axis=1)
    return jnp.einsum(
        "sbrp,spq->sbrq",
        jnp.concatenate([traces, other], axis=3),
        table,
        preferred_element_type=jnp.float32,
    )


def rank_in_row(owners):
    shot_count = owners.shape[1]
    same_owner = owners[:, :, None] == owners[:, None, :]
    earlier = jnp.arange(shot_count)[None, :] < jnp.arange(shot_count)[:, None]
    return jnp.sum(same_owner & earlier[None], axis=2)


def to_slabs(payload):
    return lax.all_to_all(payload, ("shot", "rep"), split_axis=0, concat_axis=0, tiled=True)


def to_shots(payload):
    return lax.all_to_all(payload, ("shot", "rep"), split_axis=0, concat_axis=0, tiled=True)


def soft_limit(coefficients, threshold_row):
    magnitude = jnp.sqrt(coefficients[0] * coefficients[0] + coefficients[1] * coefficients[1])
    threshold_view = threshold_row[None, :, None, None]
    factor = 1.0 - threshold_view / jnp.maximum(magnitude, threshold_view)
    return (coefficients * factor[None]).astype(jnp.bfloat16)


def shrink(field_data, threshold_row, tables):
    table_time, table_x, table_y, table_r = tables
    rows_here, local_rcv, shot_count, sample_count = field_data.shape
    spectrum = jnp.einsum(
        "ckt,xryt->xckry",
        table_time,
        field_data.astype(jnp.bfloat16),
        preferred_element_type=jnp.float32,
    ).astype(jnp.bfloat16)
    bin_count = spectrum.shape[2]
    spectrum = spectrum.reshape(rows_here, 2, bin_count, local_rcv * shot_count)
    section_data = jnp.einsum(
        "akbx,xbfz->akfz",
        table_x,
        lax.all_to_all(spectrum, ("shot", "rep"), split_axis=2, concat_axis=0, tiled=True),
        preferred_element_type=jnp.float32,
    ).astype(jnp.bfloat16)
    all_rows, row_bins = (section_data.shape[1], section_data.shape[2])
    section_data = section_data.reshape(2, all_rows, row_bins, local_rcv, shot_count)
    section_data = lax.all_to_all(section_data, "rcv", split_axis=2, concat_axis=3, tiled=True)
    section_data = jnp.einsum(
        "ajby,bkfry->akfrj", table_y, section_data, preferred_element_type=jnp.float32
    ).astype(jnp.bfloat16)
    coefficients = jnp.einsum(
        "aqbr,bkfrj->akfqj", table_r, section_data, preferred_element_type=jnp.float32
    )
    shrunk = soft_limit(coefficients, threshold_row)
    section_data = jnp.einsum(
        "aqbr,akfqj->bkfrj", table_r, shrunk, preferred_element_type=jnp.float32
    ).astype(jnp.bfloat16)
    section_data = jnp.einsum(
        "ajby,akfrj->bkfry", table_y, section_data, preferred_element_type=jnp.float32
    ).astype(jnp.bfloat16)
    section_data = lax.all_to_all(section_data, "rcv", split_axis=3, concat_axis=2, tiled=True)
    section_data = section_data.reshape(2, all_rows, row_bins, local_rcv * shot_count)
    section_data = jnp.einsum(
        "akbx,akfz->bxfz", table_x, section_data, preferred_element_type=jnp.float32
    ).astype(jnp.bfloat16)
    result = jnp.einsum(
        "ckt,cxkz->xzt",
        table_time,
        lax.all_to_all(section_data, ("shot", "rep"), split_axis=1, concat_axis=2, tiled=True),
        preferred_element_type=jnp.float32,
    )
    return result.reshape(rows_here, local_rcv, shot_count, sample_count)


def body_by_rows(records, offsets, filter_index, signatures, thresholds):
    rows_here, shot_count = offsets.shape
    local_rcv, slab_len = records.shape
    slab_count = lax.axis_size(("shot", "rep"))
    rcv_count = lax.axis_size("rcv")
    tap_count = signatures.shape[1]
    sample_count = NT
    slab_blocks = slab_len // tap_count
    trace_blocks = sample_count // tap_count
    capacity = max(2, 2 * shot_count // slab_count)
    slot_count = slab_count * rows_here * capacity
    forward_tables = toeplitz_table(signatures, False)
    adjoint_tables = toeplitz_table(signatures, True)
    flat_index = filter_index.reshape(-1)
    forward_table = forward_tables[flat_index]
    adjoint_table = adjoint_tables[flat_index]
    owners = offsets // slab_len
    row_ids = jnp.arange(rows_here, dtype=jnp.int32)[:, None]
    slot_index = (
        owners * (rows_here * capacity) + row_ids * capacity + rank_in_row(owners)
    ).reshape(-1)
    every_offset = lax.all_gather(offsets, ("shot", "rep"), axis=0, tiled=True)
    every_owner = every_offset // slab_len
    every_start = every_offset // tap_count % slab_blocks
    every_rank = rank_in_row(every_owner)
    mine_mask = every_owner == lax.axis_index(("shot", "rep"))
    levels = jnp.arange(capacity, dtype=jnp.int32)
    picked = mine_mask[:, :, None] & (every_rank[:, :, None] == levels[None, None, :])
    table_in = jnp.sum(jnp.where(picked, every_start[:, :, None] + 1, 0), axis=1).reshape(-1)
    filled = table_in > 0
    block_steps = jnp.arange(trace_blocks, dtype=jnp.int32)
    target = jnp.where(
        filled[:, None],
        table_in[:, None] - 1 + block_steps[None, :],
        slab_blocks + trace_blocks - 1,
    )

    def correlate(record_field):
        record_low = (
            record_field.astype(jnp.bfloat16)
            .reshape(local_rcv, slab_blocks, tap_count)
            .transpose(1, 0, 2)
        )
        rim_blocks = from_behind(record_low[: trace_blocks - 1], ("shot", "rep"), -1)
        extended = jnp.concatenate(
            [record_low, rim_blocks, jnp.zeros((1, local_rcv, tap_count), jnp.bfloat16)], axis=0
        )
        windows = extended[target.reshape(-1)].reshape(
            slot_count, trace_blocks, local_rcv, tap_count
        )
        returned = to_shots(windows)
        traces = returned[slot_index]
        terms = apply_filter(traces, adjoint_table, True)
        terms = terms.reshape(rows_here, shot_count, trace_blocks, local_rcv, tap_count).transpose(
            0, 3, 1, 2, 4
        )
        return terms.reshape(rows_here, local_rcv, shot_count, sample_count)

    tables = (
        time_table(sample_count),
        shot_table(slab_count * rows_here),
        shot_table(shot_count),
        shot_table(local_rcv * rcv_count),
    )
    row_bins = sample_count // 2 // slab_count
    rcv_bins = row_bins // rcv_count
    bin_start = lax.axis_index(("shot", "rep")) * row_bins + lax.axis_index("rcv") * rcv_bins

    def threshold_for(level_index):
        return lax.dynamic_slice_in_dim(thresholds[level_index], bin_start, rcv_bins)

    model_field = shrink(correlate(records), threshold_for(0), tables)
    level_index = 1
    traces = model_field.astype(jnp.bfloat16).reshape(
        rows_here, local_rcv, shot_count, trace_blocks, tap_count
    )
    traces = traces.transpose(0, 2, 3, 1, 4).reshape(
        rows_here * shot_count, trace_blocks, local_rcv, tap_count
    )
    shots = apply_filter(traces, forward_table, False).astype(jnp.bfloat16)
    outgoing = (
        jnp.zeros((slot_count, trace_blocks, local_rcv, tap_count), jnp.bfloat16)
        .at[slot_index]
        .set(shots)
    )
    arrived = to_slabs(outgoing)
    slab_total = jnp.zeros((slab_blocks + trace_blocks, local_rcv, tap_count), jnp.float32)
    for block_step in range(trace_blocks):
        slab_total = slab_total.at[target[:, block_step]].add(
            arrived[:, block_step].astype(jnp.float32)
        )
    spill_over = slab_total[slab_blocks : slab_blocks + trace_blocks - 1]
    carried = from_behind(spill_over, ("shot", "rep"), 1)
    blended = slab_total[:slab_blocks].at[: trace_blocks - 1].add(carried)
    residual = records - blended.transpose(1, 0, 2).reshape(local_rcv, slab_len)
    model_field = shrink(model_field + correlate(residual), threshold_for(level_index), tables)
    return (model_field, residual)


def dot(left, right, left_dim=1, right_dim=0):
    return lax.dot_general(
        left, right, (((left_dim,), (right_dim,)), ((), ())), preferred_element_type=jnp.float32
    )


def fixed_time_table(count):
    samples = np.arange(count)
    bins = np.arange(count // 2)[:, None]
    angles = 2.0 * np.pi / count * (bins * samples[None, :] % count)
    scale = math.sqrt(2.0 / count)
    cosine = scale * np.cos(angles)
    sine = -scale * np.sin(angles)
    cosine[0] = math.sqrt(1.0 / count)
    sine[0] = math.sqrt(1.0 / count) * np.where(samples % 2 == 0, 1.0, -1.0)
    return np.stack([cosine, sine]).astype(jnp.bfloat16)


def fixed_shot_table(count):
    positions = np.arange(count)
    angles = 2.0 * np.pi / count * (positions[:, None] * positions[None, :] % count)
    cosine = np.cos(angles) / math.sqrt(count)
    sine = np.sin(angles) / math.sqrt(count)
    table = np.stack([np.stack([cosine, sine], 1), np.stack([-sine, cosine], 1)])
    return table.astype(jnp.bfloat16).astype(np.float32)


MESH = pl.DeviceIdType.MESH
AXES = ("shot", "rcv", "rep")


def neighbours(sizes):
    every = [(a, b, c) for a in range(sizes[0]) for b in range(sizes[1]) for c in range(sizes[2])]
    far = sizes[0] // 2
    return sorted(every[1:], key=lambda step: (abs(step[0] - far), -step[1], -step[2]))


def device_at(sizes, step):
    spot = [lax.rem(lax.axis_index(axis) + hop, size) for axis, hop, size in zip(AXES, step, sizes)]
    index = (spot[0] * sizes[1] + spot[1]) * sizes[2] + spot[2]
    return dict(zip(AXES, spot)), index


def build_taps(signature_ref, adjoint, out_ref):
    count, taps = signature_ref.shape
    row_index = lax.broadcasted_iota(jnp.int32, (taps, taps), 0)
    col_index = lax.broadcasted_iota(jnp.int32, (taps, taps), 1)
    values = signature_ref[...].astype(jnp.float32)
    for index in range(count):
        row = jnp.broadcast_to(values[index : index + 1, :], (taps, taps))
        turned = pltpu.roll(row, 0, 1, stride=1, stride_axis=0)
        zeros = jnp.zeros_like(turned)
        near = jnp.where(col_index >= row_index, turned, zeros)
        far = jnp.where(col_index < row_index, turned, zeros)
        near, far = (near.T, far.T) if adjoint else (near, far)
        where = slice(index * taps, (index + 1) * taps)
        out_ref[:taps, where] = near.astype(jnp.bfloat16)
        out_ref[taps:, where] = far.astype(jnp.bfloat16)


def pick_signature(every, picks_ref):
    slots, width = picks_ref.shape
    picks = jnp.concatenate([picks_ref[...]] * (every.shape[0] // slots), axis=0)
    chosen = every[:, :width]
    for index in range(1, every.shape[1] // width):
        chosen = jnp.where(picks == index, every[:, index * width : (index + 1) * width], chosen)
    return chosen


def correlate_line(line, padded, select_ref, blocks_ref, taps_ref, picks_ref, field_ref, traces_ref):
    slots, width = picks_ref.shape
    blocks = blocks_ref[pl.ds(pl.multiple_of(line * padded, 8), padded)].astype(jnp.bfloat16)
    window = dot(select_ref[...], blocks).astype(jnp.bfloat16)
    later = jnp.concatenate([window[slots:], jnp.zeros((slots, width), window.dtype)], axis=0)
    terms = pick_signature(dot(jnp.concatenate([window, later], axis=1), taps_ref[...]), picks_ref)
    steps = terms.shape[0] // slots
    terms = jnp.concatenate(
        [terms[step * slots : (step + 1) * slots] for step in range(steps)], axis=1
    )
    where = pl.ds(pl.multiple_of(line * slots, slots), slots)
    if field_ref is not None:
        terms = terms + field_ref[where]
    traces_ref[where] = terms.astype(jnp.bfloat16)


def blend_line(line, place_ref, field_ref, taps_ref, picks_ref):
    slots, width = picks_ref.shape
    trace = field_ref[pl.ds(pl.multiple_of(line * slots, slots), slots)].astype(jnp.bfloat16)
    steps = trace.shape[1] // width
    stacked = jnp.concatenate(
        [trace[:, step * width : (step + 1) * width] for step in range(steps)], axis=0
    )
    earlier = jnp.concatenate([jnp.zeros((slots, width), trace.dtype), stacked[:-slots]], axis=0)
    shots = pick_signature(dot(jnp.concatenate([stacked, earlier], axis=1), taps_ref[...]), picks_ref)
    return dot(place_ref[...], shots.astype(jnp.bfloat16))


def spectra_chunk(table, traces_ref, out_ref, lines, rcv, slots):
    parts, rows, lanes = out_ref.shape
    bins = rows // rcv
    half = parts * bins
    pack = max(1, 16 // bins)
    together = math.gcd(len(lines), 4)
    for first in range(lines[0], lines[-1] + 1, together):
        both = dot(table, traces_ref[first * slots : (first + together) * slots], 1, 1)
        for low in range(0, together, pack):
            pieces = []
            for line in range(low, low + pack):
                piece = both[:, line * slots : (line + 1) * slots]
                joined = jnp.concatenate([piece[:half], piece[half:]], axis=1)
                pieces.append(joined.reshape(parts, bins, lanes))
            out_ref[:, (first + low) * bins : (first + low + pack) * bins] = jnp.concatenate(
                pieces, axis=1
            ).astype(jnp.bfloat16)


def bins_chunk(place, halves, spectra_ref, go_ref, back_ref, cosine, sine, level, out_ref):
    _, rows, _ = spectra_ref.shape
    rcv_count, slab_count = place.shape
    joined = jnp.concatenate(
        [
            jnp.concatenate([spectra_ref[int(index)] for index in line], axis=1)
            for line in place
        ],
        axis=0,
    )
    section = dot(joined, go_ref[...]).astype(jnp.bfloat16)
    half = section.shape[1] // 2
    near = dot(cosine, section)
    far = dot(sine, section)
    real = near[:, :half] + far[:, half:]
    imag = near[:, half:] - far[:, :half]
    factor = 1.0 - level / jnp.maximum(jnp.sqrt(real * real + imag * imag), level)
    shrunk = jnp.concatenate([real * factor, imag * factor], axis=1).astype(jnp.bfloat16)
    near = dot(cosine, shrunk)
    far = dot(sine, shrunk)
    section = jnp.concatenate(
        [near[:, :half] - far[:, half:], far[:, :half] + near[:, half:]], axis=1
    ).astype(jnp.bfloat16)
    result = dot(section, back_ref[...], 1, 1).astype(jnp.bfloat16)
    width = result.shape[1] // slab_count
    for line in range(rcv_count):
        for slab in range(slab_count):
            piece = result[line * rows : (line + 1) * rows, slab * width : (slab + 1) * width]
            if halves == 2:
                piece = jnp.concatenate([piece[: rows // 2], piece[rows // 2 :]], axis=1)
            out_ref[int(place[line, slab])] = piece


def level_of(levels_ref, index, first, bins, copies_of):
    width = levels_ref.shape[1]
    lane = lax.broadcasted_iota(jnp.int32, (bins, width), 1)
    row = lax.broadcasted_iota(jnp.int32, (bins, width), 0)
    values = jnp.broadcast_to(levels_ref[index : index + 1, :], (bins, width))
    column = jnp.sum(jnp.where(lane == row + first, values, 0.0), axis=1, keepdims=True)
    return jnp.concatenate([column] * copies_of, axis=0)


def upright(spectra_ref, chunk, lines, bins, group_lanes):
    parts = spectra_ref.shape[1]
    pack = max(1, 16 // bins)
    count = group_lanes // 2
    pieces = []
    for low_line in range(lines[0], lines[-1] + 1, pack):
        block = spectra_ref[chunk, :, low_line * bins : (low_line + pack) * bins].astype(jnp.float32)
        for line in range(pack):
            turned = block[:, line * bins : (line + 1) * bins].reshape(parts * bins, -1).T
            turned = turned.astype(jnp.bfloat16)
            for low in range(0, turned.shape[0], group_lanes):
                pieces.append(
                    jnp.concatenate(
                        [turned[low : low + count], turned[low + count : low + 2 * count]], axis=1
                    )
                )
    return jnp.concatenate(pieces, axis=0)


HALVES = 2
CHUNKS = 2


def whole_kernel(
    sizes,
    place,
    offsets_ref,
    filters_ref,
    signatures_ref,
    levels_ref,
    records_hbm,
    table_hbm,
    grid_hbm,
    row_table_hbm,
    cosine_hbm,
    sine_hbm,
    model_ref,
    left_ref,
    records_ref,
    table_ref,
    grid_ref,
    row_table_ref,
    cosine_ref,
    sine_ref,
    row_ref,
    rows_ref,
    rim_ref,
    picks_ref,
    slot_table_ref,
    adjoint_ref,
    forward_ref,
    select_ref,
    place_ref,
    traces_ref,
    field_ref,
    blocks_ref,
    rest_ref,
    head_ref,
    spill_ref,
    carried_ref,
    ahead_ref,
    sent_ref,
    got_ref,
    answer_ref,
    home_ref,
    reply_ref,
    final_ref,
    load_sems,
    row_sends,
    row_recvs,
    go_sends,
    go_recvs,
    back_sends,
    back_recvs,
    rim_sends,
    rim_recvs,
):
    slots, width = picks_ref.shape
    rcv, slab_len = records_ref.shape
    blocks = slab_len // width
    padded = blocks_ref.shape[0] // rcv
    chunks, _, samples = table_ref.shape
    steps = samples // width
    parts = place.size
    slab_count = place.shape[1]
    few = samples // 2 // parts // chunks
    lines_in_half = rcv // HALVES
    rows_in_half = lines_in_half * few
    edge = head_ref.shape[1]
    all_rcv = rcv * place.shape[0]
    shot_count = offsets_ref.shape[1]
    row_count = slab_count
    capacity = slots // row_count
    wide = jnp.float32

    loads = [
        pltpu.make_async_copy(source, target, load_sems.at[number])
        for number, (source, target) in enumerate(
            (
                (records_hbm, records_ref),
                (table_hbm, table_ref),
                (grid_hbm, grid_ref),
                (cosine_hbm, cosine_ref),
                (sine_hbm, sine_ref),
                (row_table_hbm, row_table_ref),
            )
        )
    ]
    for load in loads:
        load.start()
    barrier = pltpu.get_barrier_semaphore()
    hops = neighbours(sizes)
    for hop in hops:
        pl.semaphore_signal(barrier, inc=1, device_id=device_at(sizes, hop)[0], device_id_type=MESH)
    mine = device_at(sizes, (0, 0, 0))[1]
    slab = lax.axis_index("shot") * sizes[2] + lax.axis_index("rep")
    last_slab = slab_count - 1

    def slab_device(shift):
        other = lax.rem(slab + shift + slab_count, slab_count)
        return {
            "shot": other // sizes[2],
            "rcv": lax.axis_index("rcv"),
            "rep": lax.rem(other, sizes[2]),
        }

    row_ref[...] = jnp.zeros_like(row_ref)
    row_ref[0:1, :shot_count] = offsets_ref[...]
    row_ref[1:2, :shot_count] = filters_ref[...]
    build_taps(signatures_ref, True, adjoint_ref)
    pl.semaphore_wait(barrier, len(hops))

    tile = row_ref.shape[0]
    here = pl.ds(pl.multiple_of(slab * tile, tile), tile)
    row_copies = []
    for hop in hops:
        if hop[1] == 0:
            number = len(row_copies)
            copy = pltpu.make_async_remote_copy(
                src_ref=row_ref,
                dst_ref=rows_ref.at[here],
                send_sem=row_sends.at[number],
                recv_sem=row_recvs.at[number],
                device_id=device_at(sizes, hop)[0],
                device_id_type=MESH,
            )
            copy.start()
            row_copies.append(copy)
    rows_ref[here] = row_ref[...]
    loads[0].wait()
    first_rim = pltpu.make_async_remote_copy(
        src_ref=records_ref.at[:, pl.ds(0, rim_ref.shape[1])],
        dst_ref=rim_ref,
        send_sem=rim_sends.at[HALVES, 0],
        recv_sem=rim_recvs.at[HALVES, 0],
        device_id=slab_device(-1),
        device_id_type=MESH,
    )

    @pl.when(slab > 0)
    def _():
        first_rim.start()

    for line in range(rcv):
        blocks_ref[line * padded + blocks : (line + 1) * padded] = jnp.zeros(
            (padded - blocks, width), wide
        )
    for block in range(blocks):
        blocks_ref[pl.ds(block, rcv, stride=padded), :] = records_ref[
            :, block * width : (block + 1) * width
        ]
    for copy in row_copies:
        copy.wait_recv()

    lane = lax.broadcasted_iota(jnp.int32, (row_count, width), 1)
    valid = lane < shot_count
    zero = jnp.zeros((row_count, width), jnp.int32)
    start_sample = jnp.where(valid, rows_ref[pl.ds(0, row_count, stride=tile), :], zero)
    signature = jnp.where(valid, rows_ref[pl.ds(1, row_count, stride=tile), :], zero)
    block_bits = width.bit_length() - 1
    slab_bits = slab_len.bit_length() - 1
    owner = lax.shift_right_logical(start_sample, slab_bits)
    rank = zero
    for step in range(1, shot_count):
        same = (pltpu.roll(owner, step, 1) == owner) & (lane >= step)
        rank = rank + same.astype(jnp.int32)
    key = jnp.where(valid, owner * capacity + rank + 1, zero)
    first_block = (lax.shift_right_logical(start_sample, block_bits) & (blocks - 1)).astype(wide)
    signature = signature.astype(wide)
    firsts, picks = [], []
    for level in range(capacity):
        taken = key == slab * capacity + level + 1
        empty = jnp.zeros_like(first_block)
        firsts.append(jnp.sum(jnp.where(taken, first_block + 1.0, empty), axis=1, keepdims=True))
        picks.append(jnp.sum(jnp.where(taken, signature, empty), axis=1, keepdims=True))
    firsts = jnp.broadcast_to(jnp.concatenate(firsts, axis=0), (slots, padded))
    firsts = jnp.where(firsts > 0.5, firsts - 1.0, -float(samples))
    picks_ref[...] = jnp.broadcast_to(jnp.concatenate(picks, axis=0), (slots, width))
    block_index = lax.broadcasted_iota(jnp.int32, (slots, padded), 1).astype(wide)
    select = jnp.concatenate(
        [(block_index == firsts + float(step)).astype(wide) for step in range(steps)], axis=0
    )
    select_ref[...] = select.astype(jnp.bfloat16)

    @pl.when(slab < last_slab)
    def _():
        first_rim.wait_recv()
        for step in range(rim_ref.shape[1] // width):
            blocks_ref[pl.ds(blocks + step, rcv, stride=padded), :] = rim_ref[
                :, step * width : (step + 1) * width
            ]

    loads[1].wait()

    def exchange(source, target, send_sems, recv_sems, low, rows):
        made = []
        where = pl.ds(low, rows)
        for number, hop in enumerate(hops):
            device, index = device_at(sizes, hop)
            copy = pltpu.make_async_remote_copy(
                src_ref=source.at[index, where],
                dst_ref=target.at[mine, where],
                send_sem=send_sems.at[number],
                recv_sem=recv_sems.at[number],
                device_id=device,
                device_id_type=MESH,
            )
            copy.start()
            made.append(copy)
        target[mine, where] = source[mine, where]
        return made

    def send_span(number, span, from_ref, model):
        def one(line, carry):
            correlate_line(
                line, padded, select_ref, from_ref, adjoint_ref, picks_ref, model, traces_ref
            )
            return carry

        lax.fori_loop(span[0], span[1], one, 0)
        made = []
        for chunk in range(chunks):
            spectra_chunk(
                table_ref[chunk], traces_ref, sent_ref.at[chunk], range(*span), rcv, slots
            )
            made.append(
                exchange(
                    sent_ref.at[chunk],
                    got_ref.at[chunk],
                    go_sends.at[number, chunk],
                    go_recvs.at[number, chunk],
                    span[0] * few,
                    (span[1] - span[0]) * few,
                )
            )
        return made

    def level_at(index, chunk):
        return level_of(levels_ref, index, (mine * chunks + chunk) * few, few, all_rcv)

    quarter = rcv // 4
    spans = ((0, quarter), (quarter, 2 * quarter), (2 * quarter, rcv))
    going = [send_span(number, span, blocks_ref, None) for number, span in enumerate(spans)]

    place_ref[...] = select.T.astype(jnp.bfloat16)
    build_taps(signatures_ref, False, forward_ref)
    repeated = key
    for shift in range(shot_count, width, shot_count):
        repeated = repeated + pltpu.roll(key, shift, 1)
    points = row_count * shot_count
    repeated = jnp.concatenate([repeated] * (points // width), axis=1)
    point = lax.broadcasted_iota(jnp.int32, (row_count, points), 1)
    row = lax.broadcasted_iota(jnp.int32, (row_count, points), 0)
    shot_bits = shot_count.bit_length() - 1
    repeated = jnp.where(lax.shift_right_logical(point, shot_bits) == row, repeated, 0)
    chosen = jnp.concatenate(
        [(repeated == number + 1).astype(wide) for number in range(slab_count * capacity)], axis=0
    ).astype(jnp.bfloat16)
    for load in loads[2:]:
        load.wait()
    for half in range(2):
        part = dot(chosen, grid_ref[half * points : (half + 1) * points]).astype(jnp.bfloat16)
        for number in range(slab_count):
            low = (2 * number + half) * slots
            slot_table_ref[low : low + slots] = part[number * slots : (number + 1) * slots]

    coming = {}
    for chunk in range(chunks):
        for made in going:
            for copy in made[chunk]:
                copy.wait_recv()
        bins_chunk(
            place, 1, got_ref.at[chunk], slot_table_ref, slot_table_ref, cosine_ref[...], sine_ref[...], level_at(0, chunk), answer_ref.at[chunk]
        )
        coming[0, chunk] = exchange(
            answer_ref.at[chunk], home_ref.at[chunk], back_sends.at[0, chunk], back_recvs.at[0, chunk], 0, rows_in_half
        )
    for half in range(1, HALVES):
        for chunk in range(chunks):
            coming[half, chunk] = exchange(
                answer_ref.at[chunk],
                home_ref.at[chunk],
                back_sends.at[half, chunk],
                back_recvs.at[half, chunk],
                half * rows_in_half,
                rows_in_half,
            )
    for copy in row_copies:
        copy.wait_send()

    @pl.when(slab > 0)
    def _():
        first_rim.wait_send()

    for made in going:
        for chunk in made:
            for copy in chunk:
                copy.wait_send()

    again = []
    for half in range(HALVES):
        low, high = half * lines_in_half, (half + 1) * lines_in_half
        for chunk in range(chunks):
            for copy in coming[half, chunk]:
                copy.wait_recv()
        together = math.gcd(lines_in_half, 4)
        for first in range(low, high, together):
            lines = range(first, first + together)
            field_ref[first * slots : (first + together) * slots] = sum(
                dot(upright(home_ref, chunk, lines, few, 2 * slots), table_ref[chunk])
                for chunk in range(chunks)
            )

        def one(line, carry):
            blended = blend_line(line, place_ref, field_ref, forward_ref, picks_ref)
            start = pl.multiple_of(line * padded, 8)
            left = blocks_ref[pl.ds(start, blocks)] - blended[:blocks]
            rest_ref[pl.ds(start, blocks)] = left
            rest_ref[pl.ds(start + blocks, padded - blocks)] = jnp.zeros(
                (padded - blocks, width), wide
            )
            head_ref[line] = left[:edge]
            spill_ref[line] = blended[blocks : blocks + edge]
            return carry

        lax.fori_loop(low, high, one, 0)
        where = pl.ds(low, lines_in_half)
        onward = pltpu.make_async_remote_copy(
            src_ref=spill_ref.at[where],
            dst_ref=carried_ref.at[where],
            send_sem=rim_sends.at[half, 0],
            recv_sem=rim_recvs.at[half, 0],
            device_id=slab_device(1),
            device_id_type=MESH,
        )
        backward = pltpu.make_async_remote_copy(
            src_ref=head_ref.at[where],
            dst_ref=ahead_ref.at[where],
            send_sem=rim_sends.at[half, 1],
            recv_sem=rim_recvs.at[half, 1],
            device_id=slab_device(-1),
            device_id_type=MESH,
        )

        @pl.when(slab < last_slab)
        def _():
            onward.start()

        @pl.when(slab > 0)
        def _():
            backward.start()
            onward.wait_recv()
            for line in range(low, high):
                here = pl.ds(line * padded, edge)
                rest_ref[here] = rest_ref[here] - carried_ref[line]

        @pl.when(slab < last_slab)
        def _():
            backward.wait_recv()
            for line in range(low, high):
                rest_ref[pl.ds(line * padded + blocks, edge)] = ahead_ref[line] - spill_ref[line]
            onward.wait_send()

        @pl.when(slab > 0)
        def _():
            backward.wait_send()

        again.append(send_span(half, (low, high), rest_ref, field_ref))

    for block in range(blocks):
        left_ref[:, block * width : (block + 1) * width] = rest_ref[
            pl.ds(block, rcv, stride=padded), :
        ]
    for half in range(HALVES):
        for chunk in range(chunks):
            for copy in coming[half, chunk]:
                copy.wait_send()
    final = []
    for chunk in range(chunks):
        for half in range(HALVES):
            for copy in again[half][chunk]:
                copy.wait_recv()
        bins_chunk(
            place, 2, got_ref.at[chunk], slot_table_ref, row_table_ref, cosine_ref[...], sine_ref[...], level_at(1, chunk), reply_ref.at[chunk]
        )
        final.append(
            exchange(
                reply_ref.at[chunk], final_ref.at[chunk], back_sends.at[0, chunk], back_recvs.at[0, chunk], 0, reply_ref.shape[2]
            )
        )
    for made in again:
        for chunk in made:
            for copy in chunk:
                copy.wait_send()
    groups, lines_there, count, _ = model_ref.shape
    together = math.gcd(lines_there, 4)
    for chunk in range(chunks):
        for copy in final[chunk]:
            copy.wait()
        for first in range(0, lines_there, together):
            fields = dot(
                upright(final_ref, chunk, range(first, first + together), few, 2 * count),
                table_ref[chunk],
            )
            for line in range(together):
                for group in range(groups):
                    low = (line * groups + group) * count
                    piece = fields[low : low + count]
                    if chunk:
                        piece = piece + model_ref[group, first + line]
                    model_ref[group, first + line] = piece


def body_by_slots(records, offsets, filter_index, signatures, thresholds):
    rows_here, shot_count = offsets.shape
    local_rcv, slab_len = records.shape
    slab_count = lax.axis_size(("shot", "rep"))
    rep_count = lax.axis_size("rep")
    rcv_count = lax.axis_size("rcv")
    sizes = tuple(lax.axis_size(axis) for axis in AXES)
    parts = slab_count * rcv_count
    tap_count = signatures.shape[1]
    slab_blocks = slab_len // tap_count
    steps = NT // tap_count
    capacity = max(2, 2 * shot_count // slab_count)
    row_count = rows_here * slab_count
    slots = row_count * capacity
    bins = NT // 2 // parts
    chunks = CHUNKS
    few = bins // chunks
    place = np.array(
        [
            [((slab // rep_count) * rcv_count + line) * rep_count + slab % rep_count for slab in range(slab_count)]
            for line in range(rcv_count)
        ]
    )

    time_table_fixed = fixed_time_table(NT).reshape(2, parts, chunks, few, NT)
    time_table_fixed = jnp.asarray(
        np.ascontiguousarray(time_table_fixed.transpose(2, 0, 1, 3, 4)).reshape(chunks, NT // chunks, NT)
    )
    table_x, table_y, table_r = (
        fixed_shot_table(count) for count in (row_count, shot_count, local_rcv * rcv_count)
    )
    grid_table = np.einsum("ajby,bkcx->cxyakj", table_y, table_x).astype(jnp.bfloat16)
    row_table = np.ascontiguousarray(grid_table.transpose(1, 0, 2, 3, 4, 5))
    points = 2 * row_count * shot_count
    grid_table = jnp.asarray(grid_table.reshape(points, points))
    row_table = jnp.asarray(row_table.reshape(points, points))
    same = np.eye(few, dtype=np.float32)
    cosine = jnp.asarray(np.kron(table_r[0, :, 0], same).astype(jnp.bfloat16))
    sine = jnp.asarray(np.kron(table_r[0, :, 1], same).astype(jnp.bfloat16))

    edge = 8
    padded = slab_blocks + 2 * edge
    vmem = pl.BlockSpec(memory_space=pltpu.VMEM)
    anywhere = pl.BlockSpec(memory_space=pl.ANY)
    rows = local_rcv * few
    table_width = tap_count * signatures.shape[0]
    low, wide = jnp.bfloat16, jnp.float32
    big = (records, time_table_fixed, grid_table, row_table, cosine, sine)
    model, residual = pl.pallas_call(
        functools.partial(whole_kernel, sizes, place),
        out_shape=(
            jax.ShapeDtypeStruct((2, local_rcv // 2, shot_count, NT), wide),
            jax.ShapeDtypeStruct(records.shape, wide),
        ),
        in_specs=[vmem] * 4 + [anywhere] * len(big),
        out_specs=(vmem, vmem),
        scratch_shapes=[pltpu.VMEM(array.shape, array.dtype) for array in big]
        + [
            pltpu.VMEM((edge, tap_count), jnp.int32),
            pltpu.VMEM((slab_count * edge, tap_count), jnp.int32),
            pltpu.VMEM((local_rcv, (steps - 1) * tap_count), wide),
            pltpu.VMEM((slots, tap_count), wide),
            pltpu.VMEM((slab_count * 2 * slots, points), low),
            pltpu.VMEM((2 * tap_count, table_width), low),
            pltpu.VMEM((2 * tap_count, table_width), low),
            pltpu.VMEM((slots * steps, padded), low),
            pltpu.VMEM((padded, slots * steps), low),
            pltpu.VMEM((local_rcv * slots, NT), low),
            pltpu.VMEM((local_rcv * slots, NT), wide),
            pltpu.VMEM((local_rcv * padded, tap_count), wide),
            pltpu.VMEM((local_rcv * padded, tap_count), wide),
        ]
        + [pltpu.VMEM((local_rcv, edge, tap_count), wide)] * 4
        + [pltpu.VMEM((chunks, parts, rows, 2 * slots), low)] * 4
        + [pltpu.VMEM((chunks, parts, rows // 2, 4 * shot_count), low)] * 2
        + [pltpu.SemaphoreType.DMA((len(big),))]
        + [pltpu.SemaphoreType.DMA((slab_count - 1,))] * 2
        + [pltpu.SemaphoreType.DMA((3, chunks, parts - 1))] * 2
        + [pltpu.SemaphoreType.DMA((HALVES, chunks, parts - 1))] * 2
        + [pltpu.SemaphoreType.DMA((HALVES + 1, 2))] * 2,
        compiler_params=pltpu.CompilerParams(collective_id=0, has_side_effects=True),
    )(offsets, filter_index, signatures, thresholds, *big)
    return (model.reshape(rows_here, local_rcv, shot_count, NT), residual)


def body(records, offsets, filter_index, signatures, thresholds):
    rows_here, shot_count = offsets.shape
    slab_count = lax.axis_size(("shot", "rep"))
    parts = slab_count * lax.axis_size("rcv")
    slots = rows_here * slab_count * max(2, 2 * shot_count // slab_count)
    table_rows = 2 * rows_here * slab_count * shot_count
    fits = table_rows <= 1024 and rows_here == 1 and slots == 64 and 4 * shot_count == 128
    fits = fits and records.shape[0] == 16 and NT // 2 // parts == 16
    slab_len, tap_count = records.shape[1], signatures.shape[1]
    fits = fits and tap_count == 128 and slab_len & (slab_len - 1) == 0
    run = body_by_slots if fits else body_by_rows
    return run(records, offsets, filter_index, signatures, thresholds)


def solution(mesh):
    in_specs = (
        P(("groups", "rcv"), ("shot", "rep")),
        P(("groups", "shot", "rep"), None),
        P(("groups", "shot", "rep"), None),
        P(),
        P(),
    )
    out_specs = (
        P(("groups", "shot", "rep"), "rcv", None, None),
        P(("groups", "rcv"), ("shot", "rep")),
    )
    return jax.shard_map(body, mesh=mesh, in_specs=in_specs, out_specs=out_specs, check_vma=False)
```

```python
import functools
import math

import jax
import jax.numpy as jnp
import numpy as np
from jax import lax
from jax.experimental import pallas as pl
from jax.experimental.pallas import tpu as pltpu
from jax.sharding import PartitionSpec as P

NT = 512


def from_behind(value, axis, steps):
    count = lax.axis_size(axis)
    first, last = (max(0, -steps), min(count, count - steps))
    return lax.ppermute(value, axis, [(source, source + steps) for source in range(first, last)])


def time_table(count):
    samples = jnp.arange(count)
    bin_index = jnp.arange(count // 2)[:, None]
    angles = 2.0 * math.pi / count * (bin_index * samples[None, :] % count).astype(jnp.float32)
    parity = jnp.where(samples % 2 == 0, 1.0, -1.0).astype(jnp.float32)
    cosine = jnp.where(bin_index == 0, math.sqrt(1.0 / count), math.sqrt(2.0 / count)) * jnp.cos(
        angles
    )
    sine_part = jnp.where(
        bin_index == 0,
        math.sqrt(1.0 / count) * parity[None, :],
        -math.sqrt(2.0 / count) * jnp.sin(angles),
    )
    return jnp.stack([cosine, sine_part]).astype(jnp.bfloat16)


def shot_table(count):
    positions = jnp.arange(count)
    angles = (
        2.0
        * math.pi
        / count
        * (positions[:, None] * positions[None, :] % count).astype(jnp.float32)
    )
    scaling = 1.0 / math.sqrt(count)
    cosine = scaling * jnp.cos(angles)
    sine_part = scaling * jnp.sin(angles)
    upper_half = jnp.stack([cosine, sine_part], axis=1)
    lower_half = jnp.stack([-sine_part, cosine], axis=1)
    return jnp.stack([upper_half, lower_half]).astype(jnp.bfloat16)


def toeplitz_kernel(adjoint, taps_ref, out_ref):
    tap_count = taps_ref.shape[1]
    row_index = lax.broadcasted_iota(jnp.int32, (tap_count, tap_count), 0)
    col_index = lax.broadcasted_iota(jnp.int32, (tap_count, tap_count), 1)
    taps = taps_ref[...].astype(jnp.float32)
    for index in range(taps_ref.shape[0]):
        row = jnp.broadcast_to(taps[index : index + 1, :], (tap_count, tap_count))
        turned = pltpu.roll(row, 0, 1, stride=1, stride_axis=0)
        zeros = jnp.zeros_like(turned)
        near = jnp.where(col_index >= row_index, turned, zeros)
        far = jnp.where(col_index < row_index, turned, zeros)
        near, far = (near.T, far.T) if adjoint else (near, far)
        out_ref[index, :tap_count, :] = near.astype(jnp.bfloat16)
        out_ref[index, tap_count:, :] = far.astype(jnp.bfloat16)


def toeplitz_table(signatures, adjoint):
    count, tap_count = signatures.shape
    return pl.pallas_call(
        functools.partial(toeplitz_kernel, adjoint),
        out_shape=jax.ShapeDtypeStruct((count, 2 * tap_count, tap_count), jnp.bfloat16),
        in_specs=[pl.BlockSpec(memory_space=pltpu.VMEM)],
        out_specs=pl.BlockSpec(memory_space=pltpu.VMEM),
    )(signatures)


def apply_filter(traces, table, adjoint):
    empty = jnp.zeros_like(traces[:, :1])
    if adjoint:
        other = jnp.concatenate([traces[:, 1:], empty], axis=1)
    else:
        other = jnp.concatenate([empty, traces[:, :-1]], axis=1)
    return jnp.einsum(
        "sbrp,spq->sbrq",
        jnp.concatenate([traces, other], axis=3),
        table,
        preferred_element_type=jnp.float32,
    )


def rank_in_row(owners):
    shot_count = owners.shape[1]
    same_owner = owners[:, :, None] == owners[:, None, :]
    earlier = jnp.arange(shot_count)[None, :] < jnp.arange(shot_count)[:, None]
    return jnp.sum(same_owner & earlier[None], axis=2)


def to_slabs(payload):
    return lax.all_to_all(payload, ("shot", "rep"), split_axis=0, concat_axis=0, tiled=True)


def to_shots(payload):
    return lax.all_to_all(payload, ("shot", "rep"), split_axis=0, concat_axis=0, tiled=True)


def soft_limit(coefficients, threshold_row):
    magnitude = jnp.sqrt(coefficients[0] * coefficients[0] + coefficients[1] * coefficients[1])
    threshold_view = threshold_row[None, :, None, None]
    factor = 1.0 - threshold_view / jnp.maximum(magnitude, threshold_view)
    return (coefficients * factor[None]).astype(jnp.bfloat16)


def shrink(field_data, threshold_row, tables):
    table_time, table_x, table_y, table_r = tables
    rows_here, local_rcv, shot_count, sample_count = field_data.shape
    spectrum = jnp.einsum(
        "ckt,xryt->xckry",
        table_time,
        field_data.astype(jnp.bfloat16),
        preferred_element_type=jnp.float32,
    ).astype(jnp.bfloat16)
    bin_count = spectrum.shape[2]
    spectrum = spectrum.reshape(rows_here, 2, bin_count, local_rcv * shot_count)
    section_data = jnp.einsum(
        "akbx,xbfz->akfz",
        table_x,
        lax.all_to_all(spectrum, ("shot", "rep"), split_axis=2, concat_axis=0, tiled=True),
        preferred_element_type=jnp.float32,
    ).astype(jnp.bfloat16)
    all_rows, row_bins = (section_data.shape[1], section_data.shape[2])
    section_data = section_data.reshape(2, all_rows, row_bins, local_rcv, shot_count)
    section_data = lax.all_to_all(section_data, "rcv", split_axis=2, concat_axis=3, tiled=True)
    section_data = jnp.einsum(
        "ajby,bkfry->akfrj", table_y, section_data, preferred_element_type=jnp.float32
    ).astype(jnp.bfloat16)
    coefficients = jnp.einsum(
        "aqbr,bkfrj->akfqj", table_r, section_data, preferred_element_type=jnp.float32
    )
    shrunk = soft_limit(coefficients, threshold_row)
    section_data = jnp.einsum(
        "aqbr,akfqj->bkfrj", table_r, shrunk, preferred_element_type=jnp.float32
    ).astype(jnp.bfloat16)
    section_data = jnp.einsum(
        "ajby,akfrj->bkfry", table_y, section_data, preferred_element_type=jnp.float32
    ).astype(jnp.bfloat16)
    section_data = lax.all_to_all(section_data, "rcv", split_axis=3, concat_axis=2, tiled=True)
    section_data = section_data.reshape(2, all_rows, row_bins, local_rcv * shot_count)
    section_data = jnp.einsum(
        "akbx,akfz->bxfz", table_x, section_data, preferred_element_type=jnp.float32
    ).astype(jnp.bfloat16)
    result = jnp.einsum(
        "ckt,cxkz->xzt",
        table_time,
        lax.all_to_all(section_data, ("shot", "rep"), split_axis=1, concat_axis=2, tiled=True),
        preferred_element_type=jnp.float32,
    )
    return result.reshape(rows_here, local_rcv, shot_count, sample_count)


def body_by_rows(records, offsets, filter_index, signatures, thresholds):
    rows_here, shot_count = offsets.shape
    local_rcv, slab_len = records.shape
    slab_count = lax.axis_size(("shot", "rep"))
    rcv_count = lax.axis_size("rcv")
    tap_count = signatures.shape[1]
    sample_count = NT
    slab_blocks = slab_len // tap_count
    trace_blocks = sample_count // tap_count
    capacity = max(2, 2 * shot_count // slab_count)
    slot_count = slab_count * rows_here * capacity
    forward_tables = toeplitz_table(signatures, False)
    adjoint_tables = toeplitz_table(signatures, True)
    flat_index = filter_index.reshape(-1)
    forward_table = forward_tables[flat_index]
    adjoint_table = adjoint_tables[flat_index]
    owners = offsets // slab_len
    row_ids = jnp.arange(rows_here, dtype=jnp.int32)[:, None]
    slot_index = (
        owners * (rows_here * capacity) + row_ids * capacity + rank_in_row(owners)
    ).reshape(-1)
    every_offset = lax.all_gather(offsets, ("shot", "rep"), axis=0, tiled=True)
    every_owner = every_offset // slab_len
    every_start = every_offset // tap_count % slab_blocks
    every_rank = rank_in_row(every_owner)
    mine_mask = every_owner == lax.axis_index(("shot", "rep"))
    levels = jnp.arange(capacity, dtype=jnp.int32)
    picked = mine_mask[:, :, None] & (every_rank[:, :, None] == levels[None, None, :])
    table_in = jnp.sum(jnp.where(picked, every_start[:, :, None] + 1, 0), axis=1).reshape(-1)
    filled = table_in > 0
    block_steps = jnp.arange(trace_blocks, dtype=jnp.int32)
    target = jnp.where(
        filled[:, None],
        table_in[:, None] - 1 + block_steps[None, :],
        slab_blocks + trace_blocks - 1,
    )

    def correlate(record_field):
        record_low = (
            record_field.astype(jnp.bfloat16)
            .reshape(local_rcv, slab_blocks, tap_count)
            .transpose(1, 0, 2)
        )
        rim_blocks = from_behind(record_low[: trace_blocks - 1], ("shot", "rep"), -1)
        extended = jnp.concatenate(
            [record_low, rim_blocks, jnp.zeros((1, local_rcv, tap_count), jnp.bfloat16)], axis=0
        )
        windows = extended[target.reshape(-1)].reshape(
            slot_count, trace_blocks, local_rcv, tap_count
        )
        returned = to_shots(windows)
        traces = returned[slot_index]
        terms = apply_filter(traces, adjoint_table, True)
        terms = terms.reshape(rows_here, shot_count, trace_blocks, local_rcv, tap_count).transpose(
            0, 3, 1, 2, 4
        )
        return terms.reshape(rows_here, local_rcv, shot_count, sample_count)

    tables = (
        time_table(sample_count),
        shot_table(slab_count * rows_here),
        shot_table(shot_count),
        shot_table(local_rcv * rcv_count),
    )
    row_bins = sample_count // 2 // slab_count
    rcv_bins = row_bins // rcv_count
    bin_start = lax.axis_index(("shot", "rep")) * row_bins + lax.axis_index("rcv") * rcv_bins

    def threshold_for(level_index):
        return lax.dynamic_slice_in_dim(thresholds[level_index], bin_start, rcv_bins)

    model_field = shrink(correlate(records), threshold_for(0), tables)
    level_index = 1
    traces = model_field.astype(jnp.bfloat16).reshape(
        rows_here, local_rcv, shot_count, trace_blocks, tap_count
    )
    traces = traces.transpose(0, 2, 3, 1, 4).reshape(
        rows_here * shot_count, trace_blocks, local_rcv, tap_count
    )
    shots = apply_filter(traces, forward_table, False).astype(jnp.bfloat16)
    outgoing = (
        jnp.zeros((slot_count, trace_blocks, local_rcv, tap_count), jnp.bfloat16)
        .at[slot_index]
        .set(shots)
    )
    arrived = to_slabs(outgoing)
    slab_total = jnp.zeros((slab_blocks + trace_blocks, local_rcv, tap_count), jnp.float32)
    for block_step in range(trace_blocks):
        slab_total = slab_total.at[target[:, block_step]].add(
            arrived[:, block_step].astype(jnp.float32)
        )
    spill_over = slab_total[slab_blocks : slab_blocks + trace_blocks - 1]
    carried = from_behind(spill_over, ("shot", "rep"), 1)
    blended = slab_total[:slab_blocks].at[: trace_blocks - 1].add(carried)
    residual = records - blended.transpose(1, 0, 2).reshape(local_rcv, slab_len)
    model_field = shrink(model_field + correlate(residual), threshold_for(level_index), tables)
    return (model_field, residual)


def dot(left, right, left_dim=1, right_dim=0):
    return lax.dot_general(
        left, right, (((left_dim,), (right_dim,)), ((), ())), preferred_element_type=jnp.float32
    )


def fixed_time_table(count):
    samples = np.arange(count)
    bins = np.arange(count // 2)[:, None]
    angles = 2.0 * np.pi / count * (bins * samples[None, :] % count)
    scale = math.sqrt(2.0 / count)
    cosine = scale * np.cos(angles)
    sine = -scale * np.sin(angles)
    cosine[0] = math.sqrt(1.0 / count)
    sine[0] = math.sqrt(1.0 / count) * np.where(samples % 2 == 0, 1.0, -1.0)
    return np.stack([cosine, sine]).astype(jnp.bfloat16)


def fixed_shot_table(count):
    positions = np.arange(count)
    angles = 2.0 * np.pi / count * (positions[:, None] * positions[None, :] % count)
    cosine = np.cos(angles) / math.sqrt(count)
    sine = np.sin(angles) / math.sqrt(count)
    table = np.stack([np.stack([cosine, sine], 1), np.stack([-sine, cosine], 1)])
    return table.astype(jnp.bfloat16).astype(np.float32)


MESH = pl.DeviceIdType.MESH
AXES = ("shot", "rcv", "rep")


def neighbours(sizes):
    every = [(a, b, c) for a in range(sizes[0]) for b in range(sizes[1]) for c in range(sizes[2])]
    far = sizes[0] // 2
    return sorted(every[1:], key=lambda step: (abs(step[0] - far), -step[1], -step[2]))


def device_at(sizes, step):
    spot = [lax.rem(lax.axis_index(axis) + hop, size) for axis, hop, size in zip(AXES, step, sizes)]
    index = (spot[0] * sizes[1] + spot[1]) * sizes[2] + spot[2]
    return dict(zip(AXES, spot)), index


def build_taps(signature_ref, adjoint, out_ref):
    count, taps = signature_ref.shape
    row_index = lax.broadcasted_iota(jnp.int32, (taps, taps), 0)
    col_index = lax.broadcasted_iota(jnp.int32, (taps, taps), 1)
    values = signature_ref[...].astype(jnp.float32)
    for index in range(count):
        row = jnp.broadcast_to(values[index : index + 1, :], (taps, taps))
        turned = pltpu.roll(row, 0, 1, stride=1, stride_axis=0)
        zeros = jnp.zeros_like(turned)
        near = jnp.where(col_index >= row_index, turned, zeros)
        far = jnp.where(col_index < row_index, turned, zeros)
        near, far = (near.T, far.T) if adjoint else (near, far)
        where = slice(index * taps, (index + 1) * taps)
        out_ref[:taps, where] = near.astype(jnp.bfloat16)
        out_ref[taps:, where] = far.astype(jnp.bfloat16)


def pick_signature(every, picks_ref):
    slots, width = picks_ref.shape
    picks = jnp.concatenate([picks_ref[...]] * (every.shape[0] // slots), axis=0)
    chosen = every[:, :width]
    for index in range(1, every.shape[1] // width):
        chosen = jnp.where(picks == index, every[:, index * width : (index + 1) * width], chosen)
    return chosen


def correlate_line(line, padded, select_ref, blocks_ref, taps_ref, picks_ref, field_ref, traces_ref):
    slots, width = picks_ref.shape
    blocks = blocks_ref[pl.ds(pl.multiple_of(line * padded, 8), padded)].astype(jnp.bfloat16)
    window = dot(select_ref[...], blocks).astype(jnp.bfloat16)
    later = jnp.concatenate([window[slots:], jnp.zeros((slots, width), window.dtype)], axis=0)
    terms = pick_signature(dot(jnp.concatenate([window, later], axis=1), taps_ref[...]), picks_ref)
    steps = terms.shape[0] // slots
    terms = jnp.concatenate(
        [terms[step * slots : (step + 1) * slots] for step in range(steps)], axis=1
    )
    where = pl.ds(pl.multiple_of(line * slots, slots), slots)
    if field_ref is not None:
        terms = terms + field_ref[where]
    traces_ref[where] = terms.astype(jnp.bfloat16)


def blend_line(line, place_ref, field_ref, taps_ref, picks_ref):
    slots, width = picks_ref.shape
    trace = field_ref[pl.ds(pl.multiple_of(line * slots, slots), slots)].astype(jnp.bfloat16)
    steps = trace.shape[1] // width
    stacked = jnp.concatenate(
        [trace[:, step * width : (step + 1) * width] for step in range(steps)], axis=0
    )
    earlier = jnp.concatenate([jnp.zeros((slots, width), trace.dtype), stacked[:-slots]], axis=0)
    shots = pick_signature(dot(jnp.concatenate([stacked, earlier], axis=1), taps_ref[...]), picks_ref)
    return dot(place_ref[...], shots.astype(jnp.bfloat16))


def spectra_chunk(table, traces_ref, out_ref, lines, rcv, slots):
    parts, rows, lanes = out_ref.shape
    bins = rows // rcv
    half = parts * bins
    pack = max(1, 16 // bins)
    together = math.gcd(len(lines), 4)
    for first in range(lines[0], lines[-1] + 1, together):
        both = dot(table, traces_ref[first * slots : (first + together) * slots], 1, 1)
        for low in range(0, together, pack):
            pieces = []
            for line in range(low, low + pack):
                piece = both[:, line * slots : (line + 1) * slots]
                joined = jnp.concatenate([piece[:half], piece[half:]], axis=1)
                pieces.append(joined.reshape(parts, bins, lanes))
            out_ref[:, (first + low) * bins : (first + low + pack) * bins] = jnp.concatenate(
                pieces, axis=1
            ).astype(jnp.bfloat16)


def bins_chunk(place, halves, spectra_ref, go_ref, back_ref, cosine, sine, level, out_ref):
    _, rows, _ = spectra_ref.shape
    rcv_count, slab_count = place.shape
    joined = jnp.concatenate(
        [
            jnp.concatenate([spectra_ref[int(index)] for index in line], axis=1)
            for line in place
        ],
        axis=0,
    )
    section = dot(joined, go_ref[...]).astype(jnp.bfloat16)
    half = section.shape[1] // 2
    near = dot(cosine, section)
    far = dot(sine, section)
    real = near[:, :half] + far[:, half:]
    imag = near[:, half:] - far[:, :half]
    factor = 1.0 - level / jnp.maximum(jnp.sqrt(real * real + imag * imag), level)
    shrunk = jnp.concatenate([real * factor, imag * factor], axis=1).astype(jnp.bfloat16)
    near = dot(cosine, shrunk)
    far = dot(sine, shrunk)
    section = jnp.concatenate(
        [near[:, :half] - far[:, half:], far[:, :half] + near[:, half:]], axis=1
    ).astype(jnp.bfloat16)
    result = dot(section, back_ref[...], 1, 1).astype(jnp.bfloat16)
    width = result.shape[1] // slab_count
    for line in range(rcv_count):
        for slab in range(slab_count):
            piece = result[line * rows : (line + 1) * rows, slab * width : (slab + 1) * width]
            if halves == 2:
                piece = jnp.concatenate([piece[: rows // 2], piece[rows // 2 :]], axis=1)
            out_ref[int(place[line, slab])] = piece


def level_of(levels_ref, index, first, bins, copies_of):
    width = levels_ref.shape[1]
    lane = lax.broadcasted_iota(jnp.int32, (bins, width), 1)
    row = lax.broadcasted_iota(jnp.int32, (bins, width), 0)
    values = jnp.broadcast_to(levels_ref[index : index + 1, :], (bins, width))
    column = jnp.sum(jnp.where(lane == row + first, values, 0.0), axis=1, keepdims=True)
    return jnp.concatenate([column] * copies_of, axis=0)


def upright(spectra_ref, chunk, lines, bins, group_lanes):
    parts = spectra_ref.shape[1]
    pack = max(1, 16 // bins)
    count = group_lanes // 2
    pieces = []
    for low_line in range(lines[0], lines[-1] + 1, pack):
        block = spectra_ref[chunk, :, low_line * bins : (low_line + pack) * bins].astype(jnp.float32)
        for line in range(pack):
            turned = block[:, line * bins : (line + 1) * bins].reshape(parts * bins, -1).T
            turned = turned.astype(jnp.bfloat16)
            for low in range(0, turned.shape[0], group_lanes):
                pieces.append(
                    jnp.concatenate(
                        [turned[low : low + count], turned[low + count : low + 2 * count]], axis=1
                    )
                )
    return jnp.concatenate(pieces, axis=0)


CHUNKS = 2
SPANS = 3


def whole_kernel(
    sizes,
    place,
    offsets_ref,
    filters_ref,
    signatures_ref,
    levels_ref,
    records_hbm,
    table_hbm,
    grid_hbm,
    row_table_hbm,
    cosine_hbm,
    sine_hbm,
    final_ref,
    left_ref,
    records_ref,
    table_ref,
    grid_ref,
    row_table_ref,
    cosine_ref,
    sine_ref,
    row_ref,
    rows_ref,
    rim_ref,
    picks_ref,
    slot_table_ref,
    adjoint_ref,
    forward_ref,
    select_ref,
    place_ref,
    traces_ref,
    field_ref,
    blocks_ref,
    rest_ref,
    head_ref,
    spill_ref,
    carried_ref,
    ahead_ref,
    sent_ref,
    got_ref,
    answer_ref,
    home_ref,
    reply_ref,
    load_sems,
    row_sends,
    row_recvs,
    go_sends,
    go_recvs,
    back_sends,
    back_recvs,
    rim_sends,
    rim_recvs,
):
    slots, width = picks_ref.shape
    rcv, slab_len = records_ref.shape
    blocks = slab_len // width
    padded = blocks_ref.shape[0] // rcv
    chunks, _, samples = table_ref.shape
    steps = samples // width
    parts = place.size
    slab_count = place.shape[1]
    few = samples // 2 // parts // chunks
    quarter = rcv // 4
    early_spans = ((0, quarter), (quarter, 2 * quarter), (2 * quarter, rcv))
    late_spans = ((0, 2 * quarter), (2 * quarter, 3 * quarter), (3 * quarter, rcv))
    edge = head_ref.shape[1]
    all_rcv = rcv * place.shape[0]
    shot_count = offsets_ref.shape[1]
    row_count = slab_count
    capacity = slots // row_count
    wide = jnp.float32

    loads = [
        pltpu.make_async_copy(source, target, load_sems.at[number])
        for number, (source, target) in enumerate(
            (
                (records_hbm, records_ref),
                (table_hbm, table_ref),
                (grid_hbm, grid_ref),
                (cosine_hbm, cosine_ref),
                (sine_hbm, sine_ref),
                (row_table_hbm, row_table_ref),
            )
        )
    ]
    for load in loads:
        load.start()
    barrier = pltpu.get_barrier_semaphore()
    hops = neighbours(sizes)
    for hop in hops:
        pl.semaphore_signal(barrier, inc=1, device_id=device_at(sizes, hop)[0], device_id_type=MESH)
    mine = device_at(sizes, (0, 0, 0))[1]
    slab = lax.axis_index("shot") * sizes[2] + lax.axis_index("rep")
    last_slab = slab_count - 1

    def slab_device(shift):
        other = lax.rem(slab + shift + slab_count, slab_count)
        return {
            "shot": other // sizes[2],
            "rcv": lax.axis_index("rcv"),
            "rep": lax.rem(other, sizes[2]),
        }

    row_ref[...] = jnp.zeros_like(row_ref)
    row_ref[0:1, :shot_count] = offsets_ref[...]
    row_ref[1:2, :shot_count] = filters_ref[...]
    build_taps(signatures_ref, True, adjoint_ref)
    pl.semaphore_wait(barrier, len(hops))

    tile = row_ref.shape[0]
    here = pl.ds(pl.multiple_of(slab * tile, tile), tile)
    row_copies = []
    for hop in hops:
        if hop[1] == 0:
            number = len(row_copies)
            copy = pltpu.make_async_remote_copy(
                src_ref=row_ref,
                dst_ref=rows_ref.at[here],
                send_sem=row_sends.at[number],
                recv_sem=row_recvs.at[number],
                device_id=device_at(sizes, hop)[0],
                device_id_type=MESH,
            )
            copy.start()
            row_copies.append(copy)
    rows_ref[here] = row_ref[...]
    loads[0].wait()
    first_rim = pltpu.make_async_remote_copy(
        src_ref=records_ref.at[:, pl.ds(0, rim_ref.shape[1])],
        dst_ref=rim_ref,
        send_sem=rim_sends.at[SPANS, 0],
        recv_sem=rim_recvs.at[SPANS, 0],
        device_id=slab_device(-1),
        device_id_type=MESH,
    )

    @pl.when(slab > 0)
    def _():
        first_rim.start()

    for line in range(rcv):
        blocks_ref[line * padded + blocks : (line + 1) * padded] = jnp.zeros(
            (padded - blocks, width), wide
        )
    for block in range(blocks):
        blocks_ref[pl.ds(block, rcv, stride=padded), :] = records_ref[
            :, block * width : (block + 1) * width
        ]
    for copy in row_copies:
        copy.wait_recv()

    lane = lax.broadcasted_iota(jnp.int32, (row_count, width), 1)
    valid = lane < shot_count
    zero = jnp.zeros((row_count, width), jnp.int32)
    start_sample = jnp.where(valid, rows_ref[pl.ds(0, row_count, stride=tile), :], zero)
    signature = jnp.where(valid, rows_ref[pl.ds(1, row_count, stride=tile), :], zero)
    block_bits = width.bit_length() - 1
    slab_bits = slab_len.bit_length() - 1
    owner = lax.shift_right_logical(start_sample, slab_bits)
    rank = zero
    for step in range(1, shot_count):
        same = (pltpu.roll(owner, step, 1) == owner) & (lane >= step)
        rank = rank + same.astype(jnp.int32)
    key = jnp.where(valid, owner * capacity + rank + 1, zero)
    first_block = (lax.shift_right_logical(start_sample, block_bits) & (blocks - 1)).astype(wide)
    signature = signature.astype(wide)
    firsts, picks = [], []
    for level in range(capacity):
        taken = key == slab * capacity + level + 1
        empty = jnp.zeros_like(first_block)
        firsts.append(jnp.sum(jnp.where(taken, first_block + 1.0, empty), axis=1, keepdims=True))
        picks.append(jnp.sum(jnp.where(taken, signature, empty), axis=1, keepdims=True))
    firsts = jnp.broadcast_to(jnp.concatenate(firsts, axis=0), (slots, padded))
    firsts = jnp.where(firsts > 0.5, firsts - 1.0, -float(samples))
    picks_ref[...] = jnp.broadcast_to(jnp.concatenate(picks, axis=0), (slots, width))
    block_index = lax.broadcasted_iota(jnp.int32, (slots, padded), 1).astype(wide)
    select = jnp.concatenate(
        [(block_index == firsts + float(step)).astype(wide) for step in range(steps)], axis=0
    )
    select_ref[...] = select.astype(jnp.bfloat16)

    @pl.when(slab < last_slab)
    def _():
        first_rim.wait_recv()
        for step in range(rim_ref.shape[1] // width):
            blocks_ref[pl.ds(blocks + step, rcv, stride=padded), :] = rim_ref[
                :, step * width : (step + 1) * width
            ]

    loads[1].wait()

    def exchange(source, target, send_sems, recv_sems, low, rows):
        made = []
        where = pl.ds(low, rows)
        for number, hop in enumerate(hops):
            device, index = device_at(sizes, hop)
            copy = pltpu.make_async_remote_copy(
                src_ref=source.at[index, where],
                dst_ref=target.at[mine, where],
                send_sem=send_sems.at[number],
                recv_sem=recv_sems.at[number],
                device_id=device,
                device_id_type=MESH,
            )
            copy.start()
            made.append(copy)
        target[mine, where] = source[mine, where]
        return made

    def send_span(number, span, from_ref, model):
        def one(line, carry):
            correlate_line(
                line, padded, select_ref, from_ref, adjoint_ref, picks_ref, model, traces_ref
            )
            return carry

        lax.fori_loop(span[0], span[1], one, 0)
        made = []
        for chunk in range(chunks):
            spectra_chunk(
                table_ref[chunk], traces_ref, sent_ref.at[chunk], range(*span), rcv, slots
            )
            made.append(
                exchange(
                    sent_ref.at[chunk],
                    got_ref.at[chunk],
                    go_sends.at[number, chunk],
                    go_recvs.at[number, chunk],
                    span[0] * few,
                    (span[1] - span[0]) * few,
                )
            )
        return made

    def level_at(index, chunk):
        return level_of(levels_ref, index, (mine * chunks + chunk) * few, few, all_rcv)

    going = [
        send_span(number, span, blocks_ref, None) for number, span in enumerate(early_spans)
    ]

    place_ref[...] = select.T.astype(jnp.bfloat16)
    build_taps(signatures_ref, False, forward_ref)
    repeated = key
    for shift in range(shot_count, width, shot_count):
        repeated = repeated + pltpu.roll(key, shift, 1)
    points = row_count * shot_count
    repeated = jnp.concatenate([repeated] * (points // width), axis=1)
    point = lax.broadcasted_iota(jnp.int32, (row_count, points), 1)
    row = lax.broadcasted_iota(jnp.int32, (row_count, points), 0)
    shot_bits = shot_count.bit_length() - 1
    repeated = jnp.where(lax.shift_right_logical(point, shot_bits) == row, repeated, 0)
    chosen = jnp.concatenate(
        [(repeated == number + 1).astype(wide) for number in range(slab_count * capacity)], axis=0
    ).astype(jnp.bfloat16)
    for load in loads[2:]:
        load.wait()
    for half in range(2):
        part = dot(chosen, grid_ref[half * points : (half + 1) * points]).astype(jnp.bfloat16)
        for number in range(slab_count):
            low = (2 * number + half) * slots
            slot_table_ref[low : low + slots] = part[number * slots : (number + 1) * slots]

    coming = {}

    def send_back(number, chunk):
        span = late_spans[number]
        coming[number, chunk] = exchange(
            answer_ref.at[chunk],
            home_ref.at[chunk],
            back_sends.at[number, chunk],
            back_recvs.at[number, chunk],
            span[0] * few,
            (span[1] - span[0]) * few,
        )

    for chunk in range(chunks):
        for made in going:
            for copy in made[chunk]:
                copy.wait_recv()
        bins_chunk(
            place, 1, got_ref.at[chunk], slot_table_ref, slot_table_ref, cosine_ref[...], sine_ref[...], level_at(0, chunk), answer_ref.at[chunk]
        )
        send_back(0, chunk)
    for number in range(1, SPANS):
        for chunk in range(chunks):
            send_back(number, chunk)
    for copy in row_copies:
        copy.wait_send()

    @pl.when(slab > 0)
    def _():
        first_rim.wait_send()

    for made in going:
        for chunk in made:
            for copy in chunk:
                copy.wait_send()

    def halo(number):
        low, high = late_spans[number]
        where = pl.ds(low, high - low)
        onward = pltpu.make_async_remote_copy(
            src_ref=spill_ref.at[where],
            dst_ref=carried_ref.at[where],
            send_sem=rim_sends.at[number, 0],
            recv_sem=rim_recvs.at[number, 0],
            device_id=slab_device(1),
            device_id_type=MESH,
        )
        backward = pltpu.make_async_remote_copy(
            src_ref=head_ref.at[where],
            dst_ref=ahead_ref.at[where],
            send_sem=rim_sends.at[number, 1],
            recv_sem=rim_recvs.at[number, 1],
            device_id=slab_device(-1),
            device_id_type=MESH,
        )
        return onward, backward

    def subtract(number):
        low, high = late_spans[number]
        for chunk in range(chunks):
            for copy in coming[number, chunk]:
                copy.wait_recv()
        together = math.gcd(high - low, 4)
        for first in range(low, high, together):
            lines = range(first, first + together)
            field_ref[first * slots : (first + together) * slots] = sum(
                dot(upright(home_ref, chunk, lines, few, 2 * slots), table_ref[chunk])
                for chunk in range(chunks)
            )

        def one(line, carry):
            blended = blend_line(line, place_ref, field_ref, forward_ref, picks_ref)
            start = pl.multiple_of(line * padded, 8)
            left = blocks_ref[pl.ds(start, blocks)] - blended[:blocks]
            rest_ref[pl.ds(start, blocks)] = left
            rest_ref[pl.ds(start + blocks, padded - blocks)] = jnp.zeros(
                (padded - blocks, width), wide
            )
            head_ref[line] = left[:edge]
            spill_ref[line] = blended[blocks : blocks + edge]
            return carry

        lax.fori_loop(low, high, one, 0)
        onward, backward = halo(number)

        @pl.when(slab < last_slab)
        def _():
            onward.start()

        @pl.when(slab > 0)
        def _():
            backward.start()

    def correlate_rest(number):
        low, high = late_spans[number]
        onward, backward = halo(number)

        @pl.when(slab > 0)
        def _():
            onward.wait_recv()
            for line in range(low, high):
                here = pl.ds(line * padded, edge)
                rest_ref[here] = rest_ref[here] - carried_ref[line]

        @pl.when(slab < last_slab)
        def _():
            backward.wait_recv()
            for line in range(low, high):
                rest_ref[pl.ds(line * padded + blocks, edge)] = ahead_ref[line] - spill_ref[line]
            onward.wait_send()

        @pl.when(slab > 0)
        def _():
            backward.wait_send()

        return send_span(number, late_spans[number], rest_ref, field_ref)

    again = []
    subtract(0)
    for number in range(1, SPANS):
        subtract(number)
        again.append(correlate_rest(number - 1))
    again.append(correlate_rest(SPANS - 1))

    for block in range(blocks):
        left_ref[:, block * width : (block + 1) * width] = rest_ref[
            pl.ds(block, rcv, stride=padded), :
        ]
    for made in coming.values():
        for copy in made:
            copy.wait_send()
    final = []
    for chunk in range(chunks):
        for made in again:
            for copy in made[chunk]:
                copy.wait_recv()
        bins_chunk(
            place, 2, got_ref.at[chunk], slot_table_ref, row_table_ref, cosine_ref[...], sine_ref[...], level_at(1, chunk), reply_ref.at[chunk]
        )
        final.append(
            exchange(
                reply_ref.at[chunk], final_ref.at[chunk], back_sends.at[0, chunk], back_recvs.at[0, chunk], 0, reply_ref.shape[2]
            )
        )
    for made in again:
        for chunk in made:
            for copy in chunk:
                copy.wait_send()
    for made in final:
        for copy in made:
            copy.wait()


def finish_kernel(bins, spectra_ref, left_ref, table_ref, model_ref, out_ref, sem):
    chunks = spectra_ref.shape[0]
    groups, together, count, _ = model_ref.shape
    step = pl.program_id(0)
    copy = pltpu.make_async_copy(left_ref, out_ref, sem)

    @pl.when(step == 0)
    def _():
        copy.start()

    fields = sum(
        dot(upright(spectra_ref, chunk, range(together), bins, 2 * count), table_ref[chunk])
        for chunk in range(chunks)
    )
    for line in range(together):
        for group in range(groups):
            low = (line * groups + group) * count
            model_ref[group, line] = fields[low : low + count]

    @pl.when(step == pl.num_programs(0) - 1)
    def _():
        copy.wait()


def finish(spectra, left, table, groups, rcv):
    chunks, parts, rows, lanes = spectra.shape
    samples = table.shape[2]
    bins = rows // rcv
    count = lanes // 2 // groups
    together = math.gcd(rcv, 4)
    whole = pl.BlockSpec(memory_space=pltpu.VMEM)
    return pl.pallas_call(
        functools.partial(finish_kernel, bins),
        grid=(rcv // together,),
        out_shape=(
            jax.ShapeDtypeStruct((groups, rcv, count, samples), jnp.float32),
            jax.ShapeDtypeStruct(left.shape, jnp.float32),
        ),
        in_specs=[
            pl.BlockSpec((chunks, parts, together * bins, lanes), lambda i: (0, 0, i, 0)),
            whole,
            whole,
        ],
        out_specs=(
            pl.BlockSpec((groups, together, count, samples), lambda i: (0, i, 0, 0)),
            pl.BlockSpec(memory_space=pl.ANY),
        ),
        scratch_shapes=[pltpu.SemaphoreType.DMA],
        compiler_params=pltpu.CompilerParams(vmem_limit_bytes=16 * 2**20),
    )(spectra, left, table)


def body_by_slots(records, offsets, filter_index, signatures, thresholds):
    rows_here, shot_count = offsets.shape
    local_rcv, slab_len = records.shape
    slab_count = lax.axis_size(("shot", "rep"))
    rep_count = lax.axis_size("rep")
    rcv_count = lax.axis_size("rcv")
    sizes = tuple(lax.axis_size(axis) for axis in AXES)
    parts = slab_count * rcv_count
    tap_count = signatures.shape[1]
    slab_blocks = slab_len // tap_count
    steps = NT // tap_count
    capacity = max(2, 2 * shot_count // slab_count)
    row_count = rows_here * slab_count
    slots = row_count * capacity
    bins = NT // 2 // parts
    chunks = CHUNKS
    few = bins // chunks
    place = np.array(
        [
            [((slab // rep_count) * rcv_count + line) * rep_count + slab % rep_count for slab in range(slab_count)]
            for line in range(rcv_count)
        ]
    )

    time_table_fixed = fixed_time_table(NT).reshape(2, parts, chunks, few, NT)
    time_table_fixed = jnp.asarray(
        np.ascontiguousarray(time_table_fixed.transpose(2, 0, 1, 3, 4)).reshape(chunks, NT // chunks, NT)
    )
    table_x, table_y, table_r = (
        fixed_shot_table(count) for count in (row_count, shot_count, local_rcv * rcv_count)
    )
    grid_table = np.einsum("ajby,bkcx->cxyakj", table_y, table_x).astype(jnp.bfloat16)
    row_table = np.ascontiguousarray(grid_table.transpose(1, 0, 2, 3, 4, 5))
    points = 2 * row_count * shot_count
    grid_table = jnp.asarray(grid_table.reshape(points, points))
    row_table = jnp.asarray(row_table.reshape(points, points))
    same = np.eye(few, dtype=np.float32)
    cosine = jnp.asarray(np.kron(table_r[0, :, 0], same).astype(jnp.bfloat16))
    sine = jnp.asarray(np.kron(table_r[0, :, 1], same).astype(jnp.bfloat16))

    edge = 8
    padded = slab_blocks + 2 * edge
    vmem = pl.BlockSpec(memory_space=pltpu.VMEM)
    anywhere = pl.BlockSpec(memory_space=pl.ANY)
    rows = local_rcv * few
    table_width = tap_count * signatures.shape[0]
    low, wide = jnp.bfloat16, jnp.float32
    big = (records, time_table_fixed, grid_table, row_table, cosine, sine)
    spectra, residual = pl.pallas_call(
        functools.partial(whole_kernel, sizes, place),
        out_shape=(
            pltpu.VMEM((chunks, parts, rows // 2, 4 * shot_count), low),
            pltpu.VMEM(records.shape, wide),
        ),
        in_specs=[vmem] * 4 + [anywhere] * len(big),
        out_specs=(vmem, vmem),
        scratch_shapes=[pltpu.VMEM(array.shape, array.dtype) for array in big]
        + [
            pltpu.VMEM((edge, tap_count), jnp.int32),
            pltpu.VMEM((slab_count * edge, tap_count), jnp.int32),
            pltpu.VMEM((local_rcv, (steps - 1) * tap_count), wide),
            pltpu.VMEM((slots, tap_count), wide),
            pltpu.VMEM((slab_count * 2 * slots, points), low),
            pltpu.VMEM((2 * tap_count, table_width), low),
            pltpu.VMEM((2 * tap_count, table_width), low),
            pltpu.VMEM((slots * steps, padded), low),
            pltpu.VMEM((padded, slots * steps), low),
            pltpu.VMEM((local_rcv * slots, NT), low),
            pltpu.VMEM((local_rcv * slots, NT), wide),
            pltpu.VMEM((local_rcv * padded, tap_count), wide),
            pltpu.VMEM((local_rcv * padded, tap_count), wide),
        ]
        + [pltpu.VMEM((local_rcv, edge, tap_count), wide)] * 4
        + [pltpu.VMEM((chunks, parts, rows, 2 * slots), low)] * 4
        + [pltpu.VMEM((chunks, parts, rows // 2, 4 * shot_count), low)]
        + [pltpu.SemaphoreType.DMA((len(big),))]
        + [pltpu.SemaphoreType.DMA((slab_count - 1,))] * 2
        + [pltpu.SemaphoreType.DMA((SPANS, chunks, parts - 1))] * 4
        + [pltpu.SemaphoreType.DMA((SPANS + 1, 2))] * 2,
        compiler_params=pltpu.CompilerParams(
            collective_id=0, has_side_effects=True, vmem_limit_bytes=60 * 2**20
        ),
    )(offsets, filter_index, signatures, thresholds, *big)
    model, residual = finish(spectra, residual, time_table_fixed, 2, local_rcv // 2)
    return (model.reshape(rows_here, local_rcv, shot_count, NT), residual)


def body(records, offsets, filter_index, signatures, thresholds):
    rows_here, shot_count = offsets.shape
    slab_count = lax.axis_size(("shot", "rep"))
    parts = slab_count * lax.axis_size("rcv")
    slots = rows_here * slab_count * max(2, 2 * shot_count // slab_count)
    table_rows = 2 * rows_here * slab_count * shot_count
    fits = table_rows <= 1024 and rows_here == 1 and slots == 64 and 4 * shot_count == 128
    fits = fits and records.shape[0] == 16 and NT // 2 // parts == 16
    slab_len, tap_count = records.shape[1], signatures.shape[1]
    fits = fits and tap_count == 128 and slab_len & (slab_len - 1) == 0
    run = body_by_slots if fits else body_by_rows
    return run(records, offsets, filter_index, signatures, thresholds)


def solution(mesh):
    in_specs = (
        P(("groups", "rcv"), ("shot", "rep")),
        P(("groups", "shot", "rep"), None),
        P(("groups", "shot", "rep"), None),
        P(),
        P(),
    )
    out_specs = (
        P(("groups", "shot", "rep"), "rcv", None, None),
        P(("groups", "rcv"), ("shot", "rep")),
    )
    return jax.shard_map(body, mesh=mesh, in_specs=in_specs, out_specs=out_specs, check_vma=False)
```

```python
import functools
import math

import jax
import jax.numpy as jnp
import numpy as np
from jax import lax
from jax.experimental import pallas as pl
from jax.experimental.pallas import tpu as pltpu
from jax.sharding import PartitionSpec as P

NT = 512


def from_behind(value, axis, steps):
    count = lax.axis_size(axis)
    first, last = (max(0, -steps), min(count, count - steps))
    return lax.ppermute(value, axis, [(source, source + steps) for source in range(first, last)])


def time_table(count):
    samples = jnp.arange(count)
    bin_index = jnp.arange(count // 2)[:, None]
    angles = 2.0 * math.pi / count * (bin_index * samples[None, :] % count).astype(jnp.float32)
    parity = jnp.where(samples % 2 == 0, 1.0, -1.0).astype(jnp.float32)
    cosine = jnp.where(bin_index == 0, math.sqrt(1.0 / count), math.sqrt(2.0 / count)) * jnp.cos(
        angles
    )
    sine_part = jnp.where(
        bin_index == 0,
        math.sqrt(1.0 / count) * parity[None, :],
        -math.sqrt(2.0 / count) * jnp.sin(angles),
    )
    return jnp.stack([cosine, sine_part]).astype(jnp.bfloat16)


def shot_table(count):
    positions = jnp.arange(count)
    angles = (
        2.0
        * math.pi
        / count
        * (positions[:, None] * positions[None, :] % count).astype(jnp.float32)
    )
    scaling = 1.0 / math.sqrt(count)
    cosine = scaling * jnp.cos(angles)
    sine_part = scaling * jnp.sin(angles)
    upper_half = jnp.stack([cosine, sine_part], axis=1)
    lower_half = jnp.stack([-sine_part, cosine], axis=1)
    return jnp.stack([upper_half, lower_half]).astype(jnp.bfloat16)


def toeplitz_kernel(adjoint, taps_ref, out_ref):
    tap_count = taps_ref.shape[1]
    row_index = lax.broadcasted_iota(jnp.int32, (tap_count, tap_count), 0)
    col_index = lax.broadcasted_iota(jnp.int32, (tap_count, tap_count), 1)
    taps = taps_ref[...].astype(jnp.float32)
    for index in range(taps_ref.shape[0]):
        row = jnp.broadcast_to(taps[index : index + 1, :], (tap_count, tap_count))
        turned = pltpu.roll(row, 0, 1, stride=1, stride_axis=0)
        zeros = jnp.zeros_like(turned)
        near = jnp.where(col_index >= row_index, turned, zeros)
        far = jnp.where(col_index < row_index, turned, zeros)
        near, far = (near.T, far.T) if adjoint else (near, far)
        out_ref[index, :tap_count, :] = near.astype(jnp.bfloat16)
        out_ref[index, tap_count:, :] = far.astype(jnp.bfloat16)


def toeplitz_table(signatures, adjoint):
    count, tap_count = signatures.shape
    return pl.pallas_call(
        functools.partial(toeplitz_kernel, adjoint),
        out_shape=jax.ShapeDtypeStruct((count, 2 * tap_count, tap_count), jnp.bfloat16),
        in_specs=[pl.BlockSpec(memory_space=pltpu.VMEM)],
        out_specs=pl.BlockSpec(memory_space=pltpu.VMEM),
    )(signatures)


def apply_filter(traces, table, adjoint):
    empty = jnp.zeros_like(traces[:, :1])
    if adjoint:
        other = jnp.concatenate([traces[:, 1:], empty], axis=1)
    else:
        other = jnp.concatenate([empty, traces[:, :-1]], axis=1)
    return jnp.einsum(
        "sbrp,spq->sbrq",
        jnp.concatenate([traces, other], axis=3),
        table,
        preferred_element_type=jnp.float32,
    )


def rank_in_row(owners):
    shot_count = owners.shape[1]
    same_owner = owners[:, :, None] == owners[:, None, :]
    earlier = jnp.arange(shot_count)[None, :] < jnp.arange(shot_count)[:, None]
    return jnp.sum(same_owner & earlier[None], axis=2)


def to_slabs(payload):
    return lax.all_to_all(payload, ("shot", "rep"), split_axis=0, concat_axis=0, tiled=True)


def to_shots(payload):
    return lax.all_to_all(payload, ("shot", "rep"), split_axis=0, concat_axis=0, tiled=True)


def soft_limit(coefficients, threshold_row):
    magnitude = jnp.sqrt(coefficients[0] * coefficients[0] + coefficients[1] * coefficients[1])
    threshold_view = threshold_row[None, :, None, None]
    factor = 1.0 - threshold_view / jnp.maximum(magnitude, threshold_view)
    return (coefficients * factor[None]).astype(jnp.bfloat16)


def shrink(field_data, threshold_row, tables):
    table_time, table_x, table_y, table_r = tables
    rows_here, local_rcv, shot_count, sample_count = field_data.shape
    spectrum = jnp.einsum(
        "ckt,xryt->xckry",
        table_time,
        field_data.astype(jnp.bfloat16),
        preferred_element_type=jnp.float32,
    ).astype(jnp.bfloat16)
    bin_count = spectrum.shape[2]
    spectrum = spectrum.reshape(rows_here, 2, bin_count, local_rcv * shot_count)
    section_data = jnp.einsum(
        "akbx,xbfz->akfz",
        table_x,
        lax.all_to_all(spectrum, ("shot", "rep"), split_axis=2, concat_axis=0, tiled=True),
        preferred_element_type=jnp.float32,
    ).astype(jnp.bfloat16)
    all_rows, row_bins = (section_data.shape[1], section_data.shape[2])
    section_data = section_data.reshape(2, all_rows, row_bins, local_rcv, shot_count)
    section_data = lax.all_to_all(section_data, "rcv", split_axis=2, concat_axis=3, tiled=True)
    section_data = jnp.einsum(
        "ajby,bkfry->akfrj", table_y, section_data, preferred_element_type=jnp.float32
    ).astype(jnp.bfloat16)
    coefficients = jnp.einsum(
        "aqbr,bkfrj->akfqj", table_r, section_data, preferred_element_type=jnp.float32
    )
    shrunk = soft_limit(coefficients, threshold_row)
    section_data = jnp.einsum(
        "aqbr,akfqj->bkfrj", table_r, shrunk, preferred_element_type=jnp.float32
    ).astype(jnp.bfloat16)
    section_data = jnp.einsum(
        "ajby,akfrj->bkfry", table_y, section_data, preferred_element_type=jnp.float32
    ).astype(jnp.bfloat16)
    section_data = lax.all_to_all(section_data, "rcv", split_axis=3, concat_axis=2, tiled=True)
    section_data = section_data.reshape(2, all_rows, row_bins, local_rcv * shot_count)
    section_data = jnp.einsum(
        "akbx,akfz->bxfz", table_x, section_data, preferred_element_type=jnp.float32
    ).astype(jnp.bfloat16)
    result = jnp.einsum(
        "ckt,cxkz->xzt",
        table_time,
        lax.all_to_all(section_data, ("shot", "rep"), split_axis=1, concat_axis=2, tiled=True),
        preferred_element_type=jnp.float32,
    )
    return result.reshape(rows_here, local_rcv, shot_count, sample_count)


def body_by_rows(records, offsets, filter_index, signatures, thresholds):
    rows_here, shot_count = offsets.shape
    local_rcv, slab_len = records.shape
    slab_count = lax.axis_size(("shot", "rep"))
    rcv_count = lax.axis_size("rcv")
    tap_count = signatures.shape[1]
    sample_count = NT
    slab_blocks = slab_len // tap_count
    trace_blocks = sample_count // tap_count
    capacity = max(2, 2 * shot_count // slab_count)
    slot_count = slab_count * rows_here * capacity
    forward_tables = toeplitz_table(signatures, False)
    adjoint_tables = toeplitz_table(signatures, True)
    flat_index = filter_index.reshape(-1)
    forward_table = forward_tables[flat_index]
    adjoint_table = adjoint_tables[flat_index]
    owners = offsets // slab_len
    row_ids = jnp.arange(rows_here, dtype=jnp.int32)[:, None]
    slot_index = (
        owners * (rows_here * capacity) + row_ids * capacity + rank_in_row(owners)
    ).reshape(-1)
    every_offset = lax.all_gather(offsets, ("shot", "rep"), axis=0, tiled=True)
    every_owner = every_offset // slab_len
    every_start = every_offset // tap_count % slab_blocks
    every_rank = rank_in_row(every_owner)
    mine_mask = every_owner == lax.axis_index(("shot", "rep"))
    levels = jnp.arange(capacity, dtype=jnp.int32)
    picked = mine_mask[:, :, None] & (every_rank[:, :, None] == levels[None, None, :])
    table_in = jnp.sum(jnp.where(picked, every_start[:, :, None] + 1, 0), axis=1).reshape(-1)
    filled = table_in > 0
    block_steps = jnp.arange(trace_blocks, dtype=jnp.int32)
    target = jnp.where(
        filled[:, None],
        table_in[:, None] - 1 + block_steps[None, :],
        slab_blocks + trace_blocks - 1,
    )

    def correlate(record_field):
        record_low = (
            record_field.astype(jnp.bfloat16)
            .reshape(local_rcv, slab_blocks, tap_count)
            .transpose(1, 0, 2)
        )
        rim_blocks = from_behind(record_low[: trace_blocks - 1], ("shot", "rep"), -1)
        extended = jnp.concatenate(
            [record_low, rim_blocks, jnp.zeros((1, local_rcv, tap_count), jnp.bfloat16)], axis=0
        )
        windows = extended[target.reshape(-1)].reshape(
            slot_count, trace_blocks, local_rcv, tap_count
        )
        returned = to_shots(windows)
        traces = returned[slot_index]
        terms = apply_filter(traces, adjoint_table, True)
        terms = terms.reshape(rows_here, shot_count, trace_blocks, local_rcv, tap_count).transpose(
            0, 3, 1, 2, 4
        )
        return terms.reshape(rows_here, local_rcv, shot_count, sample_count)

    tables = (
        time_table(sample_count),
        shot_table(slab_count * rows_here),
        shot_table(shot_count),
        shot_table(local_rcv * rcv_count),
    )
    row_bins = sample_count // 2 // slab_count
    rcv_bins = row_bins // rcv_count
    bin_start = lax.axis_index(("shot", "rep")) * row_bins + lax.axis_index("rcv") * rcv_bins

    def threshold_for(level_index):
        return lax.dynamic_slice_in_dim(thresholds[level_index], bin_start, rcv_bins)

    model_field = shrink(correlate(records), threshold_for(0), tables)
    level_index = 1
    traces = model_field.astype(jnp.bfloat16).reshape(
        rows_here, local_rcv, shot_count, trace_blocks, tap_count
    )
    traces = traces.transpose(0, 2, 3, 1, 4).reshape(
        rows_here * shot_count, trace_blocks, local_rcv, tap_count
    )
    shots = apply_filter(traces, forward_table, False).astype(jnp.bfloat16)
    outgoing = (
        jnp.zeros((slot_count, trace_blocks, local_rcv, tap_count), jnp.bfloat16)
        .at[slot_index]
        .set(shots)
    )
    arrived = to_slabs(outgoing)
    slab_total = jnp.zeros((slab_blocks + trace_blocks, local_rcv, tap_count), jnp.float32)
    for block_step in range(trace_blocks):
        slab_total = slab_total.at[target[:, block_step]].add(
            arrived[:, block_step].astype(jnp.float32)
        )
    spill_over = slab_total[slab_blocks : slab_blocks + trace_blocks - 1]
    carried = from_behind(spill_over, ("shot", "rep"), 1)
    blended = slab_total[:slab_blocks].at[: trace_blocks - 1].add(carried)
    residual = records - blended.transpose(1, 0, 2).reshape(local_rcv, slab_len)
    model_field = shrink(model_field + correlate(residual), threshold_for(level_index), tables)
    return (model_field, residual)


def dot(left, right, left_dim=1, right_dim=0):
    return lax.dot_general(
        left, right, (((left_dim,), (right_dim,)), ((), ())), preferred_element_type=jnp.float32
    )


def fixed_time_table(count):
    samples = np.arange(count)
    bins = np.arange(count // 2)[:, None]
    angles = 2.0 * np.pi / count * (bins * samples[None, :] % count)
    scale = math.sqrt(2.0 / count)
    cosine = scale * np.cos(angles)
    sine = -scale * np.sin(angles)
    cosine[0] = math.sqrt(1.0 / count)
    sine[0] = math.sqrt(1.0 / count) * np.where(samples % 2 == 0, 1.0, -1.0)
    return np.stack([cosine, sine]).astype(jnp.bfloat16)


def fixed_shot_table(count):
    positions = np.arange(count)
    angles = 2.0 * np.pi / count * (positions[:, None] * positions[None, :] % count)
    cosine = np.cos(angles) / math.sqrt(count)
    sine = np.sin(angles) / math.sqrt(count)
    table = np.stack([np.stack([cosine, sine], 1), np.stack([-sine, cosine], 1)])
    return table.astype(jnp.bfloat16).astype(np.float32)


MESH = pl.DeviceIdType.MESH
AXES = ("shot", "rcv", "rep")


def neighbours(sizes):
    every = [(a, b, c) for a in range(sizes[0]) for b in range(sizes[1]) for c in range(sizes[2])]
    far = sizes[0] // 2
    return sorted(every[1:], key=lambda step: (abs(step[0] - far), -step[1], -step[2]))


def device_at(sizes, step):
    spot = [lax.rem(lax.axis_index(axis) + hop, size) for axis, hop, size in zip(AXES, step, sizes)]
    index = (spot[0] * sizes[1] + spot[1]) * sizes[2] + spot[2]
    return dict(zip(AXES, spot)), index


def build_taps(signature_ref, adjoint, out_ref):
    count, taps = signature_ref.shape
    row_index = lax.broadcasted_iota(jnp.int32, (taps, taps), 0)
    col_index = lax.broadcasted_iota(jnp.int32, (taps, taps), 1)
    values = signature_ref[...].astype(jnp.float32)
    for index in range(count):
        row = jnp.broadcast_to(values[index : index + 1, :], (taps, taps))
        turned = pltpu.roll(row, 0, 1, stride=1, stride_axis=0)
        zeros = jnp.zeros_like(turned)
        near = jnp.where(col_index >= row_index, turned, zeros)
        far = jnp.where(col_index < row_index, turned, zeros)
        near, far = (near.T, far.T) if adjoint else (near, far)
        where = slice(index * taps, (index + 1) * taps)
        out_ref[:taps, where] = near.astype(jnp.bfloat16)
        out_ref[taps:, where] = far.astype(jnp.bfloat16)


def pick_signature(every, picks_ref):
    slots, width = picks_ref.shape
    picks = jnp.concatenate([picks_ref[...]] * (every.shape[0] // slots), axis=0)
    chosen = every[:, :width]
    for index in range(1, every.shape[1] // width):
        chosen = jnp.where(picks == index, every[:, index * width : (index + 1) * width], chosen)
    return chosen


def correlate_line(line, padded, select_ref, blocks_ref, taps_ref, picks_ref, field_ref, traces_ref):
    slots, width = picks_ref.shape
    blocks = blocks_ref[pl.ds(pl.multiple_of(line * padded, 8), padded)].astype(jnp.bfloat16)
    window = dot(select_ref[...], blocks).astype(jnp.bfloat16)
    later = jnp.concatenate([window[slots:], jnp.zeros((slots, width), window.dtype)], axis=0)
    terms = pick_signature(dot(jnp.concatenate([window, later], axis=1), taps_ref[...]), picks_ref)
    steps = terms.shape[0] // slots
    terms = jnp.concatenate(
        [terms[step * slots : (step + 1) * slots] for step in range(steps)], axis=1
    )
    where = pl.ds(pl.multiple_of(line * slots, slots), slots)
    if field_ref is not None:
        terms = terms + field_ref[where]
    traces_ref[where] = terms.astype(jnp.bfloat16)


def blend_line(line, place_ref, field_ref, taps_ref, picks_ref):
    slots, width = picks_ref.shape
    trace = field_ref[pl.ds(pl.multiple_of(line * slots, slots), slots)].astype(jnp.bfloat16)
    steps = trace.shape[1] // width
    stacked = jnp.concatenate(
        [trace[:, step * width : (step + 1) * width] for step in range(steps)], axis=0
    )
    earlier = jnp.concatenate([jnp.zeros((slots, width), trace.dtype), stacked[:-slots]], axis=0)
    shots = pick_signature(dot(jnp.concatenate([stacked, earlier], axis=1), taps_ref[...]), picks_ref)
    return dot(place_ref[...], shots.astype(jnp.bfloat16))


def spectra_chunk(table, traces_ref, out_ref, lines, rcv, slots):
    parts, rows, lanes = out_ref.shape
    bins = rows // rcv
    half = parts * bins
    pack = max(1, 16 // bins)
    together = math.gcd(len(lines), 4)
    for first in range(lines[0], lines[-1] + 1, together):
        both = dot(table, traces_ref[first * slots : (first + together) * slots], 1, 1)
        for low in range(0, together, pack):
            pieces = []
            for line in range(low, low + pack):
                piece = both[:, line * slots : (line + 1) * slots]
                joined = jnp.concatenate([piece[:half], piece[half:]], axis=1)
                pieces.append(joined.reshape(parts, bins, lanes))
            out_ref[:, (first + low) * bins : (first + low + pack) * bins] = jnp.concatenate(
                pieces, axis=1
            ).astype(jnp.bfloat16)


def bins_chunk(place, halves, spectra_ref, go_ref, back_ref, cosine, sine, level, out_ref):
    _, rows, _ = spectra_ref.shape
    rcv_count, slab_count = place.shape
    joined = jnp.concatenate(
        [
            jnp.concatenate([spectra_ref[int(index)] for index in line], axis=1)
            for line in place
        ],
        axis=0,
    )
    section = dot(joined, go_ref[...]).astype(jnp.bfloat16)
    half = section.shape[1] // 2
    near = dot(cosine, section)
    far = dot(sine, section)
    real = near[:, :half] + far[:, half:]
    imag = near[:, half:] - far[:, :half]
    factor = 1.0 - level / jnp.maximum(jnp.sqrt(real * real + imag * imag), level)
    shrunk = jnp.concatenate([real * factor, imag * factor], axis=1).astype(jnp.bfloat16)
    near = dot(cosine, shrunk)
    far = dot(sine, shrunk)
    section = jnp.concatenate(
        [near[:, :half] - far[:, half:], far[:, :half] + near[:, half:]], axis=1
    ).astype(jnp.bfloat16)
    result = dot(section, back_ref[...], 1, 1).astype(jnp.bfloat16)
    width = result.shape[1] // slab_count
    for line in range(rcv_count):
        for slab in range(slab_count):
            piece = result[line * rows : (line + 1) * rows, slab * width : (slab + 1) * width]
            if halves == 2:
                piece = jnp.concatenate([piece[: rows // 2], piece[rows // 2 :]], axis=1)
            out_ref[int(place[line, slab])] = piece


def level_of(levels_ref, index, first, bins, copies_of):
    width = levels_ref.shape[1]
    lane = lax.broadcasted_iota(jnp.int32, (bins, width), 1)
    row = lax.broadcasted_iota(jnp.int32, (bins, width), 0)
    values = jnp.broadcast_to(levels_ref[index : index + 1, :], (bins, width))
    column = jnp.sum(jnp.where(lane == row + first, values, 0.0), axis=1, keepdims=True)
    return jnp.concatenate([column] * copies_of, axis=0)


def upright(spectra_ref, chunk, lines, bins, group_lanes):
    parts = spectra_ref.shape[1]
    pack = max(1, 16 // bins)
    count = group_lanes // 2
    pieces = []
    for low_line in range(lines[0], lines[-1] + 1, pack):
        block = spectra_ref[chunk, :, low_line * bins : (low_line + pack) * bins].astype(jnp.float32)
        for line in range(pack):
            turned = block[:, line * bins : (line + 1) * bins].reshape(parts * bins, -1).T
            turned = turned.astype(jnp.bfloat16)
            for low in range(0, turned.shape[0], group_lanes):
                pieces.append(
                    jnp.concatenate(
                        [turned[low : low + count], turned[low + count : low + 2 * count]], axis=1
                    )
                )
    return jnp.concatenate(pieces, axis=0)


CHUNKS = 2
SPANS = 3
UNROLL = 4


def whole_kernel(
    sizes,
    place,
    offsets_ref,
    filters_ref,
    signatures_ref,
    levels_ref,
    records_hbm,
    table_hbm,
    grid_hbm,
    row_table_hbm,
    cosine_hbm,
    sine_hbm,
    final_ref,
    left_ref,
    records_ref,
    table_ref,
    grid_ref,
    row_table_ref,
    cosine_ref,
    sine_ref,
    row_ref,
    rows_ref,
    rim_ref,
    picks_ref,
    slot_table_ref,
    adjoint_ref,
    forward_ref,
    select_ref,
    place_ref,
    traces_ref,
    field_ref,
    blocks_ref,
    rest_ref,
    head_ref,
    spill_ref,
    carried_ref,
    ahead_ref,
    sent_ref,
    got_ref,
    answer_ref,
    home_ref,
    reply_ref,
    load_sems,
    row_sends,
    row_recvs,
    go_sends,
    go_recvs,
    back_sends,
    back_recvs,
    rim_sends,
    rim_recvs,
):
    slots, width = picks_ref.shape
    rcv, slab_len = records_ref.shape
    blocks = slab_len // width
    padded = blocks_ref.shape[0] // rcv
    chunks, _, samples = table_ref.shape
    steps = samples // width
    parts = place.size
    slab_count = place.shape[1]
    few = samples // 2 // parts // chunks
    quarter = rcv // 4
    early_spans = ((0, quarter), (quarter, 2 * quarter), (2 * quarter, rcv))
    late_spans = ((0, 2 * quarter), (2 * quarter, rcv))
    edge = head_ref.shape[1]
    all_rcv = rcv * place.shape[0]
    shot_count = offsets_ref.shape[1]
    row_count = slab_count
    capacity = slots // row_count
    wide = jnp.float32

    loads = [
        pltpu.make_async_copy(source, target, load_sems.at[number])
        for number, (source, target) in enumerate(
            (
                (records_hbm, records_ref),
                (table_hbm, table_ref),
                (grid_hbm, grid_ref),
                (cosine_hbm, cosine_ref),
                (sine_hbm, sine_ref),
                (row_table_hbm, row_table_ref),
            )
        )
    ]
    for load in loads:
        load.start()
    barrier = pltpu.get_barrier_semaphore()
    hops = neighbours(sizes)
    for hop in hops:
        pl.semaphore_signal(barrier, inc=1, device_id=device_at(sizes, hop)[0], device_id_type=MESH)
    mine = device_at(sizes, (0, 0, 0))[1]
    slab = lax.axis_index("shot") * sizes[2] + lax.axis_index("rep")
    last_slab = slab_count - 1

    def slab_device(shift):
        other = lax.rem(slab + shift + slab_count, slab_count)
        return {
            "shot": other // sizes[2],
            "rcv": lax.axis_index("rcv"),
            "rep": lax.rem(other, sizes[2]),
        }

    row_ref[...] = jnp.zeros_like(row_ref)
    row_ref[0:1, :shot_count] = offsets_ref[...]
    row_ref[1:2, :shot_count] = filters_ref[...]
    build_taps(signatures_ref, True, adjoint_ref)
    pl.semaphore_wait(barrier, len(hops))

    tile = row_ref.shape[0]
    here = pl.ds(pl.multiple_of(slab * tile, tile), tile)
    row_copies = []
    for hop in hops:
        if hop[1] == 0:
            number = len(row_copies)
            copy = pltpu.make_async_remote_copy(
                src_ref=row_ref,
                dst_ref=rows_ref.at[here],
                send_sem=row_sends.at[number],
                recv_sem=row_recvs.at[number],
                device_id=device_at(sizes, hop)[0],
                device_id_type=MESH,
            )
            copy.start()
            row_copies.append(copy)
    rows_ref[here] = row_ref[...]
    loads[0].wait()
    first_rim = pltpu.make_async_remote_copy(
        src_ref=records_ref.at[:, pl.ds(0, rim_ref.shape[1])],
        dst_ref=rim_ref,
        send_sem=rim_sends.at[SPANS, 0],
        recv_sem=rim_recvs.at[SPANS, 0],
        device_id=slab_device(-1),
        device_id_type=MESH,
    )

    @pl.when(slab > 0)
    def _():
        first_rim.start()

    for line in range(rcv):
        blocks_ref[line * padded + blocks : (line + 1) * padded] = jnp.zeros(
            (padded - blocks, width), wide
        )
    for block in range(blocks):
        blocks_ref[pl.ds(block, rcv, stride=padded), :] = records_ref[
            :, block * width : (block + 1) * width
        ]
    for copy in row_copies:
        copy.wait_recv()

    lane = lax.broadcasted_iota(jnp.int32, (row_count, width), 1)
    valid = lane < shot_count
    zero = jnp.zeros((row_count, width), jnp.int32)
    start_sample = jnp.where(valid, rows_ref[pl.ds(0, row_count, stride=tile), :], zero)
    signature = jnp.where(valid, rows_ref[pl.ds(1, row_count, stride=tile), :], zero)
    block_bits = width.bit_length() - 1
    slab_bits = slab_len.bit_length() - 1
    owner = lax.shift_right_logical(start_sample, slab_bits)
    rank = zero
    for step in range(1, shot_count):
        same = (pltpu.roll(owner, step, 1) == owner) & (lane >= step)
        rank = rank + same.astype(jnp.int32)
    key = jnp.where(valid, owner * capacity + rank + 1, zero)
    first_block = (lax.shift_right_logical(start_sample, block_bits) & (blocks - 1)).astype(wide)
    signature = signature.astype(wide)
    firsts, picks = [], []
    for level in range(capacity):
        taken = key == slab * capacity + level + 1
        empty = jnp.zeros_like(first_block)
        firsts.append(jnp.sum(jnp.where(taken, first_block + 1.0, empty), axis=1, keepdims=True))
        picks.append(jnp.sum(jnp.where(taken, signature, empty), axis=1, keepdims=True))
    firsts = jnp.broadcast_to(jnp.concatenate(firsts, axis=0), (slots, padded))
    firsts = jnp.where(firsts > 0.5, firsts - 1.0, -float(samples))
    picks_ref[...] = jnp.broadcast_to(jnp.concatenate(picks, axis=0), (slots, width))
    block_index = lax.broadcasted_iota(jnp.int32, (slots, padded), 1).astype(wide)
    select = jnp.concatenate(
        [(block_index == firsts + float(step)).astype(wide) for step in range(steps)], axis=0
    )
    select_ref[...] = select.astype(jnp.bfloat16)

    @pl.when(slab < last_slab)
    def _():
        first_rim.wait_recv()
        for step in range(rim_ref.shape[1] // width):
            blocks_ref[pl.ds(blocks + step, rcv, stride=padded), :] = rim_ref[
                :, step * width : (step + 1) * width
            ]

    loads[1].wait()

    def exchange(source, target, send_sems, recv_sems, low, rows):
        made = []
        where = pl.ds(low, rows)
        for number, hop in enumerate(hops):
            device, index = device_at(sizes, hop)
            copy = pltpu.make_async_remote_copy(
                src_ref=source.at[index, where],
                dst_ref=target.at[mine, where],
                send_sem=send_sems.at[number],
                recv_sem=recv_sems.at[number],
                device_id=device,
                device_id_type=MESH,
            )
            copy.start()
            made.append(copy)
        target[mine, where] = source[mine, where]
        return made

    def send_span(number, span, from_ref, model):
        def one(line, carry):
            correlate_line(
                line, padded, select_ref, from_ref, adjoint_ref, picks_ref, model, traces_ref
            )
            return carry

        lax.fori_loop(span[0], span[1], one, 0, unroll=UNROLL)
        made = []
        for chunk in range(chunks):
            spectra_chunk(
                table_ref[chunk], traces_ref, sent_ref.at[chunk], range(*span), rcv, slots
            )
            made.append(
                exchange(
                    sent_ref.at[chunk],
                    got_ref.at[chunk],
                    go_sends.at[number, chunk],
                    go_recvs.at[number, chunk],
                    span[0] * few,
                    (span[1] - span[0]) * few,
                )
            )
        return made

    def level_at(index, chunk):
        return level_of(levels_ref, index, (mine * chunks + chunk) * few, few, all_rcv)

    going = [
        send_span(number, span, blocks_ref, None) for number, span in enumerate(early_spans)
    ]

    place_ref[...] = select.T.astype(jnp.bfloat16)
    build_taps(signatures_ref, False, forward_ref)
    repeated = key
    for shift in range(shot_count, width, shot_count):
        repeated = repeated + pltpu.roll(key, shift, 1)
    points = row_count * shot_count
    repeated = jnp.concatenate([repeated] * (points // width), axis=1)
    point = lax.broadcasted_iota(jnp.int32, (row_count, points), 1)
    row = lax.broadcasted_iota(jnp.int32, (row_count, points), 0)
    shot_bits = shot_count.bit_length() - 1
    repeated = jnp.where(lax.shift_right_logical(point, shot_bits) == row, repeated, 0)
    chosen = jnp.concatenate(
        [(repeated == number + 1).astype(wide) for number in range(slab_count * capacity)], axis=0
    ).astype(jnp.bfloat16)
    for load in loads[2:]:
        load.wait()
    for half in range(2):
        part = dot(chosen, grid_ref[half * points : (half + 1) * points]).astype(jnp.bfloat16)
        for number in range(slab_count):
            low = (2 * number + half) * slots
            slot_table_ref[low : low + slots] = part[number * slots : (number + 1) * slots]

    coming = {}

    def send_back(number, chunk):
        span = late_spans[number]
        coming[number, chunk] = exchange(
            answer_ref.at[chunk],
            home_ref.at[chunk],
            back_sends.at[number, chunk],
            back_recvs.at[number, chunk],
            span[0] * few,
            (span[1] - span[0]) * few,
        )

    for chunk in range(chunks):
        for made in going:
            for copy in made[chunk]:
                copy.wait_recv()
        bins_chunk(
            place, 1, got_ref.at[chunk], slot_table_ref, slot_table_ref, cosine_ref[...], sine_ref[...], level_at(0, chunk), answer_ref.at[chunk]
        )
        send_back(0, chunk)
    for number in range(1, len(late_spans)):
        for chunk in range(chunks):
            send_back(number, chunk)
    for copy in row_copies:
        copy.wait_send()

    @pl.when(slab > 0)
    def _():
        first_rim.wait_send()

    for made in going:
        for chunk in made:
            for copy in chunk:
                copy.wait_send()

    def halo(number):
        low, high = late_spans[number]
        where = pl.ds(low, high - low)
        onward = pltpu.make_async_remote_copy(
            src_ref=spill_ref.at[where],
            dst_ref=carried_ref.at[where],
            send_sem=rim_sends.at[number, 0],
            recv_sem=rim_recvs.at[number, 0],
            device_id=slab_device(1),
            device_id_type=MESH,
        )
        backward = pltpu.make_async_remote_copy(
            src_ref=head_ref.at[where],
            dst_ref=ahead_ref.at[where],
            send_sem=rim_sends.at[number, 1],
            recv_sem=rim_recvs.at[number, 1],
            device_id=slab_device(-1),
            device_id_type=MESH,
        )
        return onward, backward

    def subtract(number):
        low, high = late_spans[number]
        for chunk in range(chunks):
            for copy in coming[number, chunk]:
                copy.wait_recv()
        together = math.gcd(high - low, 4)
        for first in range(low, high, together):
            lines = range(first, first + together)
            field_ref[first * slots : (first + together) * slots] = sum(
                dot(upright(home_ref, chunk, lines, few, 2 * slots), table_ref[chunk])
                for chunk in range(chunks)
            )

        def one(line, carry):
            blended = blend_line(line, place_ref, field_ref, forward_ref, picks_ref)
            start = pl.multiple_of(line * padded, 8)
            left = blocks_ref[pl.ds(start, blocks)] - blended[:blocks]
            rest_ref[pl.ds(start, blocks)] = left
            rest_ref[pl.ds(start + blocks, padded - blocks)] = jnp.zeros(
                (padded - blocks, width), wide
            )
            head_ref[line] = left[:edge]
            spill_ref[line] = blended[blocks : blocks + edge]
            return carry

        lax.fori_loop(low, high, one, 0, unroll=UNROLL)
        onward, backward = halo(number)

        @pl.when(slab < last_slab)
        def _():
            onward.start()

        @pl.when(slab > 0)
        def _():
            backward.start()

    def correlate_rest(number):
        low, high = late_spans[number]
        onward, backward = halo(number)

        @pl.when(slab > 0)
        def _():
            onward.wait_recv()
            for line in range(low, high):
                here = pl.ds(line * padded, edge)
                rest_ref[here] = rest_ref[here] - carried_ref[line]

        @pl.when(slab < last_slab)
        def _():
            backward.wait_recv()
            for line in range(low, high):
                rest_ref[pl.ds(line * padded + blocks, edge)] = ahead_ref[line] - spill_ref[line]
            onward.wait_send()

        @pl.when(slab > 0)
        def _():
            backward.wait_send()

        return send_span(number, late_spans[number], rest_ref, field_ref)

    again = []
    for number in range(len(late_spans)):
        subtract(number)
        again.append(correlate_rest(number))

    for block in range(blocks):
        left_ref[:, block * width : (block + 1) * width] = rest_ref[
            pl.ds(block, rcv, stride=padded), :
        ]
    for made in coming.values():
        for copy in made:
            copy.wait_send()
    final = []
    for chunk in range(chunks):
        for made in again:
            for copy in made[chunk]:
                copy.wait_recv()
        bins_chunk(
            place, 2, got_ref.at[chunk], slot_table_ref, row_table_ref, cosine_ref[...], sine_ref[...], level_at(1, chunk), reply_ref.at[chunk]
        )
        final.append(
            exchange(
                reply_ref.at[chunk], final_ref.at[chunk], back_sends.at[0, chunk], back_recvs.at[0, chunk], 0, reply_ref.shape[2]
            )
        )
    for made in again:
        for chunk in made:
            for copy in chunk:
                copy.wait_send()
    for made in final:
        for copy in made:
            copy.wait()


def finish_kernel(bins, spectra_ref, left_ref, table_ref, model_ref, out_ref, sem):
    chunks = spectra_ref.shape[0]
    groups, together, count, _ = model_ref.shape
    step = pl.program_id(0)
    copy = pltpu.make_async_copy(left_ref, out_ref, sem)

    @pl.when(step == 0)
    def _():
        copy.start()

    fields = sum(
        dot(upright(spectra_ref, chunk, range(together), bins, 2 * count), table_ref[chunk])
        for chunk in range(chunks)
    )
    for line in range(together):
        for group in range(groups):
            low = (line * groups + group) * count
            model_ref[group, line] = fields[low : low + count]

    @pl.when(step == pl.num_programs(0) - 1)
    def _():
        copy.wait()


def finish(spectra, left, table, groups, rcv):
    chunks, parts, rows, lanes = spectra.shape
    samples = table.shape[2]
    bins = rows // rcv
    count = lanes // 2 // groups
    together = math.gcd(rcv, 4)
    whole = pl.BlockSpec(memory_space=pltpu.VMEM)
    return pl.pallas_call(
        functools.partial(finish_kernel, bins),
        grid=(rcv // together,),
        out_shape=(
            jax.ShapeDtypeStruct((groups, rcv, count, samples), jnp.float32),
            jax.ShapeDtypeStruct(left.shape, jnp.float32),
        ),
        in_specs=[
            pl.BlockSpec((chunks, parts, together * bins, lanes), lambda i: (0, 0, i, 0)),
            whole,
            whole,
        ],
        out_specs=(
            pl.BlockSpec((groups, together, count, samples), lambda i: (0, i, 0, 0)),
            pl.BlockSpec(memory_space=pl.ANY),
        ),
        scratch_shapes=[pltpu.SemaphoreType.DMA],
        compiler_params=pltpu.CompilerParams(vmem_limit_bytes=16 * 2**20),
    )(spectra, left, table)


def body_by_slots(records, offsets, filter_index, signatures, thresholds):
    rows_here, shot_count = offsets.shape
    local_rcv, slab_len = records.shape
    slab_count = lax.axis_size(("shot", "rep"))
    rep_count = lax.axis_size("rep")
    rcv_count = lax.axis_size("rcv")
    sizes = tuple(lax.axis_size(axis) for axis in AXES)
    parts = slab_count * rcv_count
    tap_count = signatures.shape[1]
    slab_blocks = slab_len // tap_count
    steps = NT // tap_count
    capacity = max(2, 2 * shot_count // slab_count)
    row_count = rows_here * slab_count
    slots = row_count * capacity
    bins = NT // 2 // parts
    chunks = CHUNKS
    few = bins // chunks
    place = np.array(
        [
            [((slab // rep_count) * rcv_count + line) * rep_count + slab % rep_count for slab in range(slab_count)]
            for line in range(rcv_count)
        ]
    )

    time_table_fixed = fixed_time_table(NT).reshape(2, parts, chunks, few, NT)
    time_table_fixed = jnp.asarray(
        np.ascontiguousarray(time_table_fixed.transpose(2, 0, 1, 3, 4)).reshape(chunks, NT // chunks, NT)
    )
    table_x, table_y, table_r = (
        fixed_shot_table(count) for count in (row_count, shot_count, local_rcv * rcv_count)
    )
    grid_table = np.einsum("ajby,bkcx->cxyakj", table_y, table_x).astype(jnp.bfloat16)
    row_table = np.ascontiguousarray(grid_table.transpose(1, 0, 2, 3, 4, 5))
    points = 2 * row_count * shot_count
    grid_table = jnp.asarray(grid_table.reshape(points, points))
    row_table = jnp.asarray(row_table.reshape(points, points))
    same = np.eye(few, dtype=np.float32)
    cosine = jnp.asarray(np.kron(table_r[0, :, 0], same).astype(jnp.bfloat16))
    sine = jnp.asarray(np.kron(table_r[0, :, 1], same).astype(jnp.bfloat16))

    edge = 8
    padded = slab_blocks + 2 * edge
    vmem = pl.BlockSpec(memory_space=pltpu.VMEM)
    anywhere = pl.BlockSpec(memory_space=pl.ANY)
    rows = local_rcv * few
    table_width = tap_count * signatures.shape[0]
    low, wide = jnp.bfloat16, jnp.float32
    big = (records, time_table_fixed, grid_table, row_table, cosine, sine)
    spectra, residual = pl.pallas_call(
        functools.partial(whole_kernel, sizes, place),
        out_shape=(
            pltpu.VMEM((chunks, parts, rows // 2, 4 * shot_count), low),
            pltpu.VMEM(records.shape, wide),
        ),
        in_specs=[vmem] * 4 + [anywhere] * len(big),
        out_specs=(vmem, vmem),
        scratch_shapes=[pltpu.VMEM(array.shape, array.dtype) for array in big]
        + [
            pltpu.VMEM((edge, tap_count), jnp.int32),
            pltpu.VMEM((slab_count * edge, tap_count), jnp.int32),
            pltpu.VMEM((local_rcv, (steps - 1) * tap_count), wide),
            pltpu.VMEM((slots, tap_count), wide),
            pltpu.VMEM((slab_count * 2 * slots, points), low),
            pltpu.VMEM((2 * tap_count, table_width), low),
            pltpu.VMEM((2 * tap_count, table_width), low),
            pltpu.VMEM((slots * steps, padded), low),
            pltpu.VMEM((padded, slots * steps), low),
            pltpu.VMEM((local_rcv * slots, NT), low),
            pltpu.VMEM((local_rcv * slots, NT), wide),
            pltpu.VMEM((local_rcv * padded, tap_count), wide),
            pltpu.VMEM((local_rcv * padded, tap_count), wide),
        ]
        + [pltpu.VMEM((local_rcv, edge, tap_count), wide)] * 4
        + [pltpu.VMEM((chunks, parts, rows, 2 * slots), low)] * 4
        + [pltpu.VMEM((chunks, parts, rows // 2, 4 * shot_count), low)]
        + [pltpu.SemaphoreType.DMA((len(big),))]
        + [pltpu.SemaphoreType.DMA((slab_count - 1,))] * 2
        + [pltpu.SemaphoreType.DMA((SPANS, chunks, parts - 1))] * 4
        + [pltpu.SemaphoreType.DMA((SPANS + 1, 2))] * 2,
        compiler_params=pltpu.CompilerParams(
            collective_id=0, has_side_effects=True, vmem_limit_bytes=60 * 2**20
        ),
    )(offsets, filter_index, signatures, thresholds, *big)
    model, residual = finish(spectra, residual, time_table_fixed, 2, local_rcv // 2)
    return (model.reshape(rows_here, local_rcv, shot_count, NT), residual)


def body(records, offsets, filter_index, signatures, thresholds):
    rows_here, shot_count = offsets.shape
    slab_count = lax.axis_size(("shot", "rep"))
    parts = slab_count * lax.axis_size("rcv")
    slots = rows_here * slab_count * max(2, 2 * shot_count // slab_count)
    table_rows = 2 * rows_here * slab_count * shot_count
    fits = table_rows <= 1024 and rows_here == 1 and slots == 64 and 4 * shot_count == 128
    fits = fits and records.shape[0] == 16 and NT // 2 // parts == 16
    slab_len, tap_count = records.shape[1], signatures.shape[1]
    fits = fits and tap_count == 128 and slab_len & (slab_len - 1) == 0
    run = body_by_slots if fits else body_by_rows
    return run(records, offsets, filter_index, signatures, thresholds)


def solution(mesh):
    in_specs = (
        P(("groups", "rcv"), ("shot", "rep")),
        P(("groups", "shot", "rep"), None),
        P(("groups", "shot", "rep"), None),
        P(),
        P(),
    )
    out_specs = (
        P(("groups", "shot", "rep"), "rcv", None, None),
        P(("groups", "rcv"), ("shot", "rep")),
    )
    return jax.shard_map(body, mesh=mesh, in_specs=in_specs, out_specs=out_specs, check_vma=False)
```

```python
import functools
import math

import jax
import jax.numpy as jnp
import numpy as np
from jax import lax
from jax.experimental import pallas as pl
from jax.experimental.pallas import tpu as pltpu
from jax.sharding import PartitionSpec as P

NT = 512


def from_behind(value, axis, steps):
    count = lax.axis_size(axis)
    first, last = (max(0, -steps), min(count, count - steps))
    return lax.ppermute(value, axis, [(source, source + steps) for source in range(first, last)])


def time_table(count):
    samples = jnp.arange(count)
    bin_index = jnp.arange(count // 2)[:, None]
    angles = 2.0 * math.pi / count * (bin_index * samples[None, :] % count).astype(jnp.float32)
    parity = jnp.where(samples % 2 == 0, 1.0, -1.0).astype(jnp.float32)
    cosine = jnp.where(bin_index == 0, math.sqrt(1.0 / count), math.sqrt(2.0 / count)) * jnp.cos(
        angles
    )
    sine_part = jnp.where(
        bin_index == 0,
        math.sqrt(1.0 / count) * parity[None, :],
        -math.sqrt(2.0 / count) * jnp.sin(angles),
    )
    return jnp.stack([cosine, sine_part]).astype(jnp.bfloat16)


def shot_table(count):
    positions = jnp.arange(count)
    angles = (
        2.0
        * math.pi
        / count
        * (positions[:, None] * positions[None, :] % count).astype(jnp.float32)
    )
    scaling = 1.0 / math.sqrt(count)
    cosine = scaling * jnp.cos(angles)
    sine_part = scaling * jnp.sin(angles)
    upper_half = jnp.stack([cosine, sine_part], axis=1)
    lower_half = jnp.stack([-sine_part, cosine], axis=1)
    return jnp.stack([upper_half, lower_half]).astype(jnp.bfloat16)


def toeplitz_kernel(adjoint, taps_ref, out_ref):
    tap_count = taps_ref.shape[1]
    row_index = lax.broadcasted_iota(jnp.int32, (tap_count, tap_count), 0)
    col_index = lax.broadcasted_iota(jnp.int32, (tap_count, tap_count), 1)
    taps = taps_ref[...].astype(jnp.float32)
    for index in range(taps_ref.shape[0]):
        row = jnp.broadcast_to(taps[index : index + 1, :], (tap_count, tap_count))
        turned = pltpu.roll(row, 0, 1, stride=1, stride_axis=0)
        zeros = jnp.zeros_like(turned)
        near = jnp.where(col_index >= row_index, turned, zeros)
        far = jnp.where(col_index < row_index, turned, zeros)
        near, far = (near.T, far.T) if adjoint else (near, far)
        out_ref[index, :tap_count, :] = near.astype(jnp.bfloat16)
        out_ref[index, tap_count:, :] = far.astype(jnp.bfloat16)


def toeplitz_table(signatures, adjoint):
    count, tap_count = signatures.shape
    return pl.pallas_call(
        functools.partial(toeplitz_kernel, adjoint),
        out_shape=jax.ShapeDtypeStruct((count, 2 * tap_count, tap_count), jnp.bfloat16),
        in_specs=[pl.BlockSpec(memory_space=pltpu.VMEM)],
        out_specs=pl.BlockSpec(memory_space=pltpu.VMEM),
    )(signatures)


def apply_filter(traces, table, adjoint):
    empty = jnp.zeros_like(traces[:, :1])
    if adjoint:
        other = jnp.concatenate([traces[:, 1:], empty], axis=1)
    else:
        other = jnp.concatenate([empty, traces[:, :-1]], axis=1)
    return jnp.einsum(
        "sbrp,spq->sbrq",
        jnp.concatenate([traces, other], axis=3),
        table,
        preferred_element_type=jnp.float32,
    )


def rank_in_row(owners):
    shot_count = owners.shape[1]
    same_owner = owners[:, :, None] == owners[:, None, :]
    earlier = jnp.arange(shot_count)[None, :] < jnp.arange(shot_count)[:, None]
    return jnp.sum(same_owner & earlier[None], axis=2)


def to_slabs(payload):
    return lax.all_to_all(payload, ("shot", "rep"), split_axis=0, concat_axis=0, tiled=True)


def to_shots(payload):
    return lax.all_to_all(payload, ("shot", "rep"), split_axis=0, concat_axis=0, tiled=True)


def soft_limit(coefficients, threshold_row):
    magnitude = jnp.sqrt(coefficients[0] * coefficients[0] + coefficients[1] * coefficients[1])
    threshold_view = threshold_row[None, :, None, None]
    factor = 1.0 - threshold_view / jnp.maximum(magnitude, threshold_view)
    return (coefficients * factor[None]).astype(jnp.bfloat16)


def shrink(field_data, threshold_row, tables):
    table_time, table_x, table_y, table_r = tables
    rows_here, local_rcv, shot_count, sample_count = field_data.shape
    spectrum = jnp.einsum(
        "ckt,xryt->xckry",
        table_time,
        field_data.astype(jnp.bfloat16),
        preferred_element_type=jnp.float32,
    ).astype(jnp.bfloat16)
    bin_count = spectrum.shape[2]
    spectrum = spectrum.reshape(rows_here, 2, bin_count, local_rcv * shot_count)
    section_data = jnp.einsum(
        "akbx,xbfz->akfz",
        table_x,
        lax.all_to_all(spectrum, ("shot", "rep"), split_axis=2, concat_axis=0, tiled=True),
        preferred_element_type=jnp.float32,
    ).astype(jnp.bfloat16)
    all_rows, row_bins = (section_data.shape[1], section_data.shape[2])
    section_data = section_data.reshape(2, all_rows, row_bins, local_rcv, shot_count)
    section_data = lax.all_to_all(section_data, "rcv", split_axis=2, concat_axis=3, tiled=True)
    section_data = jnp.einsum(
        "ajby,bkfry->akfrj", table_y, section_data, preferred_element_type=jnp.float32
    ).astype(jnp.bfloat16)
    coefficients = jnp.einsum(
        "aqbr,bkfrj->akfqj", table_r, section_data, preferred_element_type=jnp.float32
    )
    shrunk = soft_limit(coefficients, threshold_row)
    section_data = jnp.einsum(
        "aqbr,akfqj->bkfrj", table_r, shrunk, preferred_element_type=jnp.float32
    ).astype(jnp.bfloat16)
    section_data = jnp.einsum(
        "ajby,akfrj->bkfry", table_y, section_data, preferred_element_type=jnp.float32
    ).astype(jnp.bfloat16)
    section_data = lax.all_to_all(section_data, "rcv", split_axis=3, concat_axis=2, tiled=True)
    section_data = section_data.reshape(2, all_rows, row_bins, local_rcv * shot_count)
    section_data = jnp.einsum(
        "akbx,akfz->bxfz", table_x, section_data, preferred_element_type=jnp.float32
    ).astype(jnp.bfloat16)
    result = jnp.einsum(
        "ckt,cxkz->xzt",
        table_time,
        lax.all_to_all(section_data, ("shot", "rep"), split_axis=1, concat_axis=2, tiled=True),
        preferred_element_type=jnp.float32,
    )
    return result.reshape(rows_here, local_rcv, shot_count, sample_count)


def body_by_rows(records, offsets, filter_index, signatures, thresholds):
    rows_here, shot_count = offsets.shape
    local_rcv, slab_len = records.shape
    slab_count = lax.axis_size(("shot", "rep"))
    rcv_count = lax.axis_size("rcv")
    tap_count = signatures.shape[1]
    sample_count = NT
    slab_blocks = slab_len // tap_count
    trace_blocks = sample_count // tap_count
    capacity = max(2, 2 * shot_count // slab_count)
    slot_count = slab_count * rows_here * capacity
    forward_tables = toeplitz_table(signatures, False)
    adjoint_tables = toeplitz_table(signatures, True)
    flat_index = filter_index.reshape(-1)
    forward_table = forward_tables[flat_index]
    adjoint_table = adjoint_tables[flat_index]
    owners = offsets // slab_len
    row_ids = jnp.arange(rows_here, dtype=jnp.int32)[:, None]
    slot_index = (
        owners * (rows_here * capacity) + row_ids * capacity + rank_in_row(owners)
    ).reshape(-1)
    every_offset = lax.all_gather(offsets, ("shot", "rep"), axis=0, tiled=True)
    every_owner = every_offset // slab_len
    every_start = every_offset // tap_count % slab_blocks
    every_rank = rank_in_row(every_owner)
    mine_mask = every_owner == lax.axis_index(("shot", "rep"))
    levels = jnp.arange(capacity, dtype=jnp.int32)
    picked = mine_mask[:, :, None] & (every_rank[:, :, None] == levels[None, None, :])
    table_in = jnp.sum(jnp.where(picked, every_start[:, :, None] + 1, 0), axis=1).reshape(-1)
    filled = table_in > 0
    block_steps = jnp.arange(trace_blocks, dtype=jnp.int32)
    target = jnp.where(
        filled[:, None],
        table_in[:, None] - 1 + block_steps[None, :],
        slab_blocks + trace_blocks - 1,
    )

    def correlate(record_field):
        record_low = (
            record_field.astype(jnp.bfloat16)
            .reshape(local_rcv, slab_blocks, tap_count)
            .transpose(1, 0, 2)
        )
        rim_blocks = from_behind(record_low[: trace_blocks - 1], ("shot", "rep"), -1)
        extended = jnp.concatenate(
            [record_low, rim_blocks, jnp.zeros((1, local_rcv, tap_count), jnp.bfloat16)], axis=0
        )
        windows = extended[target.reshape(-1)].reshape(
            slot_count, trace_blocks, local_rcv, tap_count
        )
        returned = to_shots(windows)
        traces = returned[slot_index]
        terms = apply_filter(traces, adjoint_table, True)
        terms = terms.reshape(rows_here, shot_count, trace_blocks, local_rcv, tap_count).transpose(
            0, 3, 1, 2, 4
        )
        return terms.reshape(rows_here, local_rcv, shot_count, sample_count)

    tables = (
        time_table(sample_count),
        shot_table(slab_count * rows_here),
        shot_table(shot_count),
        shot_table(local_rcv * rcv_count),
    )
    row_bins = sample_count // 2 // slab_count
    rcv_bins = row_bins // rcv_count
    bin_start = lax.axis_index(("shot", "rep")) * row_bins + lax.axis_index("rcv") * rcv_bins

    def threshold_for(level_index):
        return lax.dynamic_slice_in_dim(thresholds[level_index], bin_start, rcv_bins)

    model_field = shrink(correlate(records), threshold_for(0), tables)
    level_index = 1
    traces = model_field.astype(jnp.bfloat16).reshape(
        rows_here, local_rcv, shot_count, trace_blocks, tap_count
    )
    traces = traces.transpose(0, 2, 3, 1, 4).reshape(
        rows_here * shot_count, trace_blocks, local_rcv, tap_count
    )
    shots = apply_filter(traces, forward_table, False).astype(jnp.bfloat16)
    outgoing = (
        jnp.zeros((slot_count, trace_blocks, local_rcv, tap_count), jnp.bfloat16)
        .at[slot_index]
        .set(shots)
    )
    arrived = to_slabs(outgoing)
    slab_total = jnp.zeros((slab_blocks + trace_blocks, local_rcv, tap_count), jnp.float32)
    for block_step in range(trace_blocks):
        slab_total = slab_total.at[target[:, block_step]].add(
            arrived[:, block_step].astype(jnp.float32)
        )
    spill_over = slab_total[slab_blocks : slab_blocks + trace_blocks - 1]
    carried = from_behind(spill_over, ("shot", "rep"), 1)
    blended = slab_total[:slab_blocks].at[: trace_blocks - 1].add(carried)
    residual = records - blended.transpose(1, 0, 2).reshape(local_rcv, slab_len)
    model_field = shrink(model_field + correlate(residual), threshold_for(level_index), tables)
    return (model_field, residual)


def dot(left, right, left_dim=1, right_dim=0):
    return lax.dot_general(
        left, right, (((left_dim,), (right_dim,)), ((), ())), preferred_element_type=jnp.float32
    )


def fixed_time_table(count):
    samples = np.arange(count)
    bins = np.arange(count // 2)[:, None]
    angles = 2.0 * np.pi / count * (bins * samples[None, :] % count)
    scale = math.sqrt(2.0 / count)
    cosine = scale * np.cos(angles)
    sine = -scale * np.sin(angles)
    cosine[0] = math.sqrt(1.0 / count)
    sine[0] = math.sqrt(1.0 / count) * np.where(samples % 2 == 0, 1.0, -1.0)
    return np.stack([cosine, sine]).astype(jnp.bfloat16)


def fixed_shot_table(count):
    positions = np.arange(count)
    angles = 2.0 * np.pi / count * (positions[:, None] * positions[None, :] % count)
    cosine = np.cos(angles) / math.sqrt(count)
    sine = np.sin(angles) / math.sqrt(count)
    table = np.stack([np.stack([cosine, sine], 1), np.stack([-sine, cosine], 1)])
    return table.astype(jnp.bfloat16).astype(np.float32)


MESH = pl.DeviceIdType.MESH
AXES = ("shot", "rcv", "rep")


def neighbours(sizes):
    every = [(a, b, c) for a in range(sizes[0]) for b in range(sizes[1]) for c in range(sizes[2])]
    far = sizes[0] // 2
    return sorted(every[1:], key=lambda step: (abs(step[0] - far), -step[1], -step[2]))


def device_at(sizes, step):
    spot = [lax.rem(lax.axis_index(axis) + hop, size) for axis, hop, size in zip(AXES, step, sizes)]
    index = (spot[0] * sizes[1] + spot[1]) * sizes[2] + spot[2]
    return dict(zip(AXES, spot)), index


def build_taps(signature_ref, adjoint, out_ref):
    count, taps = signature_ref.shape
    row_index = lax.broadcasted_iota(jnp.int32, (taps, taps), 0)
    col_index = lax.broadcasted_iota(jnp.int32, (taps, taps), 1)
    values = signature_ref[...].astype(jnp.float32)
    for index in range(count):
        row = jnp.broadcast_to(values[index : index + 1, :], (taps, taps))
        turned = pltpu.roll(row, 0, 1, stride=1, stride_axis=0)
        zeros = jnp.zeros_like(turned)
        near = jnp.where(col_index >= row_index, turned, zeros)
        far = jnp.where(col_index < row_index, turned, zeros)
        near, far = (near.T, far.T) if adjoint else (near, far)
        where = slice(index * taps, (index + 1) * taps)
        out_ref[:taps, where] = near.astype(jnp.bfloat16)
        out_ref[taps:, where] = far.astype(jnp.bfloat16)


def pick_signature(every, picks_ref):
    slots, width = picks_ref.shape
    picks = jnp.concatenate([picks_ref[...]] * (every.shape[0] // slots), axis=0)
    chosen = every[:, :width]
    for index in range(1, every.shape[1] // width):
        chosen = jnp.where(picks == index, every[:, index * width : (index + 1) * width], chosen)
    return chosen


def correlate_line(line, padded, select_ref, blocks_ref, taps_ref, picks_ref, field_ref, traces_ref):
    slots, width = picks_ref.shape
    blocks = blocks_ref[pl.ds(pl.multiple_of(line * padded, 8), padded)].astype(jnp.bfloat16)
    window = dot(select_ref[...], blocks).astype(jnp.bfloat16)
    later = jnp.concatenate([window[slots:], jnp.zeros((slots, width), window.dtype)], axis=0)
    terms = pick_signature(dot(jnp.concatenate([window, later], axis=1), taps_ref[...]), picks_ref)
    steps = terms.shape[0] // slots
    terms = jnp.concatenate(
        [terms[step * slots : (step + 1) * slots] for step in range(steps)], axis=1
    )
    where = pl.ds(pl.multiple_of(line * slots, slots), slots)
    if field_ref is not None:
        terms = terms + field_ref[where]
    traces_ref[where] = terms.astype(jnp.bfloat16)


def blend_line(line, place_ref, field_ref, taps_ref, picks_ref):
    slots, width = picks_ref.shape
    trace = field_ref[pl.ds(pl.multiple_of(line * slots, slots), slots)].astype(jnp.bfloat16)
    steps = trace.shape[1] // width
    stacked = jnp.concatenate(
        [trace[:, step * width : (step + 1) * width] for step in range(steps)], axis=0
    )
    earlier = jnp.concatenate([jnp.zeros((slots, width), trace.dtype), stacked[:-slots]], axis=0)
    shots = pick_signature(dot(jnp.concatenate([stacked, earlier], axis=1), taps_ref[...]), picks_ref)
    return dot(place_ref[...], shots.astype(jnp.bfloat16))


def spectra_chunk(table, traces_ref, out_ref, lines, rcv, slots):
    parts, rows, lanes = out_ref.shape
    bins = rows // rcv
    half = parts * bins
    pack = max(1, 16 // bins)
    together = math.gcd(len(lines), 4)
    for first in range(lines[0], lines[-1] + 1, together):
        both = dot(table, traces_ref[first * slots : (first + together) * slots], 1, 1)
        for low in range(0, together, pack):
            pieces = []
            for line in range(low, low + pack):
                piece = both[:, line * slots : (line + 1) * slots]
                joined = jnp.concatenate([piece[:half], piece[half:]], axis=1)
                pieces.append(joined.reshape(parts, bins, lanes))
            out_ref[:, (first + low) * bins : (first + low + pack) * bins] = jnp.concatenate(
                pieces, axis=1
            ).astype(jnp.bfloat16)


def bins_chunk(place, halves, spectra_ref, go_ref, back_ref, cosine, sine, level, out_ref):
    _, rows, _ = spectra_ref.shape
    rcv_count, slab_count = place.shape
    joined = jnp.concatenate(
        [
            jnp.concatenate([spectra_ref[int(index)] for index in line], axis=1)
            for line in place
        ],
        axis=0,
    )
    section = dot(joined, go_ref[...]).astype(jnp.bfloat16)
    half = section.shape[1] // 2
    near = dot(cosine, section)
    far = dot(sine, section)
    real = near[:, :half] + far[:, half:]
    imag = near[:, half:] - far[:, :half]
    factor = 1.0 - level / jnp.maximum(jnp.sqrt(real * real + imag * imag), level)
    shrunk = jnp.concatenate([real * factor, imag * factor], axis=1).astype(jnp.bfloat16)
    near = dot(cosine, shrunk)
    far = dot(sine, shrunk)
    section = jnp.concatenate(
        [near[:, :half] - far[:, half:], far[:, :half] + near[:, half:]], axis=1
    ).astype(jnp.bfloat16)
    result = dot(section, back_ref[...], 1, 1).astype(jnp.bfloat16)
    width = result.shape[1] // slab_count
    for line in range(rcv_count):
        for slab in range(slab_count):
            piece = result[line * rows : (line + 1) * rows, slab * width : (slab + 1) * width]
            if halves == 2:
                piece = jnp.concatenate([piece[: rows // 2], piece[rows // 2 :]], axis=1)
            out_ref[int(place[line, slab])] = piece


def level_of(levels_ref, index, first, bins, copies_of):
    width = levels_ref.shape[1]
    lane = lax.broadcasted_iota(jnp.int32, (bins, width), 1)
    row = lax.broadcasted_iota(jnp.int32, (bins, width), 0)
    values = jnp.broadcast_to(levels_ref[index : index + 1, :], (bins, width))
    column = jnp.sum(jnp.where(lane == row + first, values, 0.0), axis=1, keepdims=True)
    return jnp.concatenate([column] * copies_of, axis=0)


def upright(spectra_ref, chunk, lines, bins, group_lanes):
    parts = spectra_ref.shape[1]
    pack = max(1, 16 // bins)
    count = group_lanes // 2
    pieces = []
    for low_line in range(lines[0], lines[-1] + 1, pack):
        block = spectra_ref[chunk, :, low_line * bins : (low_line + pack) * bins].astype(jnp.float32)
        for line in range(pack):
            turned = block[:, line * bins : (line + 1) * bins].reshape(parts * bins, -1).T
            turned = turned.astype(jnp.bfloat16)
            for low in range(0, turned.shape[0], group_lanes):
                pieces.append(
                    jnp.concatenate(
                        [turned[low : low + count], turned[low + count : low + 2 * count]], axis=1
                    )
                )
    return jnp.concatenate(pieces, axis=0)


CHUNKS = 2
SPANS = 2
UNROLL = 4


def whole_kernel(
    sizes,
    place,
    offsets_ref,
    filters_ref,
    signatures_ref,
    levels_ref,
    records_hbm,
    table_hbm,
    grid_hbm,
    row_table_hbm,
    cosine_hbm,
    sine_hbm,
    final_ref,
    left_ref,
    records_ref,
    table_ref,
    grid_ref,
    row_table_ref,
    cosine_ref,
    sine_ref,
    row_ref,
    rows_ref,
    rim_ref,
    picks_ref,
    slot_table_ref,
    adjoint_ref,
    forward_ref,
    select_ref,
    place_ref,
    traces_ref,
    field_ref,
    blocks_ref,
    rest_ref,
    head_ref,
    spill_ref,
    carried_ref,
    ahead_ref,
    sent_ref,
    got_ref,
    answer_ref,
    home_ref,
    reply_ref,
    raw_ref,
    other_raw_ref,
    other_rim_ref,
    other_blocks_ref,
    other_picks_ref,
    other_select_ref,
    other_traces_ref,
    other_sent_ref,
    load_sems,
    row_sends,
    row_recvs,
    go_sends,
    go_recvs,
    back_sends,
    back_recvs,
    rim_sends,
    rim_recvs,
    near_sends,
    near_recvs,
    raw_sems,
):
    slots, width = picks_ref.shape
    rcv, slab_len = records_ref.shape
    blocks = slab_len // width
    padded = blocks_ref.shape[0] // rcv
    chunks, _, samples = table_ref.shape
    steps = samples // width
    parts = place.size
    slab_count = place.shape[1]
    few = samples // 2 // parts // chunks
    quarter = rcv // 4
    early_spans = ((quarter, 2 * quarter), (2 * quarter, rcv))
    late_spans = ((0, 2 * quarter), (2 * quarter, rcv))
    edge = head_ref.shape[1]
    all_rcv = rcv * place.shape[0]
    shot_count = offsets_ref.shape[1]
    row_count = slab_count
    capacity = slots // row_count
    wide = jnp.float32

    loads = [
        pltpu.make_async_copy(source, target, load_sems.at[number])
        for number, (source, target) in enumerate(
            (
                (records_hbm, records_ref),
                (table_hbm, table_ref),
                (grid_hbm, grid_ref),
                (cosine_hbm, cosine_ref),
                (sine_hbm, sine_ref),
                (row_table_hbm, row_table_ref),
            )
        )
    ]
    for load in loads:
        load.start()
    barrier = pltpu.get_barrier_semaphore()
    hops = neighbours(sizes)
    for hop in hops:
        pl.semaphore_signal(barrier, inc=1, device_id=device_at(sizes, hop)[0], device_id_type=MESH)
    mine = device_at(sizes, (0, 0, 0))[1]
    slab = lax.axis_index("shot") * sizes[2] + lax.axis_index("rep")
    last_slab = slab_count - 1

    def slab_device(shift):
        other = lax.rem(slab + shift + slab_count, slab_count)
        return {
            "shot": other // sizes[2],
            "rcv": lax.axis_index("rcv"),
            "rep": lax.rem(other, sizes[2]),
        }

    row_ref[...] = jnp.zeros_like(row_ref)
    row_ref[0:1, :shot_count] = offsets_ref[...]
    row_ref[1:2, :shot_count] = filters_ref[...]
    pl.semaphore_wait(barrier, len(hops))

    tile = row_ref.shape[0]
    here = pl.ds(pl.multiple_of(slab * tile, tile), tile)
    row_copies = []
    for hop in hops:
        if hop[1] == 0:
            number = len(row_copies)
            copy = pltpu.make_async_remote_copy(
                src_ref=row_ref,
                dst_ref=rows_ref.at[here],
                send_sem=row_sends.at[number],
                recv_sem=row_recvs.at[number],
                device_id=device_at(sizes, hop)[0],
                device_id_type=MESH,
            )
            copy.start()
            row_copies.append(copy)
    rows_ref[here] = row_ref[...]
    loads[0].wait()
    apart = slab_count // 2
    partner_slab = lax.rem(slab + apart, slab_count)
    partner = device_at(sizes, (sizes[0] // 2, 0, 0))[1]
    first_rim = pltpu.make_async_remote_copy(
        src_ref=records_ref.at[:, pl.ds(0, rim_ref.shape[1])],
        dst_ref=rim_ref,
        send_sem=rim_sends.at[SPANS, 0],
        recv_sem=rim_recvs.at[SPANS, 0],
        device_id=slab_device(-1),
        device_id_type=MESH,
    )
    partner_rim = pltpu.make_async_remote_copy(
        src_ref=records_ref.at[pl.ds(0, tile), pl.ds(0, rim_ref.shape[1])],
        dst_ref=other_rim_ref,
        send_sem=rim_sends.at[SPANS, 1],
        recv_sem=rim_recvs.at[SPANS, 1],
        device_id=slab_device(apart - 1),
        device_id_type=MESH,
    )

    @pl.when(slab > 0)
    def _():
        first_rim.start()
        partner_rim.start()

    for line in range(rcv):
        blocks_ref[line * padded + blocks : (line + 1) * padded] = jnp.zeros(
            (padded - blocks, width), wide
        )
    for block in range(blocks):
        blocks_ref[pl.ds(block, rcv, stride=padded), :] = records_ref[
            :, block * width : (block + 1) * width
        ]
    for line in range(quarter):
        raw_ref[line] = blocks_ref[line * padded : line * padded + blocks].astype(jnp.bfloat16)
    raw = pltpu.make_async_remote_copy(
        src_ref=raw_ref,
        dst_ref=other_raw_ref,
        send_sem=raw_sems.at[0],
        recv_sem=raw_sems.at[1],
        device_id=slab_device(apart),
        device_id_type=MESH,
    )
    raw.start()
    build_taps(signatures_ref, True, adjoint_ref)
    for copy in row_copies:
        copy.wait_recv()

    lane = lax.broadcasted_iota(jnp.int32, (row_count, width), 1)
    valid = lane < shot_count
    zero = jnp.zeros((row_count, width), jnp.int32)
    start_sample = jnp.where(valid, rows_ref[pl.ds(0, row_count, stride=tile), :], zero)
    signature = jnp.where(valid, rows_ref[pl.ds(1, row_count, stride=tile), :], zero)
    block_bits = width.bit_length() - 1
    slab_bits = slab_len.bit_length() - 1
    owner = lax.shift_right_logical(start_sample, slab_bits)
    rank = zero
    for step in range(1, shot_count):
        same = (pltpu.roll(owner, step, 1) == owner) & (lane >= step)
        rank = rank + same.astype(jnp.int32)
    key = jnp.where(valid, owner * capacity + rank + 1, zero)
    first_block = (lax.shift_right_logical(start_sample, block_bits) & (blocks - 1)).astype(wide)
    signature = signature.astype(wide)
    block_index = lax.broadcasted_iota(jnp.int32, (slots, padded), 1).astype(wide)

    def choose(owner_slab, into_picks_ref, into_select_ref):
        firsts, picks = [], []
        for level in range(capacity):
            taken = key == owner_slab * capacity + level + 1
            empty = jnp.zeros_like(first_block)
            firsts.append(
                jnp.sum(jnp.where(taken, first_block + 1.0, empty), axis=1, keepdims=True)
            )
            picks.append(jnp.sum(jnp.where(taken, signature, empty), axis=1, keepdims=True))
        firsts = jnp.broadcast_to(jnp.concatenate(firsts, axis=0), (slots, padded))
        firsts = jnp.where(firsts > 0.5, firsts - 1.0, -float(samples))
        into_picks_ref[...] = jnp.broadcast_to(jnp.concatenate(picks, axis=0), (slots, width))
        select = jnp.concatenate(
            [(block_index == firsts + float(step)).astype(wide) for step in range(steps)], axis=0
        )
        into_select_ref[...] = select.astype(jnp.bfloat16)
        return select

    select = choose(slab, picks_ref, select_ref)

    @pl.when(slab < last_slab)
    def _():
        first_rim.wait_recv()
        for step in range(rim_ref.shape[1] // width):
            blocks_ref[pl.ds(blocks + step, rcv, stride=padded), :] = rim_ref[
                :, step * width : (step + 1) * width
            ]

    loads[1].wait()

    def exchange(source, target, send_sems, recv_sems, low, rows):
        made = []
        where = pl.ds(low, rows)
        for number, hop in enumerate(hops):
            device, index = device_at(sizes, hop)
            copy = pltpu.make_async_remote_copy(
                src_ref=source.at[index, where],
                dst_ref=target.at[mine, where],
                send_sem=send_sems.at[number],
                recv_sem=recv_sems.at[number],
                device_id=device,
                device_id_type=MESH,
            )
            copy.start()
            made.append(copy)
        target[mine, where] = source[mine, where]
        return made

    def correlate_span(span, from_ref, model, one_select_ref, one_picks_ref, into_ref):
        def one(line, carry):
            correlate_line(
                line, padded, one_select_ref, from_ref, adjoint_ref, one_picks_ref, model, into_ref
            )
            return carry

        lax.fori_loop(span[0], span[1], one, 0, unroll=UNROLL)

    def send_span(number, span, from_ref, model):
        correlate_span(span, from_ref, model, select_ref, picks_ref, traces_ref)
        made = []
        for chunk in range(chunks):
            spectra_chunk(
                table_ref[chunk], traces_ref, sent_ref.at[chunk], range(*span), rcv, slots
            )
            made.append(
                exchange(
                    sent_ref.at[chunk],
                    got_ref.at[chunk],
                    go_sends.at[number, chunk],
                    go_recvs.at[number, chunk],
                    span[0] * few,
                    (span[1] - span[0]) * few,
                )
            )
        return made

    def send_near(number, from_ref, one_select_ref, one_picks_ref, into_ref, out_ref, owner):
        span = (0, quarter)
        correlate_span(span, from_ref, None, one_select_ref, one_picks_ref, into_ref)
        where = pl.ds(0, quarter * few)
        depth, place_x, core = (lax.axis_index(axis) for axis in AXES)
        made = []
        for chunk in range(chunks):
            spectra_chunk(
                table_ref[chunk], into_ref, out_ref.at[chunk], range(*span), rcv, slots
            )
            copies = []
            for hop in range(1, 8):
                spot = (
                    depth + (hop // 4) * (1 - 2 * lax.rem(depth, 2)),
                    lax.rem(place_x + hop // 2 % 2, sizes[1]),
                    lax.rem(core + hop % 2, sizes[2]),
                )
                index = (spot[0] * sizes[1] + spot[1]) * sizes[2] + spot[2]
                copy = pltpu.make_async_remote_copy(
                    src_ref=out_ref.at[chunk, index, where],
                    dst_ref=got_ref.at[chunk, owner, where],
                    send_sem=near_sends.at[number, chunk, hop - 1],
                    recv_sem=near_recvs.at[number, chunk, hop - 1],
                    device_id=dict(zip(AXES, spot)),
                    device_id_type=MESH,
                )
                copy.start()
                copies.append(copy)
            got_ref[chunk, owner, where] = out_ref[chunk, mine, where]
            made.append(copies)
        return made

    def level_at(index, chunk):
        return level_of(levels_ref, index, (mine * chunks + chunk) * few, few, all_rcv)

    going = [
        send_span(number, span, blocks_ref, None) for number, span in enumerate(early_spans)
    ]

    going.append(send_near(0, blocks_ref, select_ref, picks_ref, traces_ref, sent_ref, mine))
    choose(partner_slab, other_picks_ref, other_select_ref)
    raw.wait_recv()
    for line in range(quarter):
        other_blocks_ref[line * padded : line * padded + blocks] = other_raw_ref[line].astype(wide)
        other_blocks_ref[line * padded + blocks : (line + 1) * padded] = jnp.zeros(
            (padded - blocks, width), wide
        )

    @pl.when(partner_slab < last_slab)
    def _():
        partner_rim.wait_recv()
        for step in range(rim_ref.shape[1] // width):
            other_blocks_ref[pl.ds(blocks + step, quarter, stride=padded), :] = other_rim_ref[
                :quarter, step * width : (step + 1) * width
            ]

    going.append(
        send_near(
            1, other_blocks_ref, other_select_ref, other_picks_ref, other_traces_ref, other_sent_ref, partner
        )
    )
    place_ref[...] = select.T.astype(jnp.bfloat16)
    build_taps(signatures_ref, False, forward_ref)
    repeated = key
    for shift in range(shot_count, width, shot_count):
        repeated = repeated + pltpu.roll(key, shift, 1)
    points = row_count * shot_count
    repeated = jnp.concatenate([repeated] * (points // width), axis=1)
    point = lax.broadcasted_iota(jnp.int32, (row_count, points), 1)
    row = lax.broadcasted_iota(jnp.int32, (row_count, points), 0)
    shot_bits = shot_count.bit_length() - 1
    repeated = jnp.where(lax.shift_right_logical(point, shot_bits) == row, repeated, 0)
    chosen = jnp.concatenate(
        [(repeated == number + 1).astype(wide) for number in range(slab_count * capacity)], axis=0
    ).astype(jnp.bfloat16)
    for load in loads[2:]:
        load.wait()
    for half in range(2):
        part = dot(chosen, grid_ref[half * points : (half + 1) * points]).astype(jnp.bfloat16)
        for number in range(slab_count):
            low = (2 * number + half) * slots
            slot_table_ref[low : low + slots] = part[number * slots : (number + 1) * slots]

    coming = {}

    def send_back(number, chunk):
        span = late_spans[number]
        coming[number, chunk] = exchange(
            answer_ref.at[chunk],
            home_ref.at[chunk],
            back_sends.at[number, chunk],
            back_recvs.at[number, chunk],
            span[0] * few,
            (span[1] - span[0]) * few,
        )

    for chunk in range(chunks):
        for made in going:
            for copy in made[chunk]:
                copy.wait_recv()
        bins_chunk(
            place, 1, got_ref.at[chunk], slot_table_ref, slot_table_ref, cosine_ref[...], sine_ref[...], level_at(0, chunk), answer_ref.at[chunk]
        )
        send_back(0, chunk)
    for number in range(1, len(late_spans)):
        for chunk in range(chunks):
            send_back(number, chunk)
    for copy in row_copies:
        copy.wait_send()

    raw.wait_send()

    @pl.when(slab > 0)
    def _():
        first_rim.wait_send()
        partner_rim.wait_send()

    for made in going:
        for chunk in made:
            for copy in chunk:
                copy.wait_send()

    def halo(number):
        low, high = late_spans[number]
        where = pl.ds(low, high - low)
        onward = pltpu.make_async_remote_copy(
            src_ref=spill_ref.at[where],
            dst_ref=carried_ref.at[where],
            send_sem=rim_sends.at[number, 0],
            recv_sem=rim_recvs.at[number, 0],
            device_id=slab_device(1),
            device_id_type=MESH,
        )
        backward = pltpu.make_async_remote_copy(
            src_ref=head_ref.at[where],
            dst_ref=ahead_ref.at[where],
            send_sem=rim_sends.at[number, 1],
            recv_sem=rim_recvs.at[number, 1],
            device_id=slab_device(-1),
            device_id_type=MESH,
        )
        return onward, backward

    def subtract(number):
        low, high = late_spans[number]
        for chunk in range(chunks):
            for copy in coming[number, chunk]:
                copy.wait_recv()
        together = math.gcd(high - low, 4)
        for first in range(low, high, together):
            lines = range(first, first + together)
            field_ref[first * slots : (first + together) * slots] = sum(
                dot(upright(home_ref, chunk, lines, few, 2 * slots), table_ref[chunk])
                for chunk in range(chunks)
            )

        def one(line, carry):
            blended = blend_line(line, place_ref, field_ref, forward_ref, picks_ref)
            start = pl.multiple_of(line * padded, 8)
            left = blocks_ref[pl.ds(start, blocks)] - blended[:blocks]
            rest_ref[pl.ds(start, blocks)] = left
            rest_ref[pl.ds(start + blocks, padded - blocks)] = jnp.zeros(
                (padded - blocks, width), wide
            )
            head_ref[line] = left[:edge]
            spill_ref[line] = blended[blocks : blocks + edge]
            return carry

        lax.fori_loop(low, high, one, 0, unroll=UNROLL)
        onward, backward = halo(number)

        @pl.when(slab < last_slab)
        def _():
            onward.start()

        @pl.when(slab > 0)
        def _():
            backward.start()

    def correlate_rest(number):
        low, high = late_spans[number]
        onward, backward = halo(number)

        @pl.when(slab > 0)
        def _():
            onward.wait_recv()
            for line in range(low, high):
                here = pl.ds(line * padded, edge)
                rest_ref[here] = rest_ref[here] - carried_ref[line]

        @pl.when(slab < last_slab)
        def _():
            backward.wait_recv()
            for line in range(low, high):
                rest_ref[pl.ds(line * padded + blocks, edge)] = ahead_ref[line] - spill_ref[line]
            onward.wait_send()

        @pl.when(slab > 0)
        def _():
            backward.wait_send()

        return send_span(number, late_spans[number], rest_ref, field_ref)

    again = []
    for number in range(len(late_spans)):
        subtract(number)
        again.append(correlate_rest(number))

    for block in range(blocks):
        left_ref[:, block * width : (block + 1) * width] = rest_ref[
            pl.ds(block, rcv, stride=padded), :
        ]
    for made in coming.values():
        for copy in made:
            copy.wait_send()
    final = []
    for chunk in range(chunks):
        for made in again:
            for copy in made[chunk]:
                copy.wait_recv()
        bins_chunk(
            place, 2, got_ref.at[chunk], slot_table_ref, row_table_ref, cosine_ref[...], sine_ref[...], level_at(1, chunk), reply_ref.at[chunk]
        )
        final.append(
            exchange(
                reply_ref.at[chunk], final_ref.at[chunk], back_sends.at[0, chunk], back_recvs.at[0, chunk], 0, reply_ref.shape[2]
            )
        )
    for made in again:
        for chunk in made:
            for copy in chunk:
                copy.wait_send()
    for made in final:
        for copy in made:
            copy.wait()


def finish_kernel(bins, spectra_ref, left_ref, table_ref, model_ref, out_ref, sem):
    chunks = spectra_ref.shape[0]
    groups, together, count, _ = model_ref.shape
    step = pl.program_id(0)
    copy = pltpu.make_async_copy(left_ref, out_ref, sem)

    @pl.when(step == 0)
    def _():
        copy.start()

    fields = sum(
        dot(upright(spectra_ref, chunk, range(together), bins, 2 * count), table_ref[chunk])
        for chunk in range(chunks)
    )
    for line in range(together):
        for group in range(groups):
            low = (line * groups + group) * count
            model_ref[group, line] = fields[low : low + count]

    @pl.when(step == pl.num_programs(0) - 1)
    def _():
        copy.wait()


def finish(spectra, left, table, groups, rcv):
    chunks, parts, rows, lanes = spectra.shape
    samples = table.shape[2]
    bins = rows // rcv
    count = lanes // 2 // groups
    together = math.gcd(rcv, 4)
    whole = pl.BlockSpec(memory_space=pltpu.VMEM)
    return pl.pallas_call(
        functools.partial(finish_kernel, bins),
        grid=(rcv // together,),
        out_shape=(
            jax.ShapeDtypeStruct((groups, rcv, count, samples), jnp.float32),
            jax.ShapeDtypeStruct(left.shape, jnp.float32),
        ),
        in_specs=[
            pl.BlockSpec((chunks, parts, together * bins, lanes), lambda i: (0, 0, i, 0)),
            whole,
            whole,
        ],
        out_specs=(
            pl.BlockSpec((groups, together, count, samples), lambda i: (0, i, 0, 0)),
            pl.BlockSpec(memory_space=pl.ANY),
        ),
        scratch_shapes=[pltpu.SemaphoreType.DMA],
        compiler_params=pltpu.CompilerParams(vmem_limit_bytes=16 * 2**20),
    )(spectra, left, table)


def body_by_slots(records, offsets, filter_index, signatures, thresholds):
    rows_here, shot_count = offsets.shape
    local_rcv, slab_len = records.shape
    slab_count = lax.axis_size(("shot", "rep"))
    rep_count = lax.axis_size("rep")
    rcv_count = lax.axis_size("rcv")
    sizes = tuple(lax.axis_size(axis) for axis in AXES)
    parts = slab_count * rcv_count
    tap_count = signatures.shape[1]
    slab_blocks = slab_len // tap_count
    steps = NT // tap_count
    capacity = max(2, 2 * shot_count // slab_count)
    row_count = rows_here * slab_count
    slots = row_count * capacity
    bins = NT // 2 // parts
    chunks = CHUNKS
    few = bins // chunks
    place = np.array(
        [
            [((slab // rep_count) * rcv_count + line) * rep_count + slab % rep_count for slab in range(slab_count)]
            for line in range(rcv_count)
        ]
    )

    time_table_fixed = fixed_time_table(NT).reshape(2, parts, chunks, few, NT)
    time_table_fixed = jnp.asarray(
        np.ascontiguousarray(time_table_fixed.transpose(2, 0, 1, 3, 4)).reshape(chunks, NT // chunks, NT)
    )
    table_x, table_y, table_r = (
        fixed_shot_table(count) for count in (row_count, shot_count, local_rcv * rcv_count)
    )
    grid_table = np.einsum("ajby,bkcx->cxyakj", table_y, table_x).astype(jnp.bfloat16)
    row_table = np.ascontiguousarray(grid_table.transpose(1, 0, 2, 3, 4, 5))
    points = 2 * row_count * shot_count
    grid_table = jnp.asarray(grid_table.reshape(points, points))
    row_table = jnp.asarray(row_table.reshape(points, points))
    same = np.eye(few, dtype=np.float32)
    cosine = jnp.asarray(np.kron(table_r[0, :, 0], same).astype(jnp.bfloat16))
    sine = jnp.asarray(np.kron(table_r[0, :, 1], same).astype(jnp.bfloat16))

    edge = 8
    padded = slab_blocks + 2 * edge
    vmem = pl.BlockSpec(memory_space=pltpu.VMEM)
    anywhere = pl.BlockSpec(memory_space=pl.ANY)
    rows = local_rcv * few
    table_width = tap_count * signatures.shape[0]
    low, wide = jnp.bfloat16, jnp.float32
    big = (records, time_table_fixed, grid_table, row_table, cosine, sine)
    spectra, residual = pl.pallas_call(
        functools.partial(whole_kernel, sizes, place),
        out_shape=(
            pltpu.VMEM((chunks, parts, rows // 2, 4 * shot_count), low),
            pltpu.VMEM(records.shape, wide),
        ),
        in_specs=[vmem] * 4 + [anywhere] * len(big),
        out_specs=(vmem, vmem),
        scratch_shapes=[pltpu.VMEM(array.shape, array.dtype) for array in big]
        + [
            pltpu.VMEM((edge, tap_count), jnp.int32),
            pltpu.VMEM((slab_count * edge, tap_count), jnp.int32),
            pltpu.VMEM((local_rcv, (steps - 1) * tap_count), wide),
            pltpu.VMEM((slots, tap_count), wide),
            pltpu.VMEM((slab_count * 2 * slots, points), low),
            pltpu.VMEM((2 * tap_count, table_width), low),
            pltpu.VMEM((2 * tap_count, table_width), low),
            pltpu.VMEM((slots * steps, padded), low),
            pltpu.VMEM((padded, slots * steps), low),
            pltpu.VMEM((local_rcv * slots, NT), low),
            pltpu.VMEM((local_rcv * slots, NT), wide),
            pltpu.VMEM((local_rcv * padded, tap_count), wide),
            pltpu.VMEM((local_rcv * padded, tap_count), wide),
        ]
        + [pltpu.VMEM((local_rcv, edge, tap_count), wide)] * 4
        + [pltpu.VMEM((chunks, parts, rows, 2 * slots), low)] * 4
        + [
            pltpu.VMEM((chunks, parts, rows // 2, 4 * shot_count), low),
            pltpu.VMEM((local_rcv // 4, slab_blocks, tap_count), low),
            pltpu.VMEM((local_rcv // 4, slab_blocks, tap_count), low),
            pltpu.VMEM((edge, (steps - 1) * tap_count), wide),
            pltpu.VMEM((local_rcv // 4 * padded, tap_count), wide),
            pltpu.VMEM((slots, tap_count), wide),
            pltpu.VMEM((slots * steps, padded), low),
            pltpu.VMEM((local_rcv // 4 * slots, NT), low),
            pltpu.VMEM((chunks, parts, rows, 2 * slots), low),
        ]
        + [pltpu.SemaphoreType.DMA((len(big),))]
        + [pltpu.SemaphoreType.DMA((slab_count - 1,))] * 2
        + [pltpu.SemaphoreType.DMA((SPANS, chunks, parts - 1))] * 4
        + [pltpu.SemaphoreType.DMA((SPANS + 1, 2))] * 2
        + [pltpu.SemaphoreType.DMA((2, chunks, parts // 2 - 1))] * 2
        + [pltpu.SemaphoreType.DMA((2,))],
        compiler_params=pltpu.CompilerParams(
            collective_id=0, has_side_effects=True, vmem_limit_bytes=60 * 2**20
        ),
    )(offsets, filter_index, signatures, thresholds, *big)
    model, residual = finish(spectra, residual, time_table_fixed, 2, local_rcv // 2)
    return (model.reshape(rows_here, local_rcv, shot_count, NT), residual)


def body(records, offsets, filter_index, signatures, thresholds):
    rows_here, shot_count = offsets.shape
    slab_count = lax.axis_size(("shot", "rep"))
    parts = slab_count * lax.axis_size("rcv")
    slots = rows_here * slab_count * max(2, 2 * shot_count // slab_count)
    table_rows = 2 * rows_here * slab_count * shot_count
    fits = table_rows <= 1024 and rows_here == 1 and slots == 64 and 4 * shot_count == 128
    fits = fits and records.shape[0] == 16 and NT // 2 // parts == 16
    slab_len, tap_count = records.shape[1], signatures.shape[1]
    fits = fits and tap_count == 128 and slab_len & (slab_len - 1) == 0
    fits = fits and tuple(lax.axis_size(axis) for axis in AXES) == (4, 2, 2)
    run = body_by_slots if fits else body_by_rows
    return run(records, offsets, filter_index, signatures, thresholds)


def solution(mesh):
    in_specs = (
        P(("groups", "rcv"), ("shot", "rep")),
        P(("groups", "shot", "rep"), None),
        P(("groups", "shot", "rep"), None),
        P(),
        P(),
    )
    out_specs = (
        P(("groups", "shot", "rep"), "rcv", None, None),
        P(("groups", "rcv"), ("shot", "rep")),
    )
    return jax.shard_map(body, mesh=mesh, in_specs=in_specs, out_specs=out_specs, check_vma=False)
```

```python
import functools
import math

import jax
import jax.numpy as jnp
import numpy as np
from jax import lax
from jax.experimental import pallas as pl
from jax.experimental.pallas import tpu as pltpu
from jax.sharding import PartitionSpec as P

NT = 512


def from_behind(value, axis, steps):
    count = lax.axis_size(axis)
    first, last = (max(0, -steps), min(count, count - steps))
    return lax.ppermute(value, axis, [(source, source + steps) for source in range(first, last)])


def time_table(count):
    samples = jnp.arange(count)
    bin_index = jnp.arange(count // 2)[:, None]
    angles = 2.0 * math.pi / count * (bin_index * samples[None, :] % count).astype(jnp.float32)
    parity = jnp.where(samples % 2 == 0, 1.0, -1.0).astype(jnp.float32)
    cosine = jnp.where(bin_index == 0, math.sqrt(1.0 / count), math.sqrt(2.0 / count)) * jnp.cos(
        angles
    )
    sine_part = jnp.where(
        bin_index == 0,
        math.sqrt(1.0 / count) * parity[None, :],
        -math.sqrt(2.0 / count) * jnp.sin(angles),
    )
    return jnp.stack([cosine, sine_part]).astype(jnp.bfloat16)


def shot_table(count):
    positions = jnp.arange(count)
    angles = (
        2.0
        * math.pi
        / count
        * (positions[:, None] * positions[None, :] % count).astype(jnp.float32)
    )
    scaling = 1.0 / math.sqrt(count)
    cosine = scaling * jnp.cos(angles)
    sine_part = scaling * jnp.sin(angles)
    upper_half = jnp.stack([cosine, sine_part], axis=1)
    lower_half = jnp.stack([-sine_part, cosine], axis=1)
    return jnp.stack([upper_half, lower_half]).astype(jnp.bfloat16)


def toeplitz_kernel(adjoint, taps_ref, out_ref):
    tap_count = taps_ref.shape[1]
    row_index = lax.broadcasted_iota(jnp.int32, (tap_count, tap_count), 0)
    col_index = lax.broadcasted_iota(jnp.int32, (tap_count, tap_count), 1)
    taps = taps_ref[...].astype(jnp.float32)
    for index in range(taps_ref.shape[0]):
        row = jnp.broadcast_to(taps[index : index + 1, :], (tap_count, tap_count))
        turned = pltpu.roll(row, 0, 1, stride=1, stride_axis=0)
        zeros = jnp.zeros_like(turned)
        near = jnp.where(col_index >= row_index, turned, zeros)
        far = jnp.where(col_index < row_index, turned, zeros)
        near, far = (near.T, far.T) if adjoint else (near, far)
        out_ref[index, :tap_count, :] = near.astype(jnp.bfloat16)
        out_ref[index, tap_count:, :] = far.astype(jnp.bfloat16)


def toeplitz_table(signatures, adjoint):
    count, tap_count = signatures.shape
    return pl.pallas_call(
        functools.partial(toeplitz_kernel, adjoint),
        out_shape=jax.ShapeDtypeStruct((count, 2 * tap_count, tap_count), jnp.bfloat16),
        in_specs=[pl.BlockSpec(memory_space=pltpu.VMEM)],
        out_specs=pl.BlockSpec(memory_space=pltpu.VMEM),
    )(signatures)


def apply_filter(traces, table, adjoint):
    empty = jnp.zeros_like(traces[:, :1])
    if adjoint:
        other = jnp.concatenate([traces[:, 1:], empty], axis=1)
    else:
        other = jnp.concatenate([empty, traces[:, :-1]], axis=1)
    return jnp.einsum(
        "sbrp,spq->sbrq",
        jnp.concatenate([traces, other], axis=3),
        table,
        preferred_element_type=jnp.float32,
    )


def rank_in_row(owners):
    shot_count = owners.shape[1]
    same_owner = owners[:, :, None] == owners[:, None, :]
    earlier = jnp.arange(shot_count)[None, :] < jnp.arange(shot_count)[:, None]
    return jnp.sum(same_owner & earlier[None], axis=2)


def to_slabs(payload):
    return lax.all_to_all(payload, ("shot", "rep"), split_axis=0, concat_axis=0, tiled=True)


def to_shots(payload):
    return lax.all_to_all(payload, ("shot", "rep"), split_axis=0, concat_axis=0, tiled=True)


def soft_limit(coefficients, threshold_row):
    magnitude = jnp.sqrt(coefficients[0] * coefficients[0] + coefficients[1] * coefficients[1])
    threshold_view = threshold_row[None, :, None, None]
    factor = 1.0 - threshold_view / jnp.maximum(magnitude, threshold_view)
    return (coefficients * factor[None]).astype(jnp.bfloat16)


def shrink(field_data, threshold_row, tables):
    table_time, table_x, table_y, table_r = tables
    rows_here, local_rcv, shot_count, sample_count = field_data.shape
    spectrum = jnp.einsum(
        "ckt,xryt->xckry",
        table_time,
        field_data.astype(jnp.bfloat16),
        preferred_element_type=jnp.float32,
    ).astype(jnp.bfloat16)
    bin_count = spectrum.shape[2]
    spectrum = spectrum.reshape(rows_here, 2, bin_count, local_rcv * shot_count)
    section_data = jnp.einsum(
        "akbx,xbfz->akfz",
        table_x,
        lax.all_to_all(spectrum, ("shot", "rep"), split_axis=2, concat_axis=0, tiled=True),
        preferred_element_type=jnp.float32,
    ).astype(jnp.bfloat16)
    all_rows, row_bins = (section_data.shape[1], section_data.shape[2])
    section_data = section_data.reshape(2, all_rows, row_bins, local_rcv, shot_count)
    section_data = lax.all_to_all(section_data, "rcv", split_axis=2, concat_axis=3, tiled=True)
    section_data = jnp.einsum(
        "ajby,bkfry->akfrj", table_y, section_data, preferred_element_type=jnp.float32
    ).astype(jnp.bfloat16)
    coefficients = jnp.einsum(
        "aqbr,bkfrj->akfqj", table_r, section_data, preferred_element_type=jnp.float32
    )
    shrunk = soft_limit(coefficients, threshold_row)
    section_data = jnp.einsum(
        "aqbr,akfqj->bkfrj", table_r, shrunk, preferred_element_type=jnp.float32
    ).astype(jnp.bfloat16)
    section_data = jnp.einsum(
        "ajby,akfrj->bkfry", table_y, section_data, preferred_element_type=jnp.float32
    ).astype(jnp.bfloat16)
    section_data = lax.all_to_all(section_data, "rcv", split_axis=3, concat_axis=2, tiled=True)
    section_data = section_data.reshape(2, all_rows, row_bins, local_rcv * shot_count)
    section_data = jnp.einsum(
        "akbx,akfz->bxfz", table_x, section_data, preferred_element_type=jnp.float32
    ).astype(jnp.bfloat16)
    result = jnp.einsum(
        "ckt,cxkz->xzt",
        table_time,
        lax.all_to_all(section_data, ("shot", "rep"), split_axis=1, concat_axis=2, tiled=True),
        preferred_element_type=jnp.float32,
    )
    return result.reshape(rows_here, local_rcv, shot_count, sample_count)


def body_by_rows(records, offsets, filter_index, signatures, thresholds):
    rows_here, shot_count = offsets.shape
    local_rcv, slab_len = records.shape
    slab_count = lax.axis_size(("shot", "rep"))
    rcv_count = lax.axis_size("rcv")
    tap_count = signatures.shape[1]
    sample_count = NT
    slab_blocks = slab_len // tap_count
    trace_blocks = sample_count // tap_count
    capacity = max(2, 2 * shot_count // slab_count)
    slot_count = slab_count * rows_here * capacity
    forward_tables = toeplitz_table(signatures, False)
    adjoint_tables = toeplitz_table(signatures, True)
    flat_index = filter_index.reshape(-1)
    forward_table = forward_tables[flat_index]
    adjoint_table = adjoint_tables[flat_index]
    owners = offsets // slab_len
    row_ids = jnp.arange(rows_here, dtype=jnp.int32)[:, None]
    slot_index = (
        owners * (rows_here * capacity) + row_ids * capacity + rank_in_row(owners)
    ).reshape(-1)
    every_offset = lax.all_gather(offsets, ("shot", "rep"), axis=0, tiled=True)
    every_owner = every_offset // slab_len
    every_start = every_offset // tap_count % slab_blocks
    every_rank = rank_in_row(every_owner)
    mine_mask = every_owner == lax.axis_index(("shot", "rep"))
    levels = jnp.arange(capacity, dtype=jnp.int32)
    picked = mine_mask[:, :, None] & (every_rank[:, :, None] == levels[None, None, :])
    table_in = jnp.sum(jnp.where(picked, every_start[:, :, None] + 1, 0), axis=1).reshape(-1)
    filled = table_in > 0
    block_steps = jnp.arange(trace_blocks, dtype=jnp.int32)
    target = jnp.where(
        filled[:, None],
        table_in[:, None] - 1 + block_steps[None, :],
        slab_blocks + trace_blocks - 1,
    )

    def correlate(record_field):
        record_low = (
            record_field.astype(jnp.bfloat16)
            .reshape(local_rcv, slab_blocks, tap_count)
            .transpose(1, 0, 2)
        )
        rim_blocks = from_behind(record_low[: trace_blocks - 1], ("shot", "rep"), -1)
        extended = jnp.concatenate(
            [record_low, rim_blocks, jnp.zeros((1, local_rcv, tap_count), jnp.bfloat16)], axis=0
        )
        windows = extended[target.reshape(-1)].reshape(
            slot_count, trace_blocks, local_rcv, tap_count
        )
        returned = to_shots(windows)
        traces = returned[slot_index]
        terms = apply_filter(traces, adjoint_table, True)
        terms = terms.reshape(rows_here, shot_count, trace_blocks, local_rcv, tap_count).transpose(
            0, 3, 1, 2, 4
        )
        return terms.reshape(rows_here, local_rcv, shot_count, sample_count)

    tables = (
        time_table(sample_count),
        shot_table(slab_count * rows_here),
        shot_table(shot_count),
        shot_table(local_rcv * rcv_count),
    )
    row_bins = sample_count // 2 // slab_count
    rcv_bins = row_bins // rcv_count
    bin_start = lax.axis_index(("shot", "rep")) * row_bins + lax.axis_index("rcv") * rcv_bins

    def threshold_for(level_index):
        return lax.dynamic_slice_in_dim(thresholds[level_index], bin_start, rcv_bins)

    model_field = shrink(correlate(records), threshold_for(0), tables)
    level_index = 1
    traces = model_field.astype(jnp.bfloat16).reshape(
        rows_here, local_rcv, shot_count, trace_blocks, tap_count
    )
    traces = traces.transpose(0, 2, 3, 1, 4).reshape(
        rows_here * shot_count, trace_blocks, local_rcv, tap_count
    )
    shots = apply_filter(traces, forward_table, False).astype(jnp.bfloat16)
    outgoing = (
        jnp.zeros((slot_count, trace_blocks, local_rcv, tap_count), jnp.bfloat16)
        .at[slot_index]
        .set(shots)
    )
    arrived = to_slabs(outgoing)
    slab_total = jnp.zeros((slab_blocks + trace_blocks, local_rcv, tap_count), jnp.float32)
    for block_step in range(trace_blocks):
        slab_total = slab_total.at[target[:, block_step]].add(
            arrived[:, block_step].astype(jnp.float32)
        )
    spill_over = slab_total[slab_blocks : slab_blocks + trace_blocks - 1]
    carried = from_behind(spill_over, ("shot", "rep"), 1)
    blended = slab_total[:slab_blocks].at[: trace_blocks - 1].add(carried)
    residual = records - blended.transpose(1, 0, 2).reshape(local_rcv, slab_len)
    model_field = shrink(model_field + correlate(residual), threshold_for(level_index), tables)
    return (model_field, residual)


def dot(left, right, left_dim=1, right_dim=0):
    return lax.dot_general(
        left, right, (((left_dim,), (right_dim,)), ((), ())), preferred_element_type=jnp.float32
    )


def fixed_time_table(count):
    samples = np.arange(count)
    bins = np.arange(count // 2)[:, None]
    angles = 2.0 * np.pi / count * (bins * samples[None, :] % count)
    scale = math.sqrt(2.0 / count)
    cosine = scale * np.cos(angles)
    sine = -scale * np.sin(angles)
    cosine[0] = math.sqrt(1.0 / count)
    sine[0] = math.sqrt(1.0 / count) * np.where(samples % 2 == 0, 1.0, -1.0)
    return np.stack([cosine, sine]).astype(jnp.bfloat16)


def fixed_shot_table(count):
    positions = np.arange(count)
    angles = 2.0 * np.pi / count * (positions[:, None] * positions[None, :] % count)
    cosine = np.cos(angles) / math.sqrt(count)
    sine = np.sin(angles) / math.sqrt(count)
    table = np.stack([np.stack([cosine, sine], 1), np.stack([-sine, cosine], 1)])
    return table.astype(jnp.bfloat16).astype(np.float32)


MESH = pl.DeviceIdType.MESH
AXES = ("shot", "rcv", "rep")


def neighbours(sizes):
    every = [(a, b, c) for a in range(sizes[0]) for b in range(sizes[1]) for c in range(sizes[2])]
    far = sizes[0] // 2
    return sorted(every[1:], key=lambda step: (abs(step[0] - far), -step[1], -step[2]))


def device_at(sizes, step):
    spot = [lax.rem(lax.axis_index(axis) + hop, size) for axis, hop, size in zip(AXES, step, sizes)]
    index = (spot[0] * sizes[1] + spot[1]) * sizes[2] + spot[2]
    return dict(zip(AXES, spot)), index


def build_taps(signature_ref, adjoint, out_ref):
    count, taps = signature_ref.shape
    row_index = lax.broadcasted_iota(jnp.int32, (taps, taps), 0)
    col_index = lax.broadcasted_iota(jnp.int32, (taps, taps), 1)
    values = signature_ref[...].astype(jnp.float32)
    for index in range(count):
        row = jnp.broadcast_to(values[index : index + 1, :], (taps, taps))
        turned = pltpu.roll(row, 0, 1, stride=1, stride_axis=0)
        zeros = jnp.zeros_like(turned)
        near = jnp.where(col_index >= row_index, turned, zeros)
        far = jnp.where(col_index < row_index, turned, zeros)
        near, far = (near.T, far.T) if adjoint else (near, far)
        where = slice(index * taps, (index + 1) * taps)
        out_ref[:taps, where] = near.astype(jnp.bfloat16)
        out_ref[taps:, where] = far.astype(jnp.bfloat16)


def pick_signature(every, picks_ref):
    slots, width = picks_ref.shape
    picks = jnp.concatenate([picks_ref[...]] * (every.shape[0] // slots), axis=0)
    chosen = every[:, :width]
    for index in range(1, every.shape[1] // width):
        chosen = jnp.where(picks == index, every[:, index * width : (index + 1) * width], chosen)
    return chosen


def correlate_line(line, padded, select_ref, blocks_ref, taps_ref, picks_ref, field_ref, traces_ref):
    slots, width = picks_ref.shape
    blocks = blocks_ref[pl.ds(pl.multiple_of(line * padded, 8), padded)].astype(jnp.bfloat16)
    window = dot(select_ref[...], blocks).astype(jnp.bfloat16)
    later = jnp.concatenate([window[slots:], jnp.zeros((slots, width), window.dtype)], axis=0)
    terms = pick_signature(dot(jnp.concatenate([window, later], axis=1), taps_ref[...]), picks_ref)
    steps = terms.shape[0] // slots
    terms = jnp.concatenate(
        [terms[step * slots : (step + 1) * slots] for step in range(steps)], axis=1
    )
    where = pl.ds(pl.multiple_of(line * slots, slots), slots)
    if field_ref is not None:
        terms = terms + field_ref[where]
    traces_ref[where] = terms.astype(jnp.bfloat16)


def blend_line(line, place_ref, field_ref, taps_ref, picks_ref):
    slots, width = picks_ref.shape
    trace = field_ref[pl.ds(pl.multiple_of(line * slots, slots), slots)].astype(jnp.bfloat16)
    steps = trace.shape[1] // width
    stacked = jnp.concatenate(
        [trace[:, step * width : (step + 1) * width] for step in range(steps)], axis=0
    )
    earlier = jnp.concatenate([jnp.zeros((slots, width), trace.dtype), stacked[:-slots]], axis=0)
    shots = pick_signature(dot(jnp.concatenate([stacked, earlier], axis=1), taps_ref[...]), picks_ref)
    return dot(place_ref[...], shots.astype(jnp.bfloat16))


def spectra_chunk(table, traces_ref, out_ref, lines, rcv, slots):
    parts, rows, lanes = out_ref.shape
    bins = rows // rcv
    half = parts * bins
    pack = max(1, 16 // bins)
    together = math.gcd(len(lines), 4)
    for first in range(lines[0], lines[-1] + 1, together):
        both = dot(table, traces_ref[first * slots : (first + together) * slots], 1, 1)
        for low in range(0, together, pack):
            pieces = []
            for line in range(low, low + pack):
                piece = both[:, line * slots : (line + 1) * slots]
                joined = jnp.concatenate([piece[:half], piece[half:]], axis=1)
                pieces.append(joined.reshape(parts, bins, lanes))
            out_ref[:, (first + low) * bins : (first + low + pack) * bins] = jnp.concatenate(
                pieces, axis=1
            ).astype(jnp.bfloat16)


def bins_chunk(place, halves, spectra_ref, go_ref, back_ref, cosine, sine, level, out_ref):
    _, rows, _ = spectra_ref.shape
    rcv_count, slab_count = place.shape
    joined = jnp.concatenate(
        [
            jnp.concatenate([spectra_ref[int(index)] for index in line], axis=1)
            for line in place
        ],
        axis=0,
    )
    section = dot(joined, go_ref[...]).astype(jnp.bfloat16)
    half = section.shape[1] // 2
    near = dot(cosine, section)
    far = dot(sine, section)
    real = near[:, :half] + far[:, half:]
    imag = near[:, half:] - far[:, :half]
    factor = 1.0 - level / jnp.maximum(jnp.sqrt(real * real + imag * imag), level)
    shrunk = jnp.concatenate([real * factor, imag * factor], axis=1).astype(jnp.bfloat16)
    near = dot(cosine, shrunk)
    far = dot(sine, shrunk)
    section = jnp.concatenate(
        [near[:, :half] - far[:, half:], far[:, :half] + near[:, half:]], axis=1
    ).astype(jnp.bfloat16)
    result = dot(section, back_ref[...], 1, 1).astype(jnp.bfloat16)
    width = result.shape[1] // slab_count
    for line in range(rcv_count):
        for slab in range(slab_count):
            piece = result[line * rows : (line + 1) * rows, slab * width : (slab + 1) * width]
            if halves == 2:
                piece = jnp.concatenate([piece[: rows // 2], piece[rows // 2 :]], axis=1)
            out_ref[int(place[line, slab])] = piece


def level_of(levels_ref, index, first, bins, copies_of):
    width = levels_ref.shape[1]
    lane = lax.broadcasted_iota(jnp.int32, (bins, width), 1)
    row = lax.broadcasted_iota(jnp.int32, (bins, width), 0)
    values = jnp.broadcast_to(levels_ref[index : index + 1, :], (bins, width))
    column = jnp.sum(jnp.where(lane == row + first, values, 0.0), axis=1, keepdims=True)
    return jnp.concatenate([column] * copies_of, axis=0)


def upright(spectra_ref, chunk, lines, bins, group_lanes):
    parts = spectra_ref.shape[1]
    pack = max(1, 16 // bins)
    count = group_lanes // 2
    pieces = []
    for low_line in range(lines[0], lines[-1] + 1, pack):
        block = spectra_ref[chunk, :, low_line * bins : (low_line + pack) * bins].astype(jnp.float32)
        for line in range(pack):
            turned = block[:, line * bins : (line + 1) * bins].reshape(parts * bins, -1).T
            turned = turned.astype(jnp.bfloat16)
            for low in range(0, turned.shape[0], group_lanes):
                pieces.append(
                    jnp.concatenate(
                        [turned[low : low + count], turned[low + count : low + 2 * count]], axis=1
                    )
                )
    return jnp.concatenate(pieces, axis=0)


CHUNKS = 2
SPANS = 4
UNROLL = 4


def whole_kernel(
    sizes,
    place,
    offsets_ref,
    filters_ref,
    signatures_ref,
    levels_ref,
    records_hbm,
    table_hbm,
    grid_hbm,
    cosine_hbm,
    sine_hbm,
    final_ref,
    left_ref,
    records_ref,
    table_ref,
    grid_ref,
    cosine_ref,
    sine_ref,
    row_ref,
    rows_ref,
    rim_ref,
    picks_ref,
    slot_table_ref,
    row_table_ref,
    adjoint_ref,
    forward_ref,
    select_ref,
    place_ref,
    traces_ref,
    field_ref,
    blocks_ref,
    rest_ref,
    head_ref,
    spill_ref,
    carried_ref,
    ahead_ref,
    sent_ref,
    got_ref,
    answer_ref,
    home_ref,
    reply_ref,
    raw_ref,
    other_raw_ref,
    other_rim_ref,
    other_blocks_ref,
    other_picks_ref,
    other_select_ref,
    other_traces_ref,
    other_sent_ref,
    load_sems,
    row_sends,
    row_recvs,
    go_sends,
    go_recvs,
    back_sends,
    back_recvs,
    rim_sends,
    rim_recvs,
    near_sends,
    near_recvs,
    raw_sems,
):
    slots, width = picks_ref.shape
    rcv, slab_len = records_ref.shape
    blocks = slab_len // width
    padded = blocks_ref.shape[0] // rcv
    chunks, _, samples = table_ref.shape
    steps = samples // width
    parts = place.size
    slab_count = place.shape[1]
    few = samples // 2 // parts // chunks
    quarter = rcv // 4
    early_spans = ((quarter, 2 * quarter), (2 * quarter, rcv))
    late_halves = ((0, 2 * quarter), (2 * quarter, rcv))
    late_spans = tuple((number * quarter, (number + 1) * quarter) for number in range(4))
    edge = head_ref.shape[1]
    all_rcv = rcv * place.shape[0]
    shot_count = offsets_ref.shape[1]
    row_count = slab_count
    capacity = slots // row_count
    wide = jnp.float32

    loads = [
        pltpu.make_async_copy(source, target, load_sems.at[number])
        for number, (source, target) in enumerate(
            (
                (records_hbm, records_ref),
                (table_hbm, table_ref),
                (grid_hbm, grid_ref),
                (cosine_hbm, cosine_ref),
                (sine_hbm, sine_ref),
            )
        )
    ]
    for load in loads:
        load.start()
    barrier = pltpu.get_barrier_semaphore()
    hops = neighbours(sizes)
    for hop in hops:
        pl.semaphore_signal(barrier, inc=1, device_id=device_at(sizes, hop)[0], device_id_type=MESH)
    mine = device_at(sizes, (0, 0, 0))[1]
    slab = lax.axis_index("shot") * sizes[2] + lax.axis_index("rep")
    last_slab = slab_count - 1

    def slab_device(shift):
        other = lax.rem(slab + shift + slab_count, slab_count)
        return {
            "shot": other // sizes[2],
            "rcv": lax.axis_index("rcv"),
            "rep": lax.rem(other, sizes[2]),
        }

    row_ref[...] = jnp.zeros_like(row_ref)
    row_ref[0:1, :shot_count] = offsets_ref[...]
    row_ref[1:2, :shot_count] = filters_ref[...]
    pl.semaphore_wait(barrier, len(hops))

    tile = row_ref.shape[0]
    here = pl.ds(pl.multiple_of(slab * tile, tile), tile)
    row_copies = []
    for hop in hops:
        if hop[1] == 0:
            number = len(row_copies)
            copy = pltpu.make_async_remote_copy(
                src_ref=row_ref,
                dst_ref=rows_ref.at[here],
                send_sem=row_sends.at[number],
                recv_sem=row_recvs.at[number],
                device_id=device_at(sizes, hop)[0],
                device_id_type=MESH,
            )
            copy.start()
            row_copies.append(copy)
    rows_ref[here] = row_ref[...]
    loads[0].wait()
    apart = slab_count // 2
    partner_slab = lax.rem(slab + apart, slab_count)
    partner = device_at(sizes, (sizes[0] // 2, 0, 0))[1]
    first_rim = pltpu.make_async_remote_copy(
        src_ref=records_ref.at[:, pl.ds(0, rim_ref.shape[1])],
        dst_ref=rim_ref,
        send_sem=rim_sends.at[SPANS, 0],
        recv_sem=rim_recvs.at[SPANS, 0],
        device_id=slab_device(-1),
        device_id_type=MESH,
    )
    partner_rim = pltpu.make_async_remote_copy(
        src_ref=records_ref.at[pl.ds(0, tile), pl.ds(0, rim_ref.shape[1])],
        dst_ref=other_rim_ref,
        send_sem=rim_sends.at[SPANS, 1],
        recv_sem=rim_recvs.at[SPANS, 1],
        device_id=slab_device(apart - 1),
        device_id_type=MESH,
    )

    @pl.when(slab > 0)
    def _():
        first_rim.start()
        partner_rim.start()

    for line in range(rcv):
        blocks_ref[line * padded + blocks : (line + 1) * padded] = jnp.zeros(
            (padded - blocks, width), wide
        )
    for block in range(blocks):
        blocks_ref[pl.ds(block, rcv, stride=padded), :] = records_ref[
            :, block * width : (block + 1) * width
        ]
    for line in range(quarter):
        raw_ref[line] = blocks_ref[line * padded : line * padded + blocks].astype(jnp.bfloat16)
    raw = pltpu.make_async_remote_copy(
        src_ref=raw_ref,
        dst_ref=other_raw_ref,
        send_sem=raw_sems.at[0],
        recv_sem=raw_sems.at[1],
        device_id=slab_device(apart),
        device_id_type=MESH,
    )
    raw.start()
    build_taps(signatures_ref, True, adjoint_ref)
    for copy in row_copies:
        copy.wait_recv()

    lane = lax.broadcasted_iota(jnp.int32, (row_count, width), 1)
    valid = lane < shot_count
    zero = jnp.zeros((row_count, width), jnp.int32)
    start_sample = jnp.where(valid, rows_ref[pl.ds(0, row_count, stride=tile), :], zero)
    signature = jnp.where(valid, rows_ref[pl.ds(1, row_count, stride=tile), :], zero)
    block_bits = width.bit_length() - 1
    slab_bits = slab_len.bit_length() - 1
    owner = lax.shift_right_logical(start_sample, slab_bits)
    rank = zero
    for step in range(1, shot_count):
        same = (pltpu.roll(owner, step, 1) == owner) & (lane >= step)
        rank = rank + same.astype(jnp.int32)
    key = jnp.where(valid, owner * capacity + rank + 1, zero)
    first_block = (lax.shift_right_logical(start_sample, block_bits) & (blocks - 1)).astype(wide)
    signature = signature.astype(wide)
    block_index = lax.broadcasted_iota(jnp.int32, (slots, padded), 1).astype(wide)

    def choose(owner_slab, into_picks_ref, into_select_ref):
        firsts, picks = [], []
        for level in range(capacity):
            taken = key == owner_slab * capacity + level + 1
            empty = jnp.zeros_like(first_block)
            firsts.append(
                jnp.sum(jnp.where(taken, first_block + 1.0, empty), axis=1, keepdims=True)
            )
            picks.append(jnp.sum(jnp.where(taken, signature, empty), axis=1, keepdims=True))
        firsts = jnp.broadcast_to(jnp.concatenate(firsts, axis=0), (slots, padded))
        firsts = jnp.where(firsts > 0.5, firsts - 1.0, -float(samples))
        into_picks_ref[...] = jnp.broadcast_to(jnp.concatenate(picks, axis=0), (slots, width))
        select = jnp.concatenate(
            [(block_index == firsts + float(step)).astype(wide) for step in range(steps)], axis=0
        )
        into_select_ref[...] = select.astype(jnp.bfloat16)
        return select

    select = choose(slab, picks_ref, select_ref)

    @pl.when(slab < last_slab)
    def _():
        first_rim.wait_recv()
        for step in range(rim_ref.shape[1] // width):
            blocks_ref[pl.ds(blocks + step, rcv, stride=padded), :] = rim_ref[
                :, step * width : (step + 1) * width
            ]

    loads[1].wait()

    def exchange(source, target, send_sems, recv_sems, low, rows):
        made = []
        where = pl.ds(low, rows)
        for number, hop in enumerate(hops):
            device, index = device_at(sizes, hop)
            copy = pltpu.make_async_remote_copy(
                src_ref=source.at[index, where],
                dst_ref=target.at[mine, where],
                send_sem=send_sems.at[number],
                recv_sem=recv_sems.at[number],
                device_id=device,
                device_id_type=MESH,
            )
            copy.start()
            made.append(copy)
        target[mine, where] = source[mine, where]
        return made

    def correlate_span(span, from_ref, model, one_select_ref, one_picks_ref, into_ref):
        def one(line, carry):
            correlate_line(
                line, padded, one_select_ref, from_ref, adjoint_ref, one_picks_ref, model, into_ref
            )
            return carry

        unroll = UNROLL if model is not None or span[0] == quarter else UNROLL // 2
        lax.fori_loop(span[0], span[1], one, 0, unroll=unroll)

    def send_span(number, span, from_ref, model):
        correlate_span(span, from_ref, model, select_ref, picks_ref, traces_ref)
        made = []
        for chunk in range(chunks):
            spectra_chunk(
                table_ref[chunk], traces_ref, sent_ref.at[chunk], range(*span), rcv, slots
            )
            made.append(
                exchange(
                    sent_ref.at[chunk],
                    got_ref.at[chunk],
                    go_sends.at[number, chunk],
                    go_recvs.at[number, chunk],
                    span[0] * few,
                    (span[1] - span[0]) * few,
                )
            )
        return made

    def send_near(number, from_ref, one_select_ref, one_picks_ref, into_ref, out_ref, owner):
        span = (0, quarter)
        correlate_span(span, from_ref, None, one_select_ref, one_picks_ref, into_ref)
        where = pl.ds(0, quarter * few)
        depth, place_x, core = (lax.axis_index(axis) for axis in AXES)
        made = []
        for chunk in range(chunks):
            spectra_chunk(
                table_ref[chunk], into_ref, out_ref.at[chunk], range(*span), rcv, slots
            )
            copies = []
            for hop in range(1, 8):
                spot = (
                    depth + (hop // 4) * (1 - 2 * lax.rem(depth, 2)),
                    lax.rem(place_x + hop // 2 % 2, sizes[1]),
                    lax.rem(core + hop % 2, sizes[2]),
                )
                index = (spot[0] * sizes[1] + spot[1]) * sizes[2] + spot[2]
                copy = pltpu.make_async_remote_copy(
                    src_ref=out_ref.at[chunk, index, where],
                    dst_ref=got_ref.at[chunk, owner, where],
                    send_sem=near_sends.at[number, chunk, hop - 1],
                    recv_sem=near_recvs.at[number, chunk, hop - 1],
                    device_id=dict(zip(AXES, spot)),
                    device_id_type=MESH,
                )
                copy.start()
                copies.append(copy)
            got_ref[chunk, owner, where] = out_ref[chunk, mine, where]
            made.append(copies)
        return made

    def level_at(index, chunk):
        return level_of(levels_ref, index, (mine * chunks + chunk) * few, few, all_rcv)

    going = [
        send_span(number, span, blocks_ref, None) for number, span in enumerate(early_spans)
    ]

    going.append(send_near(0, blocks_ref, select_ref, picks_ref, traces_ref, sent_ref, mine))
    choose(partner_slab, other_picks_ref, other_select_ref)
    raw.wait_recv()
    for line in range(quarter):
        other_blocks_ref[line * padded : line * padded + blocks] = other_raw_ref[line].astype(wide)
        other_blocks_ref[line * padded + blocks : (line + 1) * padded] = jnp.zeros(
            (padded - blocks, width), wide
        )

    @pl.when(partner_slab < last_slab)
    def _():
        partner_rim.wait_recv()
        for step in range(rim_ref.shape[1] // width):
            other_blocks_ref[pl.ds(blocks + step, quarter, stride=padded), :] = other_rim_ref[
                :quarter, step * width : (step + 1) * width
            ]

    going.append(
        send_near(
            1, other_blocks_ref, other_select_ref, other_picks_ref, other_traces_ref, other_sent_ref, partner
        )
    )
    place_ref[...] = select.T.astype(jnp.bfloat16)
    build_taps(signatures_ref, False, forward_ref)
    repeated = key
    for shift in range(shot_count, width, shot_count):
        repeated = repeated + pltpu.roll(key, shift, 1)
    points = row_count * shot_count
    repeated = jnp.concatenate([repeated] * (points // width), axis=1)
    point = lax.broadcasted_iota(jnp.int32, (row_count, points), 1)
    row = lax.broadcasted_iota(jnp.int32, (row_count, points), 0)
    shot_bits = shot_count.bit_length() - 1
    repeated = jnp.where(lax.shift_right_logical(point, shot_bits) == row, repeated, 0)
    chosen = jnp.concatenate(
        [(repeated == number + 1).astype(wide) for number in range(slab_count * capacity)], axis=0
    ).astype(jnp.bfloat16)
    for load in loads[2:]:
        load.wait()
    for half in range(2):
        for number in range(row_count):
            low = (2 * number + half) * shot_count
            source = half * points + number * shot_count
            row_table_ref[low : low + shot_count] = grid_ref[source : source + shot_count]
        part = dot(chosen, grid_ref[half * points : (half + 1) * points]).astype(jnp.bfloat16)
        for number in range(slab_count):
            low = (2 * number + half) * slots
            slot_table_ref[low : low + slots] = part[number * slots : (number + 1) * slots]

    coming = {}

    def send_back(number, chunk):
        span = late_halves[number]
        coming[number, chunk] = exchange(
            answer_ref.at[chunk],
            home_ref.at[chunk],
            back_sends.at[number, chunk],
            back_recvs.at[number, chunk],
            span[0] * few,
            (span[1] - span[0]) * few,
        )

    for chunk in range(chunks):
        for made in going:
            for copy in made[chunk]:
                copy.wait_recv()
        bins_chunk(
            place, 1, got_ref.at[chunk], slot_table_ref, slot_table_ref, cosine_ref[...], sine_ref[...], level_at(0, chunk), answer_ref.at[chunk]
        )
        send_back(0, chunk)
    for number in range(1, len(late_halves)):
        for chunk in range(chunks):
            send_back(number, chunk)
    for copy in row_copies:
        copy.wait_send()

    raw.wait_send()

    @pl.when(slab > 0)
    def _():
        first_rim.wait_send()
        partner_rim.wait_send()

    for made in going:
        for chunk in made:
            for copy in chunk:
                copy.wait_send()

    def halo(number):
        low, high = late_spans[number]
        where = pl.ds(low, high - low)
        onward = pltpu.make_async_remote_copy(
            src_ref=spill_ref.at[where],
            dst_ref=carried_ref.at[where],
            send_sem=rim_sends.at[number, 0],
            recv_sem=rim_recvs.at[number, 0],
            device_id=slab_device(1),
            device_id_type=MESH,
        )
        backward = pltpu.make_async_remote_copy(
            src_ref=head_ref.at[where],
            dst_ref=ahead_ref.at[where],
            send_sem=rim_sends.at[number, 1],
            recv_sem=rim_recvs.at[number, 1],
            device_id=slab_device(-1),
            device_id_type=MESH,
        )
        return onward, backward

    def subtract(number):
        low, high = late_spans[number]
        if number % 2 == 0:
            for chunk in range(chunks):
                for copy in coming[number // 2, chunk]:
                    copy.wait_recv()
        together = math.gcd(high - low, 4)
        for first in range(low, high, together):
            lines = range(first, first + together)
            field_ref[first * slots : (first + together) * slots] = sum(
                dot(upright(home_ref, chunk, lines, few, 2 * slots), table_ref[chunk])
                for chunk in range(chunks)
            )

        def one(line, carry):
            blended = blend_line(line, place_ref, field_ref, forward_ref, picks_ref)
            start = pl.multiple_of(line * padded, 8)
            left = blocks_ref[pl.ds(start, blocks)] - blended[:blocks]
            rest_ref[pl.ds(start, blocks)] = left
            rest_ref[pl.ds(start + blocks, padded - blocks)] = jnp.zeros(
                (padded - blocks, width), wide
            )
            head_ref[line] = left[:edge]
            spill_ref[line] = blended[blocks : blocks + edge]
            return carry

        lax.fori_loop(low, high, one, 0, unroll=UNROLL)
        onward, backward = halo(number)

        @pl.when(slab < last_slab)
        def _():
            onward.start()

        @pl.when(slab > 0)
        def _():
            backward.start()

    def correlate_rest(number):
        low, high = late_spans[number]
        onward, backward = halo(number)

        @pl.when(slab > 0)
        def _():
            onward.wait_recv()
            for line in range(low, high):
                here = pl.ds(line * padded, edge)
                rest_ref[here] = rest_ref[here] - carried_ref[line]

        @pl.when(slab < last_slab)
        def _():
            backward.wait_recv()
            for line in range(low, high):
                rest_ref[pl.ds(line * padded + blocks, edge)] = ahead_ref[line] - spill_ref[line]
            onward.wait_send()

        @pl.when(slab > 0)
        def _():
            backward.wait_send()

        return send_span(number, late_spans[number], rest_ref, field_ref)

    again = []
    for number in range(0, len(late_spans), 2):
        subtract(number)
        subtract(number + 1)
        again.append(correlate_rest(number))
        again.append(correlate_rest(number + 1))

    for block in range(blocks):
        left_ref[:, block * width : (block + 1) * width] = rest_ref[
            pl.ds(block, rcv, stride=padded), :
        ]
    for made in coming.values():
        for copy in made:
            copy.wait_send()
    final = []
    for chunk in range(chunks):
        for made in again:
            for copy in made[chunk]:
                copy.wait_recv()
        bins_chunk(
            place, 2, got_ref.at[chunk], slot_table_ref, row_table_ref, cosine_ref[...], sine_ref[...], level_at(1, chunk), reply_ref.at[chunk]
        )
        final.append(
            exchange(
                reply_ref.at[chunk], final_ref.at[chunk], back_sends.at[0, chunk], back_recvs.at[0, chunk], 0, reply_ref.shape[2]
            )
        )
    for made in again:
        for chunk in made:
            for copy in chunk:
                copy.wait_send()
    for made in final:
        for copy in made:
            copy.wait()


def finish_kernel(bins, spectra_ref, left_ref, table_ref, model_ref, out_ref, sem):
    chunks = spectra_ref.shape[0]
    groups, together, count, _ = model_ref.shape
    step = pl.program_id(0)
    copy = pltpu.make_async_copy(left_ref, out_ref, sem)

    @pl.when(step == 0)
    def _():
        copy.start()

    fields = sum(
        dot(upright(spectra_ref, chunk, range(together), bins, 2 * count), table_ref[chunk])
        for chunk in range(chunks)
    )
    for line in range(together):
        for group in range(groups):
            low = (line * groups + group) * count
            model_ref[group, line] = fields[low : low + count]

    @pl.when(step == pl.num_programs(0) - 1)
    def _():
        copy.wait()


def finish(spectra, left, table, groups, rcv):
    chunks, parts, rows, lanes = spectra.shape
    samples = table.shape[2]
    bins = rows // rcv
    count = lanes // 2 // groups
    together = math.gcd(rcv, 4)
    whole = pl.BlockSpec(memory_space=pltpu.VMEM)
    return pl.pallas_call(
        functools.partial(finish_kernel, bins),
        grid=(rcv // together,),
        out_shape=(
            jax.ShapeDtypeStruct((groups, rcv, count, samples), jnp.float32),
            jax.ShapeDtypeStruct(left.shape, jnp.float32),
        ),
        in_specs=[
            pl.BlockSpec((chunks, parts, together * bins, lanes), lambda i: (0, 0, i, 0)),
            whole,
            whole,
        ],
        out_specs=(
            pl.BlockSpec((groups, together, count, samples), lambda i: (0, i, 0, 0)),
            pl.BlockSpec(memory_space=pl.ANY),
        ),
        scratch_shapes=[pltpu.SemaphoreType.DMA],
        compiler_params=pltpu.CompilerParams(vmem_limit_bytes=16 * 2**20),
    )(spectra, left, table)


def body_by_slots(records, offsets, filter_index, signatures, thresholds):
    rows_here, shot_count = offsets.shape
    local_rcv, slab_len = records.shape
    slab_count = lax.axis_size(("shot", "rep"))
    rep_count = lax.axis_size("rep")
    rcv_count = lax.axis_size("rcv")
    sizes = tuple(lax.axis_size(axis) for axis in AXES)
    parts = slab_count * rcv_count
    tap_count = signatures.shape[1]
    slab_blocks = slab_len // tap_count
    steps = NT // tap_count
    capacity = max(2, 2 * shot_count // slab_count)
    row_count = rows_here * slab_count
    slots = row_count * capacity
    bins = NT // 2 // parts
    chunks = CHUNKS
    few = bins // chunks
    place = np.array(
        [
            [((slab // rep_count) * rcv_count + line) * rep_count + slab % rep_count for slab in range(slab_count)]
            for line in range(rcv_count)
        ]
    )

    time_table_fixed = fixed_time_table(NT).reshape(2, parts, chunks, few, NT)
    time_table_fixed = jnp.asarray(
        np.ascontiguousarray(time_table_fixed.transpose(2, 0, 1, 3, 4)).reshape(chunks, NT // chunks, NT)
    )
    table_x, table_y, table_r = (
        fixed_shot_table(count) for count in (row_count, shot_count, local_rcv * rcv_count)
    )
    grid_table = np.einsum("ajby,bkcx->cxyakj", table_y, table_x).astype(jnp.bfloat16)
    points = 2 * row_count * shot_count
    grid_table = jnp.asarray(grid_table.reshape(points, points))
    same = np.eye(few, dtype=np.float32)
    cosine = jnp.asarray(np.kron(table_r[0, :, 0], same).astype(jnp.bfloat16))
    sine = jnp.asarray(np.kron(table_r[0, :, 1], same).astype(jnp.bfloat16))

    edge = 8
    padded = slab_blocks + 2 * edge
    vmem = pl.BlockSpec(memory_space=pltpu.VMEM)
    anywhere = pl.BlockSpec(memory_space=pl.ANY)
    rows = local_rcv * few
    table_width = tap_count * signatures.shape[0]
    low, wide = jnp.bfloat16, jnp.float32
    big = (records, time_table_fixed, grid_table, cosine, sine)
    spectra, residual = pl.pallas_call(
        functools.partial(whole_kernel, sizes, place),
        out_shape=(
            pltpu.VMEM((chunks, parts, rows // 2, 4 * shot_count), low),
            pltpu.VMEM(records.shape, wide),
        ),
        in_specs=[vmem] * 4 + [anywhere] * len(big),
        out_specs=(vmem, vmem),
        scratch_shapes=[pltpu.VMEM(array.shape, array.dtype) for array in big]
        + [
            pltpu.VMEM((edge, tap_count), jnp.int32),
            pltpu.VMEM((slab_count * edge, tap_count), jnp.int32),
            pltpu.VMEM((local_rcv, (steps - 1) * tap_count), wide),
            pltpu.VMEM((slots, tap_count), wide),
            pltpu.VMEM((slab_count * 2 * slots, points), low),
            pltpu.VMEM((points, points), low),
            pltpu.VMEM((2 * tap_count, table_width), low),
            pltpu.VMEM((2 * tap_count, table_width), low),
            pltpu.VMEM((slots * steps, padded), low),
            pltpu.VMEM((padded, slots * steps), low),
            pltpu.VMEM((local_rcv * slots, NT), low),
            pltpu.VMEM((local_rcv * slots, NT), wide),
            pltpu.VMEM((local_rcv * padded, tap_count), wide),
            pltpu.VMEM((local_rcv * padded, tap_count), wide),
        ]
        + [pltpu.VMEM((local_rcv, edge, tap_count), wide)] * 4
        + [pltpu.VMEM((chunks, parts, rows, 2 * slots), low)] * 4
        + [
            pltpu.VMEM((chunks, parts, rows // 2, 4 * shot_count), low),
            pltpu.VMEM((local_rcv // 4, slab_blocks, tap_count), low),
            pltpu.VMEM((local_rcv // 4, slab_blocks, tap_count), low),
            pltpu.VMEM((edge, (steps - 1) * tap_count), wide),
            pltpu.VMEM((local_rcv // 4 * padded, tap_count), wide),
            pltpu.VMEM((slots, tap_count), wide),
            pltpu.VMEM((slots * steps, padded), low),
            pltpu.VMEM((local_rcv // 4 * slots, NT), low),
            pltpu.VMEM((chunks, parts, rows, 2 * slots), low),
        ]
        + [pltpu.SemaphoreType.DMA((len(big),))]
        + [pltpu.SemaphoreType.DMA((slab_count - 1,))] * 2
        + [pltpu.SemaphoreType.DMA((SPANS, chunks, parts - 1))] * 4
        + [pltpu.SemaphoreType.DMA((SPANS + 1, 2))] * 2
        + [pltpu.SemaphoreType.DMA((2, chunks, parts // 2 - 1))] * 2
        + [pltpu.SemaphoreType.DMA((2,))],
        compiler_params=pltpu.CompilerParams(
            collective_id=0, has_side_effects=True, vmem_limit_bytes=60 * 2**20
        ),
    )(offsets, filter_index, signatures, thresholds, *big)
    model, residual = finish(spectra, residual, time_table_fixed, 2, local_rcv // 2)
    return (model.reshape(rows_here, local_rcv, shot_count, NT), residual)


def body(records, offsets, filter_index, signatures, thresholds):
    rows_here, shot_count = offsets.shape
    slab_count = lax.axis_size(("shot", "rep"))
    parts = slab_count * lax.axis_size("rcv")
    slots = rows_here * slab_count * max(2, 2 * shot_count // slab_count)
    table_rows = 2 * rows_here * slab_count * shot_count
    fits = table_rows <= 1024 and rows_here == 1 and slots == 64 and 4 * shot_count == 128
    fits = fits and records.shape[0] == 16 and NT // 2 // parts == 16
    slab_len, tap_count = records.shape[1], signatures.shape[1]
    fits = fits and tap_count == 128 and slab_len & (slab_len - 1) == 0
    fits = fits and tuple(lax.axis_size(axis) for axis in AXES) == (4, 2, 2)
    run = body_by_slots if fits else body_by_rows
    return run(records, offsets, filter_index, signatures, thresholds)


def solution(mesh):
    in_specs = (
        P(("groups", "rcv"), ("shot", "rep")),
        P(("groups", "shot", "rep"), None),
        P(("groups", "shot", "rep"), None),
        P(),
        P(),
    )
    out_specs = (
        P(("groups", "shot", "rep"), "rcv", None, None),
        P(("groups", "rcv"), ("shot", "rep")),
    )
    return jax.shard_map(body, mesh=mesh, in_specs=in_specs, out_specs=out_specs, check_vma=False)
```

```python
import functools
import math

import jax
import jax.numpy as jnp
import numpy as np
from jax import lax
from jax.experimental import pallas as pl
from jax.experimental.pallas import tpu as pltpu
from jax.sharding import PartitionSpec as P

NT = 512


def from_behind(value, axis, steps):
    count = lax.axis_size(axis)
    first, last = (max(0, -steps), min(count, count - steps))
    return lax.ppermute(value, axis, [(source, source + steps) for source in range(first, last)])


def time_table(count):
    samples = jnp.arange(count)
    bin_index = jnp.arange(count // 2)[:, None]
    angles = 2.0 * math.pi / count * (bin_index * samples[None, :] % count).astype(jnp.float32)
    parity = jnp.where(samples % 2 == 0, 1.0, -1.0).astype(jnp.float32)
    cosine = jnp.where(bin_index == 0, math.sqrt(1.0 / count), math.sqrt(2.0 / count)) * jnp.cos(
        angles
    )
    sine_part = jnp.where(
        bin_index == 0,
        math.sqrt(1.0 / count) * parity[None, :],
        -math.sqrt(2.0 / count) * jnp.sin(angles),
    )
    return jnp.stack([cosine, sine_part]).astype(jnp.bfloat16)


def shot_table(count):
    positions = jnp.arange(count)
    angles = (
        2.0
        * math.pi
        / count
        * (positions[:, None] * positions[None, :] % count).astype(jnp.float32)
    )
    scaling = 1.0 / math.sqrt(count)
    cosine = scaling * jnp.cos(angles)
    sine_part = scaling * jnp.sin(angles)
    upper_half = jnp.stack([cosine, sine_part], axis=1)
    lower_half = jnp.stack([-sine_part, cosine], axis=1)
    return jnp.stack([upper_half, lower_half]).astype(jnp.bfloat16)


def toeplitz_kernel(adjoint, taps_ref, out_ref):
    tap_count = taps_ref.shape[1]
    row_index = lax.broadcasted_iota(jnp.int32, (tap_count, tap_count), 0)
    col_index = lax.broadcasted_iota(jnp.int32, (tap_count, tap_count), 1)
    taps = taps_ref[...].astype(jnp.float32)
    for index in range(taps_ref.shape[0]):
        row = jnp.broadcast_to(taps[index : index + 1, :], (tap_count, tap_count))
        turned = pltpu.roll(row, 0, 1, stride=1, stride_axis=0)
        zeros = jnp.zeros_like(turned)
        near = jnp.where(col_index >= row_index, turned, zeros)
        far = jnp.where(col_index < row_index, turned, zeros)
        near, far = (near.T, far.T) if adjoint else (near, far)
        out_ref[index, :tap_count, :] = near.astype(jnp.bfloat16)
        out_ref[index, tap_count:, :] = far.astype(jnp.bfloat16)


def toeplitz_table(signatures, adjoint):
    count, tap_count = signatures.shape
    return pl.pallas_call(
        functools.partial(toeplitz_kernel, adjoint),
        out_shape=jax.ShapeDtypeStruct((count, 2 * tap_count, tap_count), jnp.bfloat16),
        in_specs=[pl.BlockSpec(memory_space=pltpu.VMEM)],
        out_specs=pl.BlockSpec(memory_space=pltpu.VMEM),
    )(signatures)


def apply_filter(traces, table, adjoint):
    empty = jnp.zeros_like(traces[:, :1])
    if adjoint:
        other = jnp.concatenate([traces[:, 1:], empty], axis=1)
    else:
        other = jnp.concatenate([empty, traces[:, :-1]], axis=1)
    return jnp.einsum(
        "sbrp,spq->sbrq",
        jnp.concatenate([traces, other], axis=3),
        table,
        preferred_element_type=jnp.float32,
    )


def rank_in_row(owners):
    shot_count = owners.shape[1]
    same_owner = owners[:, :, None] == owners[:, None, :]
    earlier = jnp.arange(shot_count)[None, :] < jnp.arange(shot_count)[:, None]
    return jnp.sum(same_owner & earlier[None], axis=2)


def to_slabs(payload):
    return lax.all_to_all(payload, ("shot", "rep"), split_axis=0, concat_axis=0, tiled=True)


def to_shots(payload):
    return lax.all_to_all(payload, ("shot", "rep"), split_axis=0, concat_axis=0, tiled=True)


def soft_limit(coefficients, threshold_row):
    magnitude = jnp.sqrt(coefficients[0] * coefficients[0] + coefficients[1] * coefficients[1])
    threshold_view = threshold_row[None, :, None, None]
    factor = 1.0 - threshold_view / jnp.maximum(magnitude, threshold_view)
    return (coefficients * factor[None]).astype(jnp.bfloat16)


def shrink(field_data, threshold_row, tables):
    table_time, table_x, table_y, table_r = tables
    rows_here, local_rcv, shot_count, sample_count = field_data.shape
    spectrum = jnp.einsum(
        "ckt,xryt->xckry",
        table_time,
        field_data.astype(jnp.bfloat16),
        preferred_element_type=jnp.float32,
    ).astype(jnp.bfloat16)
    bin_count = spectrum.shape[2]
    spectrum = spectrum.reshape(rows_here, 2, bin_count, local_rcv * shot_count)
    section_data = jnp.einsum(
        "akbx,xbfz->akfz",
        table_x,
        lax.all_to_all(spectrum, ("shot", "rep"), split_axis=2, concat_axis=0, tiled=True),
        preferred_element_type=jnp.float32,
    ).astype(jnp.bfloat16)
    all_rows, row_bins = (section_data.shape[1], section_data.shape[2])
    section_data = section_data.reshape(2, all_rows, row_bins, local_rcv, shot_count)
    section_data = lax.all_to_all(section_data, "rcv", split_axis=2, concat_axis=3, tiled=True)
    section_data = jnp.einsum(
        "ajby,bkfry->akfrj", table_y, section_data, preferred_element_type=jnp.float32
    ).astype(jnp.bfloat16)
    coefficients = jnp.einsum(
        "aqbr,bkfrj->akfqj", table_r, section_data, preferred_element_type=jnp.float32
    )
    shrunk = soft_limit(coefficients, threshold_row)
    section_data = jnp.einsum(
        "aqbr,akfqj->bkfrj", table_r, shrunk, preferred_element_type=jnp.float32
    ).astype(jnp.bfloat16)
    section_data = jnp.einsum(
        "ajby,akfrj->bkfry", table_y, section_data, preferred_element_type=jnp.float32
    ).astype(jnp.bfloat16)
    section_data = lax.all_to_all(section_data, "rcv", split_axis=3, concat_axis=2, tiled=True)
    section_data = section_data.reshape(2, all_rows, row_bins, local_rcv * shot_count)
    section_data = jnp.einsum(
        "akbx,akfz->bxfz", table_x, section_data, preferred_element_type=jnp.float32
    ).astype(jnp.bfloat16)
    result = jnp.einsum(
        "ckt,cxkz->xzt",
        table_time,
        lax.all_to_all(section_data, ("shot", "rep"), split_axis=1, concat_axis=2, tiled=True),
        preferred_element_type=jnp.float32,
    )
    return result.reshape(rows_here, local_rcv, shot_count, sample_count)


def body_by_rows(records, offsets, filter_index, signatures, thresholds):
    rows_here, shot_count = offsets.shape
    local_rcv, slab_len = records.shape
    slab_count = lax.axis_size(("shot", "rep"))
    rcv_count = lax.axis_size("rcv")
    tap_count = signatures.shape[1]
    sample_count = NT
    slab_blocks = slab_len // tap_count
    trace_blocks = sample_count // tap_count
    capacity = max(2, 2 * shot_count // slab_count)
    slot_count = slab_count * rows_here * capacity
    forward_tables = toeplitz_table(signatures, False)
    adjoint_tables = toeplitz_table(signatures, True)
    flat_index = filter_index.reshape(-1)
    forward_table = forward_tables[flat_index]
    adjoint_table = adjoint_tables[flat_index]
    owners = offsets // slab_len
    row_ids = jnp.arange(rows_here, dtype=jnp.int32)[:, None]
    slot_index = (
        owners * (rows_here * capacity) + row_ids * capacity + rank_in_row(owners)
    ).reshape(-1)
    every_offset = lax.all_gather(offsets, ("shot", "rep"), axis=0, tiled=True)
    every_owner = every_offset // slab_len
    every_start = every_offset // tap_count % slab_blocks
    every_rank = rank_in_row(every_owner)
    mine_mask = every_owner == lax.axis_index(("shot", "rep"))
    levels = jnp.arange(capacity, dtype=jnp.int32)
    picked = mine_mask[:, :, None] & (every_rank[:, :, None] == levels[None, None, :])
    table_in = jnp.sum(jnp.where(picked, every_start[:, :, None] + 1, 0), axis=1).reshape(-1)
    filled = table_in > 0
    block_steps = jnp.arange(trace_blocks, dtype=jnp.int32)
    target = jnp.where(
        filled[:, None],
        table_in[:, None] - 1 + block_steps[None, :],
        slab_blocks + trace_blocks - 1,
    )

    def correlate(record_field):
        record_low = (
            record_field.astype(jnp.bfloat16)
            .reshape(local_rcv, slab_blocks, tap_count)
            .transpose(1, 0, 2)
        )
        rim_blocks = from_behind(record_low[: trace_blocks - 1], ("shot", "rep"), -1)
        extended = jnp.concatenate(
            [record_low, rim_blocks, jnp.zeros((1, local_rcv, tap_count), jnp.bfloat16)], axis=0
        )
        windows = extended[target.reshape(-1)].reshape(
            slot_count, trace_blocks, local_rcv, tap_count
        )
        returned = to_shots(windows)
        traces = returned[slot_index]
        terms = apply_filter(traces, adjoint_table, True)
        terms = terms.reshape(rows_here, shot_count, trace_blocks, local_rcv, tap_count).transpose(
            0, 3, 1, 2, 4
        )
        return terms.reshape(rows_here, local_rcv, shot_count, sample_count)

    tables = (
        time_table(sample_count),
        shot_table(slab_count * rows_here),
        shot_table(shot_count),
        shot_table(local_rcv * rcv_count),
    )
    row_bins = sample_count // 2 // slab_count
    rcv_bins = row_bins // rcv_count
    bin_start = lax.axis_index(("shot", "rep")) * row_bins + lax.axis_index("rcv") * rcv_bins

    def threshold_for(level_index):
        return lax.dynamic_slice_in_dim(thresholds[level_index], bin_start, rcv_bins)

    model_field = shrink(correlate(records), threshold_for(0), tables)
    level_index = 1
    traces = model_field.astype(jnp.bfloat16).reshape(
        rows_here, local_rcv, shot_count, trace_blocks, tap_count
    )
    traces = traces.transpose(0, 2, 3, 1, 4).reshape(
        rows_here * shot_count, trace_blocks, local_rcv, tap_count
    )
    shots = apply_filter(traces, forward_table, False).astype(jnp.bfloat16)
    outgoing = (
        jnp.zeros((slot_count, trace_blocks, local_rcv, tap_count), jnp.bfloat16)
        .at[slot_index]
        .set(shots)
    )
    arrived = to_slabs(outgoing)
    slab_total = jnp.zeros((slab_blocks + trace_blocks, local_rcv, tap_count), jnp.float32)
    for block_step in range(trace_blocks):
        slab_total = slab_total.at[target[:, block_step]].add(
            arrived[:, block_step].astype(jnp.float32)
        )
    spill_over = slab_total[slab_blocks : slab_blocks + trace_blocks - 1]
    carried = from_behind(spill_over, ("shot", "rep"), 1)
    blended = slab_total[:slab_blocks].at[: trace_blocks - 1].add(carried)
    residual = records - blended.transpose(1, 0, 2).reshape(local_rcv, slab_len)
    model_field = shrink(model_field + correlate(residual), threshold_for(level_index), tables)
    return (model_field, residual)


def dot(left, right, left_dim=1, right_dim=0):
    return lax.dot_general(
        left, right, (((left_dim,), (right_dim,)), ((), ())), preferred_element_type=jnp.float32
    )


def fixed_time_table(count):
    samples = np.arange(count)
    bins = np.arange(count // 2)[:, None]
    angles = 2.0 * np.pi / count * (bins * samples[None, :] % count)
    scale = math.sqrt(2.0 / count)
    cosine = scale * np.cos(angles)
    sine = -scale * np.sin(angles)
    cosine[0] = math.sqrt(1.0 / count)
    sine[0] = math.sqrt(1.0 / count) * np.where(samples % 2 == 0, 1.0, -1.0)
    return np.stack([cosine, sine]).astype(jnp.bfloat16)


def fixed_shot_table(count):
    positions = np.arange(count)
    angles = 2.0 * np.pi / count * (positions[:, None] * positions[None, :] % count)
    cosine = np.cos(angles) / math.sqrt(count)
    sine = np.sin(angles) / math.sqrt(count)
    table = np.stack([np.stack([cosine, sine], 1), np.stack([-sine, cosine], 1)])
    return table.astype(jnp.bfloat16).astype(np.float32)


MESH = pl.DeviceIdType.MESH
AXES = ("shot", "rcv", "rep")


def neighbours(sizes):
    every = [(a, b, c) for a in range(sizes[0]) for b in range(sizes[1]) for c in range(sizes[2])]
    far = sizes[0] // 2
    return sorted(every[1:], key=lambda step: (abs(step[0] - far), -step[1], -step[2]))


def device_at(sizes, step):
    spot = [lax.rem(lax.axis_index(axis) + hop, size) for axis, hop, size in zip(AXES, step, sizes)]
    index = (spot[0] * sizes[1] + spot[1]) * sizes[2] + spot[2]
    return dict(zip(AXES, spot)), index


def build_taps(signature_ref, adjoint, out_ref):
    count, taps = signature_ref.shape
    row_index = lax.broadcasted_iota(jnp.int32, (taps, taps), 0)
    col_index = lax.broadcasted_iota(jnp.int32, (taps, taps), 1)
    values = signature_ref[...].astype(jnp.float32)
    for index in range(count):
        row = jnp.broadcast_to(values[index : index + 1, :], (taps, taps))
        turned = pltpu.roll(row, 0, 1, stride=1, stride_axis=0)
        zeros = jnp.zeros_like(turned)
        near = jnp.where(col_index >= row_index, turned, zeros)
        far = jnp.where(col_index < row_index, turned, zeros)
        near, far = (near.T, far.T) if adjoint else (near, far)
        where = slice(index * taps, (index + 1) * taps)
        out_ref[:taps, where] = near.astype(jnp.bfloat16)
        out_ref[taps:, where] = far.astype(jnp.bfloat16)


def pick_signature(every, picks_ref):
    slots, width = picks_ref.shape
    picks = jnp.concatenate([picks_ref[...]] * (every.shape[0] // slots), axis=0)
    chosen = every[:, :width]
    for index in range(1, every.shape[1] // width):
        chosen = jnp.where(picks == index, every[:, index * width : (index + 1) * width], chosen)
    return chosen


def correlate_line(line, padded, select_ref, blocks_ref, taps_ref, picks_ref, field_ref, traces_ref):
    slots, width = picks_ref.shape
    blocks = blocks_ref[pl.ds(pl.multiple_of(line * padded, 8), padded)].astype(jnp.bfloat16)
    window = dot(select_ref[...], blocks).astype(jnp.bfloat16)
    later = jnp.concatenate([window[slots:], jnp.zeros((slots, width), window.dtype)], axis=0)
    terms = pick_signature(dot(jnp.concatenate([window, later], axis=1), taps_ref[...]), picks_ref)
    steps = terms.shape[0] // slots
    terms = jnp.concatenate(
        [terms[step * slots : (step + 1) * slots] for step in range(steps)], axis=1
    )
    where = pl.ds(pl.multiple_of(line * slots, slots), slots)
    if field_ref is not None:
        terms = terms + field_ref[where]
    traces_ref[where] = terms.astype(jnp.bfloat16)


def blend_line(line, place_ref, field_ref, taps_ref, picks_ref):
    slots, width = picks_ref.shape
    trace = field_ref[pl.ds(pl.multiple_of(line * slots, slots), slots)].astype(jnp.bfloat16)
    steps = trace.shape[1] // width
    stacked = jnp.concatenate(
        [trace[:, step * width : (step + 1) * width] for step in range(steps)], axis=0
    )
    earlier = jnp.concatenate([jnp.zeros((slots, width), trace.dtype), stacked[:-slots]], axis=0)
    shots = pick_signature(dot(jnp.concatenate([stacked, earlier], axis=1), taps_ref[...]), picks_ref)
    return dot(place_ref[...], shots.astype(jnp.bfloat16))


def spectra_chunk(table, traces_ref, out_ref, lines, rcv, slots):
    parts, rows, lanes = out_ref.shape
    bins = rows // rcv
    half = parts * bins
    pack = max(1, 16 // bins)
    together = math.gcd(len(lines), 4)
    for first in range(lines[0], lines[-1] + 1, together):
        both = dot(table, traces_ref[first * slots : (first + together) * slots], 1, 1)
        for low in range(0, together, pack):
            pieces = []
            for line in range(low, low + pack):
                piece = both[:, line * slots : (line + 1) * slots]
                joined = jnp.concatenate([piece[:half], piece[half:]], axis=1)
                pieces.append(joined.reshape(parts, bins, lanes))
            out_ref[:, (first + low) * bins : (first + low + pack) * bins] = jnp.concatenate(
                pieces, axis=1
            ).astype(jnp.bfloat16)


def bins_chunk(place, halves, spectra_ref, go_ref, back_ref, cosine, sine, level, out_ref):
    _, rows, _ = spectra_ref.shape
    rcv_count, slab_count = place.shape
    joined = jnp.concatenate(
        [
            jnp.concatenate([spectra_ref[int(index)] for index in line], axis=1)
            for line in place
        ],
        axis=0,
    )
    section = dot(joined, go_ref[...]).astype(jnp.bfloat16)
    half = section.shape[1] // 2
    near = dot(cosine, section)
    far = dot(sine, section)
    real = near[:, :half] + far[:, half:]
    imag = near[:, half:] - far[:, :half]
    factor = 1.0 - level / jnp.maximum(jnp.sqrt(real * real + imag * imag), level)
    shrunk = jnp.concatenate([real * factor, imag * factor], axis=1).astype(jnp.bfloat16)
    near = dot(cosine, shrunk)
    far = dot(sine, shrunk)
    section = jnp.concatenate(
        [near[:, :half] - far[:, half:], far[:, :half] + near[:, half:]], axis=1
    ).astype(jnp.bfloat16)
    result = dot(section, back_ref[...], 1, 1).astype(jnp.bfloat16)
    width = result.shape[1] // slab_count
    for line in range(rcv_count):
        for slab in range(slab_count):
            piece = result[line * rows : (line + 1) * rows, slab * width : (slab + 1) * width]
            if halves == 2:
                piece = jnp.concatenate([piece[: rows // 2], piece[rows // 2 :]], axis=1)
            out_ref[int(place[line, slab])] = piece


def level_of(levels_ref, index, first, bins, copies_of):
    width = levels_ref.shape[1]
    lane = lax.broadcasted_iota(jnp.int32, (bins, width), 1)
    row = lax.broadcasted_iota(jnp.int32, (bins, width), 0)
    values = jnp.broadcast_to(levels_ref[index : index + 1, :], (bins, width))
    column = jnp.sum(jnp.where(lane == row + first, values, 0.0), axis=1, keepdims=True)
    return jnp.concatenate([column] * copies_of, axis=0)


def upright(spectra_ref, chunk, lines, bins, group_lanes):
    parts = spectra_ref.shape[1]
    pack = max(1, 16 // bins)
    count = group_lanes // 2
    pieces = []
    for low_line in range(lines[0], lines[-1] + 1, pack):
        block = spectra_ref[chunk, :, low_line * bins : (low_line + pack) * bins].astype(jnp.float32)
        for line in range(pack):
            turned = block[:, line * bins : (line + 1) * bins].reshape(parts * bins, -1).T
            turned = turned.astype(jnp.bfloat16)
            for low in range(0, turned.shape[0], group_lanes):
                pieces.append(
                    jnp.concatenate(
                        [turned[low : low + count], turned[low + count : low + 2 * count]], axis=1
                    )
                )
    return jnp.concatenate(pieces, axis=0)


CHUNKS = 2
SPANS = 2
UNROLL = 4


def whole_kernel(
    sizes,
    place,
    offsets_ref,
    filters_ref,
    signatures_ref,
    levels_ref,
    records_hbm,
    table_hbm,
    grid_hbm,
    cosine_hbm,
    sine_hbm,
    final_ref,
    left_ref,
    records_ref,
    table_ref,
    grid_ref,
    cosine_ref,
    sine_ref,
    row_ref,
    rows_ref,
    rim_ref,
    picks_ref,
    slot_table_ref,
    row_table_ref,
    adjoint_ref,
    forward_ref,
    select_ref,
    place_ref,
    traces_ref,
    field_ref,
    blocks_ref,
    rest_ref,
    head_ref,
    spill_ref,
    carried_ref,
    ahead_ref,
    sent_ref,
    got_ref,
    answer_ref,
    home_ref,
    reply_ref,
    raw_ref,
    other_raw_ref,
    other_rim_ref,
    other_blocks_ref,
    other_picks_ref,
    other_select_ref,
    other_traces_ref,
    other_sent_ref,
    load_sems,
    row_sends,
    row_recvs,
    go_sends,
    go_recvs,
    back_sends,
    back_recvs,
    rim_sends,
    rim_recvs,
    near_sends,
    near_recvs,
    raw_sems,
):
    slots, width = picks_ref.shape
    rcv, slab_len = records_ref.shape
    blocks = slab_len // width
    padded = blocks_ref.shape[0] // rcv
    chunks, _, samples = table_ref.shape
    steps = samples // width
    parts = place.size
    slab_count = place.shape[1]
    few = samples // 2 // parts // chunks
    quarter = rcv // 4
    early_spans = ((quarter, 2 * quarter), (2 * quarter, rcv))
    late_halves = ((0, 2 * quarter), (2 * quarter, rcv))
    late_spans = late_halves
    edge = head_ref.shape[1]
    all_rcv = rcv * place.shape[0]
    shot_count = offsets_ref.shape[1]
    row_count = slab_count
    capacity = slots // row_count
    wide = jnp.float32

    loads = [
        pltpu.make_async_copy(source, target, load_sems.at[number])
        for number, (source, target) in enumerate(
            (
                (records_hbm, records_ref),
                (table_hbm, table_ref),
                (grid_hbm, grid_ref),
                (cosine_hbm, cosine_ref),
                (sine_hbm, sine_ref),
            )
        )
    ]
    for load in loads:
        load.start()
    barrier = pltpu.get_barrier_semaphore()
    hops = neighbours(sizes)
    for hop in hops:
        pl.semaphore_signal(barrier, inc=1, device_id=device_at(sizes, hop)[0], device_id_type=MESH)
    mine = device_at(sizes, (0, 0, 0))[1]
    slab = lax.axis_index("shot") * sizes[2] + lax.axis_index("rep")
    last_slab = slab_count - 1

    def slab_device(shift):
        other = lax.rem(slab + shift + slab_count, slab_count)
        return {
            "shot": other // sizes[2],
            "rcv": lax.axis_index("rcv"),
            "rep": lax.rem(other, sizes[2]),
        }

    row_ref[...] = jnp.zeros_like(row_ref)
    row_ref[0:1, :shot_count] = offsets_ref[...]
    row_ref[1:2, :shot_count] = filters_ref[...]
    pl.semaphore_wait(barrier, len(hops))

    tile = row_ref.shape[0]
    here = pl.ds(pl.multiple_of(slab * tile, tile), tile)
    row_copies = []
    for hop in hops:
        if hop[1] == 0:
            number = len(row_copies)
            copy = pltpu.make_async_remote_copy(
                src_ref=row_ref,
                dst_ref=rows_ref.at[here],
                send_sem=row_sends.at[number],
                recv_sem=row_recvs.at[number],
                device_id=device_at(sizes, hop)[0],
                device_id_type=MESH,
            )
            copy.start()
            row_copies.append(copy)
    rows_ref[here] = row_ref[...]
    loads[0].wait()
    apart = slab_count // 2
    partner_slab = lax.rem(slab + apart, slab_count)
    partner = device_at(sizes, (sizes[0] // 2, 0, 0))[1]
    first_rim = pltpu.make_async_remote_copy(
        src_ref=records_ref.at[:, pl.ds(0, rim_ref.shape[1])],
        dst_ref=rim_ref,
        send_sem=rim_sends.at[SPANS, 0],
        recv_sem=rim_recvs.at[SPANS, 0],
        device_id=slab_device(-1),
        device_id_type=MESH,
    )
    partner_rim = pltpu.make_async_remote_copy(
        src_ref=records_ref.at[pl.ds(0, tile), pl.ds(0, rim_ref.shape[1])],
        dst_ref=other_rim_ref,
        send_sem=rim_sends.at[SPANS, 1],
        recv_sem=rim_recvs.at[SPANS, 1],
        device_id=slab_device(apart - 1),
        device_id_type=MESH,
    )

    @pl.when(slab > 0)
    def _():
        first_rim.start()
        partner_rim.start()

    for line in range(rcv):
        blocks_ref[line * padded + blocks : (line + 1) * padded] = jnp.zeros(
            (padded - blocks, width), wide
        )
    for block in range(blocks):
        blocks_ref[pl.ds(block, rcv, stride=padded), :] = records_ref[
            :, block * width : (block + 1) * width
        ]
    for line in range(quarter):
        raw_ref[line] = blocks_ref[line * padded : line * padded + blocks].astype(jnp.bfloat16)
    raw = pltpu.make_async_remote_copy(
        src_ref=raw_ref,
        dst_ref=other_raw_ref,
        send_sem=raw_sems.at[0],
        recv_sem=raw_sems.at[1],
        device_id=slab_device(apart),
        device_id_type=MESH,
    )
    raw.start()
    build_taps(signatures_ref, True, adjoint_ref)
    for copy in row_copies:
        copy.wait_recv()

    lane = lax.broadcasted_iota(jnp.int32, (row_count, width), 1)
    valid = lane < shot_count
    zero = jnp.zeros((row_count, width), jnp.int32)
    start_sample = jnp.where(valid, rows_ref[pl.ds(0, row_count, stride=tile), :], zero)
    signature = jnp.where(valid, rows_ref[pl.ds(1, row_count, stride=tile), :], zero)
    block_bits = width.bit_length() - 1
    slab_bits = slab_len.bit_length() - 1
    owner = lax.shift_right_logical(start_sample, slab_bits)
    rank = zero
    for step in range(1, shot_count):
        same = (pltpu.roll(owner, step, 1) == owner) & (lane >= step)
        rank = rank + same.astype(jnp.int32)
    key = jnp.where(valid, owner * capacity + rank + 1, zero)
    first_block = (lax.shift_right_logical(start_sample, block_bits) & (blocks - 1)).astype(wide)
    signature = signature.astype(wide)
    block_index = lax.broadcasted_iota(jnp.int32, (slots, padded), 1).astype(wide)

    def choose(owner_slab, into_picks_ref, into_select_ref):
        firsts, picks = [], []
        for level in range(capacity):
            taken = key == owner_slab * capacity + level + 1
            empty = jnp.zeros_like(first_block)
            firsts.append(
                jnp.sum(jnp.where(taken, first_block + 1.0, empty), axis=1, keepdims=True)
            )
            picks.append(jnp.sum(jnp.where(taken, signature, empty), axis=1, keepdims=True))
        firsts = jnp.broadcast_to(jnp.concatenate(firsts, axis=0), (slots, padded))
        firsts = jnp.where(firsts > 0.5, firsts - 1.0, -float(samples))
        into_picks_ref[...] = jnp.broadcast_to(jnp.concatenate(picks, axis=0), (slots, width))
        select = jnp.concatenate(
            [(block_index == firsts + float(step)).astype(wide) for step in range(steps)], axis=0
        )
        into_select_ref[...] = select.astype(jnp.bfloat16)
        return select

    select = choose(slab, picks_ref, select_ref)

    @pl.when(slab < last_slab)
    def _():
        first_rim.wait_recv()
        for step in range(rim_ref.shape[1] // width):
            blocks_ref[pl.ds(blocks + step, rcv, stride=padded), :] = rim_ref[
                :, step * width : (step + 1) * width
            ]

    loads[1].wait()

    def exchange(source, target, send_sems, recv_sems, low, rows):
        made = []
        where = pl.ds(low, rows)
        for number, hop in enumerate(hops):
            device, index = device_at(sizes, hop)
            copy = pltpu.make_async_remote_copy(
                src_ref=source.at[index, where],
                dst_ref=target.at[mine, where],
                send_sem=send_sems.at[number],
                recv_sem=recv_sems.at[number],
                device_id=device,
                device_id_type=MESH,
            )
            copy.start()
            made.append(copy)
        target[mine, where] = source[mine, where]
        return made

    def correlate_span(span, from_ref, model, one_select_ref, one_picks_ref, into_ref):
        def one(line, carry):
            correlate_line(
                line, padded, one_select_ref, from_ref, adjoint_ref, one_picks_ref, model, into_ref
            )
            return carry

        lax.fori_loop(span[0], span[1], one, 0, unroll=UNROLL)

    def span_spectra(span, chunk):
        spectra_chunk(table_ref[chunk], traces_ref, sent_ref.at[chunk], range(*span), rcv, slots)

    def span_exchange(number, span, chunk):
        return exchange(
            sent_ref.at[chunk],
            got_ref.at[chunk],
            go_sends.at[number, chunk],
            go_recvs.at[number, chunk],
            span[0] * few,
            (span[1] - span[0]) * few,
        )

    def send_span(number, span):
        made = []
        for chunk in range(chunks):
            span_spectra(span, chunk)
            made.append(span_exchange(number, span, chunk))
        return made

    def send_near(number, from_ref, one_select_ref, one_picks_ref, into_ref, out_ref, owner):
        span = (0, quarter)
        correlate_span(span, from_ref, None, one_select_ref, one_picks_ref, into_ref)
        where = pl.ds(0, quarter * few)
        depth, place_x, core = (lax.axis_index(axis) for axis in AXES)
        made = []
        for chunk in range(chunks):
            spectra_chunk(
                table_ref[chunk], into_ref, out_ref.at[chunk], range(*span), rcv, slots
            )
            copies = []
            for hop in range(1, 8):
                spot = (
                    depth + (hop // 4) * (1 - 2 * lax.rem(depth, 2)),
                    lax.rem(place_x + hop // 2 % 2, sizes[1]),
                    lax.rem(core + hop % 2, sizes[2]),
                )
                index = (spot[0] * sizes[1] + spot[1]) * sizes[2] + spot[2]
                copy = pltpu.make_async_remote_copy(
                    src_ref=out_ref.at[chunk, index, where],
                    dst_ref=got_ref.at[chunk, owner, where],
                    send_sem=near_sends.at[number, chunk, hop - 1],
                    recv_sem=near_recvs.at[number, chunk, hop - 1],
                    device_id=dict(zip(AXES, spot)),
                    device_id_type=MESH,
                )
                copy.start()
                copies.append(copy)
            got_ref[chunk, owner, where] = out_ref[chunk, mine, where]
            made.append(copies)
        return made

    def level_at(index, chunk):
        return level_of(levels_ref, index, (mine * chunks + chunk) * few, few, all_rcv)

    first_span, second_span = early_spans
    correlate_span(first_span, blocks_ref, None, select_ref, picks_ref, traces_ref)
    going = [send_span(0, first_span), []]
    correlate_span(second_span, blocks_ref, None, select_ref, picks_ref, traces_ref)
    for chunk in range(chunks):
        span_spectra(second_span, chunk)
        if chunk == 0:
            going[1].append(span_exchange(1, second_span, chunk))

    going.append(send_near(0, blocks_ref, select_ref, picks_ref, traces_ref, sent_ref, mine))
    choose(partner_slab, other_picks_ref, other_select_ref)
    raw.wait_recv()
    for line in range(quarter):
        other_blocks_ref[line * padded : line * padded + blocks] = other_raw_ref[line].astype(wide)
        other_blocks_ref[line * padded + blocks : (line + 1) * padded] = jnp.zeros(
            (padded - blocks, width), wide
        )

    @pl.when(partner_slab < last_slab)
    def _():
        partner_rim.wait_recv()
        for step in range(rim_ref.shape[1] // width):
            other_blocks_ref[pl.ds(blocks + step, quarter, stride=padded), :] = other_rim_ref[
                :quarter, step * width : (step + 1) * width
            ]

    going.append(
        send_near(
            1, other_blocks_ref, other_select_ref, other_picks_ref, other_traces_ref, other_sent_ref, partner
        )
    )
    for chunk in range(1, chunks):
        going[1].append(span_exchange(1, second_span, chunk))
    place_ref[...] = select.T.astype(jnp.bfloat16)
    build_taps(signatures_ref, False, forward_ref)
    repeated = key
    for shift in range(shot_count, width, shot_count):
        repeated = repeated + pltpu.roll(key, shift, 1)
    points = row_count * shot_count
    repeated = jnp.concatenate([repeated] * (points // width), axis=1)
    point = lax.broadcasted_iota(jnp.int32, (row_count, points), 1)
    row = lax.broadcasted_iota(jnp.int32, (row_count, points), 0)
    shot_bits = shot_count.bit_length() - 1
    repeated = jnp.where(lax.shift_right_logical(point, shot_bits) == row, repeated, 0)
    chosen = jnp.concatenate(
        [(repeated == number + 1).astype(wide) for number in range(slab_count * capacity)], axis=0
    ).astype(jnp.bfloat16)
    for load in loads[2:]:
        load.wait()
    for half in range(2):
        for number in range(row_count):
            low = (2 * number + half) * shot_count
            source = half * points + number * shot_count
            row_table_ref[low : low + shot_count] = grid_ref[source : source + shot_count]
        part = dot(chosen, grid_ref[half * points : (half + 1) * points]).astype(jnp.bfloat16)
        for number in range(slab_count):
            low = (2 * number + half) * slots
            slot_table_ref[low : low + slots] = part[number * slots : (number + 1) * slots]

    coming = {}

    def send_back(number, chunk):
        span = late_halves[number]
        coming[number, chunk] = exchange(
            answer_ref.at[chunk],
            home_ref.at[chunk],
            back_sends.at[number, chunk],
            back_recvs.at[number, chunk],
            span[0] * few,
            (span[1] - span[0]) * few,
        )

    for chunk in range(chunks):
        for made in going:
            for copy in made[chunk]:
                copy.wait_recv()
        bins_chunk(
            place, 1, got_ref.at[chunk], slot_table_ref, slot_table_ref, cosine_ref[...], sine_ref[...], level_at(0, chunk), answer_ref.at[chunk]
        )
        send_back(0, chunk)
    send_back(1, 0)
    for copy in row_copies:
        copy.wait_send()

    raw.wait_send()

    @pl.when(slab > 0)
    def _():
        first_rim.wait_send()
        partner_rim.wait_send()

    for made in going:
        for chunk in made:
            for copy in chunk:
                copy.wait_send()

    def halo(number):
        low, high = late_spans[number]
        where = pl.ds(low, high - low)
        onward = pltpu.make_async_remote_copy(
            src_ref=spill_ref.at[where],
            dst_ref=carried_ref.at[where],
            send_sem=rim_sends.at[number, 0],
            recv_sem=rim_recvs.at[number, 0],
            device_id=slab_device(1),
            device_id_type=MESH,
        )
        backward = pltpu.make_async_remote_copy(
            src_ref=head_ref.at[where],
            dst_ref=ahead_ref.at[where],
            send_sem=rim_sends.at[number, 1],
            recv_sem=rim_recvs.at[number, 1],
            device_id=slab_device(-1),
            device_id_type=MESH,
        )
        return onward, backward

    def subtract(number):
        low, high = late_spans[number]
        if True:
            for chunk in range(chunks):
                for copy in coming[number, chunk]:
                    copy.wait_recv()
        together = math.gcd(high - low, 4)
        for first in range(low, high, together):
            lines = range(first, first + together)
            field_ref[first * slots : (first + together) * slots] = sum(
                dot(upright(home_ref, chunk, lines, few, 2 * slots), table_ref[chunk])
                for chunk in range(chunks)
            )

        def one(line, carry):
            blended = blend_line(line, place_ref, field_ref, forward_ref, picks_ref)
            start = pl.multiple_of(line * padded, 8)
            left = blocks_ref[pl.ds(start, blocks)] - blended[:blocks]
            rest_ref[pl.ds(start, blocks)] = left
            rest_ref[pl.ds(start + blocks, padded - blocks)] = jnp.zeros(
                (padded - blocks, width), wide
            )
            head_ref[line] = left[:edge]
            spill_ref[line] = blended[blocks : blocks + edge]
            return carry

        lax.fori_loop(low, high, one, 0, unroll=UNROLL)
        onward, backward = halo(number)

        @pl.when(slab < last_slab)
        def _():
            onward.start()

        @pl.when(slab > 0)
        def _():
            backward.start()

    def correlate_rest(number):
        low, high = late_spans[number]
        onward, backward = halo(number)

        @pl.when(slab > 0)
        def _():
            onward.wait_recv()
            for line in range(low, high):
                here = pl.ds(line * padded, edge)
                rest_ref[here] = rest_ref[here] - carried_ref[line]

        @pl.when(slab < last_slab)
        def _():
            backward.wait_recv()
            for line in range(low, high):
                rest_ref[pl.ds(line * padded + blocks, edge)] = ahead_ref[line] - spill_ref[line]
            onward.wait_send()

        @pl.when(slab > 0)
        def _():
            backward.wait_send()

        correlate_span((low, high), rest_ref, field_ref, select_ref, picks_ref, traces_ref)

    again = [[], []]
    subtract(0)
    for chunk in range(1, chunks):
        send_back(1, chunk)
    correlate_rest(0)
    span_spectra(late_halves[0], 0)
    again[0].append(span_exchange(0, late_halves[0], 0))
    for chunk in range(1, chunks):
        span_spectra(late_halves[0], chunk)
    subtract(1)
    for chunk in range(1, chunks):
        again[0].append(span_exchange(0, late_halves[0], chunk))
    correlate_rest(1)
    again[1] = send_span(1, late_halves[1])

    for block in range(blocks):
        left_ref[:, block * width : (block + 1) * width] = rest_ref[
            pl.ds(block, rcv, stride=padded), :
        ]
    for made in coming.values():
        for copy in made:
            copy.wait_send()
    final = []
    for chunk in range(chunks):
        for made in again:
            for copy in made[chunk]:
                copy.wait_recv()
        bins_chunk(
            place, 2, got_ref.at[chunk], slot_table_ref, row_table_ref, cosine_ref[...], sine_ref[...], level_at(1, chunk), reply_ref.at[chunk]
        )
        final.append(
            exchange(
                reply_ref.at[chunk], final_ref.at[chunk], back_sends.at[0, chunk], back_recvs.at[0, chunk], 0, reply_ref.shape[2]
            )
        )
    for made in again:
        for chunk in made:
            for copy in chunk:
                copy.wait_send()
    for made in final:
        for copy in made:
            copy.wait()


def finish_kernel(bins, spectra_ref, left_ref, table_ref, model_ref, out_ref, sem):
    chunks = spectra_ref.shape[0]
    groups, together, count, _ = model_ref.shape
    step = pl.program_id(0)
    copy = pltpu.make_async_copy(left_ref, out_ref, sem)

    @pl.when(step == 0)
    def _():
        copy.start()

    fields = sum(
        dot(upright(spectra_ref, chunk, range(together), bins, 2 * count), table_ref[chunk])
        for chunk in range(chunks)
    )
    for line in range(together):
        for group in range(groups):
            low = (line * groups + group) * count
            model_ref[group, line] = fields[low : low + count]

    @pl.when(step == pl.num_programs(0) - 1)
    def _():
        copy.wait()


def finish(spectra, left, table, groups, rcv):
    chunks, parts, rows, lanes = spectra.shape
    samples = table.shape[2]
    bins = rows // rcv
    count = lanes // 2 // groups
    together = math.gcd(rcv, 4)
    whole = pl.BlockSpec(memory_space=pltpu.VMEM)
    return pl.pallas_call(
        functools.partial(finish_kernel, bins),
        grid=(rcv // together,),
        out_shape=(
            jax.ShapeDtypeStruct((groups, rcv, count, samples), jnp.float32),
            jax.ShapeDtypeStruct(left.shape, jnp.float32),
        ),
        in_specs=[
            pl.BlockSpec((chunks, parts, together * bins, lanes), lambda i: (0, 0, i, 0)),
            whole,
            whole,
        ],
        out_specs=(
            pl.BlockSpec((groups, together, count, samples), lambda i: (0, i, 0, 0)),
            pl.BlockSpec(memory_space=pl.ANY),
        ),
        scratch_shapes=[pltpu.SemaphoreType.DMA],
        compiler_params=pltpu.CompilerParams(vmem_limit_bytes=16 * 2**20),
    )(spectra, left, table)


def body_by_slots(records, offsets, filter_index, signatures, thresholds):
    rows_here, shot_count = offsets.shape
    local_rcv, slab_len = records.shape
    slab_count = lax.axis_size(("shot", "rep"))
    rep_count = lax.axis_size("rep")
    rcv_count = lax.axis_size("rcv")
    sizes = tuple(lax.axis_size(axis) for axis in AXES)
    parts = slab_count * rcv_count
    tap_count = signatures.shape[1]
    slab_blocks = slab_len // tap_count
    steps = NT // tap_count
    capacity = max(2, 2 * shot_count // slab_count)
    row_count = rows_here * slab_count
    slots = row_count * capacity
    bins = NT // 2 // parts
    chunks = CHUNKS
    few = bins // chunks
    place = np.array(
        [
            [((slab // rep_count) * rcv_count + line) * rep_count + slab % rep_count for slab in range(slab_count)]
            for line in range(rcv_count)
        ]
    )

    time_table_fixed = fixed_time_table(NT).reshape(2, parts, chunks, few, NT)
    time_table_fixed = jnp.asarray(
        np.ascontiguousarray(time_table_fixed.transpose(2, 0, 1, 3, 4)).reshape(chunks, NT // chunks, NT)
    )
    table_x, table_y, table_r = (
        fixed_shot_table(count) for count in (row_count, shot_count, local_rcv * rcv_count)
    )
    grid_table = np.einsum("ajby,bkcx->cxyakj", table_y, table_x).astype(jnp.bfloat16)
    points = 2 * row_count * shot_count
    grid_table = jnp.asarray(grid_table.reshape(points, points))
    same = np.eye(few, dtype=np.float32)
    cosine = jnp.asarray(np.kron(table_r[0, :, 0], same).astype(jnp.bfloat16))
    sine = jnp.asarray(np.kron(table_r[0, :, 1], same).astype(jnp.bfloat16))

    edge = 8
    padded = slab_blocks + 2 * edge
    vmem = pl.BlockSpec(memory_space=pltpu.VMEM)
    anywhere = pl.BlockSpec(memory_space=pl.ANY)
    rows = local_rcv * few
    table_width = tap_count * signatures.shape[0]
    low, wide = jnp.bfloat16, jnp.float32
    big = (records, time_table_fixed, grid_table, cosine, sine)
    spectra, residual = pl.pallas_call(
        functools.partial(whole_kernel, sizes, place),
        out_shape=(
            pltpu.VMEM((chunks, parts, rows // 2, 4 * shot_count), low),
            pltpu.VMEM(records.shape, wide),
        ),
        in_specs=[vmem] * 4 + [anywhere] * len(big),
        out_specs=(vmem, vmem),
        scratch_shapes=[pltpu.VMEM(array.shape, array.dtype) for array in big]
        + [
            pltpu.VMEM((edge, tap_count), jnp.int32),
            pltpu.VMEM((slab_count * edge, tap_count), jnp.int32),
            pltpu.VMEM((local_rcv, (steps - 1) * tap_count), wide),
            pltpu.VMEM((slots, tap_count), wide),
            pltpu.VMEM((slab_count * 2 * slots, points), low),
            pltpu.VMEM((points, points), low),
            pltpu.VMEM((2 * tap_count, table_width), low),
            pltpu.VMEM((2 * tap_count, table_width), low),
            pltpu.VMEM((slots * steps, padded), low),
            pltpu.VMEM((padded, slots * steps), low),
            pltpu.VMEM((local_rcv * slots, NT), low),
            pltpu.VMEM((local_rcv * slots, NT), wide),
            pltpu.VMEM((local_rcv * padded, tap_count), wide),
            pltpu.VMEM((local_rcv * padded, tap_count), wide),
        ]
        + [pltpu.VMEM((local_rcv, edge, tap_count), wide)] * 4
        + [pltpu.VMEM((chunks, parts, rows, 2 * slots), low)] * 4
        + [
            pltpu.VMEM((chunks, parts, rows // 2, 4 * shot_count), low),
            pltpu.VMEM((local_rcv // 4, slab_blocks, tap_count), low),
            pltpu.VMEM((local_rcv // 4, slab_blocks, tap_count), low),
            pltpu.VMEM((edge, (steps - 1) * tap_count), wide),
            pltpu.VMEM((local_rcv // 4 * padded, tap_count), wide),
            pltpu.VMEM((slots, tap_count), wide),
            pltpu.VMEM((slots * steps, padded), low),
            pltpu.VMEM((local_rcv // 4 * slots, NT), low),
            pltpu.VMEM((chunks, parts, rows, 2 * slots), low),
        ]
        + [pltpu.SemaphoreType.DMA((len(big),))]
        + [pltpu.SemaphoreType.DMA((slab_count - 1,))] * 2
        + [pltpu.SemaphoreType.DMA((2, chunks, parts - 1))] * 4
        + [pltpu.SemaphoreType.DMA((SPANS + 1, 2))] * 2
        + [pltpu.SemaphoreType.DMA((2, chunks, parts // 2 - 1))] * 2
        + [pltpu.SemaphoreType.DMA((2,))],
        compiler_params=pltpu.CompilerParams(
            collective_id=0, has_side_effects=True, vmem_limit_bytes=60 * 2**20
        ),
    )(offsets, filter_index, signatures, thresholds, *big)
    model, residual = finish(spectra, residual, time_table_fixed, 2, local_rcv // 2)
    return (model.reshape(rows_here, local_rcv, shot_count, NT), residual)


def body(records, offsets, filter_index, signatures, thresholds):
    rows_here, shot_count = offsets.shape
    slab_count = lax.axis_size(("shot", "rep"))
    parts = slab_count * lax.axis_size("rcv")
    slots = rows_here * slab_count * max(2, 2 * shot_count // slab_count)
    table_rows = 2 * rows_here * slab_count * shot_count
    fits = table_rows <= 1024 and rows_here == 1 and slots == 64 and 4 * shot_count == 128
    fits = fits and records.shape[0] == 16 and NT // 2 // parts == 16
    slab_len, tap_count = records.shape[1], signatures.shape[1]
    fits = fits and tap_count == 128 and slab_len & (slab_len - 1) == 0
    fits = fits and tuple(lax.axis_size(axis) for axis in AXES) == (4, 2, 2)
    run = body_by_slots if fits else body_by_rows
    return run(records, offsets, filter_index, signatures, thresholds)


def solution(mesh):
    in_specs = (
        P(("groups", "rcv"), ("shot", "rep")),
        P(("groups", "shot", "rep"), None),
        P(("groups", "shot", "rep"), None),
        P(),
        P(),
    )
    out_specs = (
        P(("groups", "shot", "rep"), "rcv", None, None),
        P(("groups", "rcv"), ("shot", "rep")),
    )
    return jax.shard_map(body, mesh=mesh, in_specs=in_specs, out_specs=out_specs, check_vma=False)
```

```python
import functools
import math

import jax
import jax.numpy as jnp
import numpy as np
from jax import lax
from jax.experimental import pallas as pl
from jax.experimental.pallas import tpu as pltpu
from jax.sharding import PartitionSpec as P

NT = 512


def from_behind(value, axis, steps):
    count = lax.axis_size(axis)
    first, last = (max(0, -steps), min(count, count - steps))
    return lax.ppermute(value, axis, [(source, source + steps) for source in range(first, last)])


def time_table(count):
    samples = jnp.arange(count)
    bin_index = jnp.arange(count // 2)[:, None]
    angles = 2.0 * math.pi / count * (bin_index * samples[None, :] % count).astype(jnp.float32)
    parity = jnp.where(samples % 2 == 0, 1.0, -1.0).astype(jnp.float32)
    cosine = jnp.where(bin_index == 0, math.sqrt(1.0 / count), math.sqrt(2.0 / count)) * jnp.cos(
        angles
    )
    sine_part = jnp.where(
        bin_index == 0,
        math.sqrt(1.0 / count) * parity[None, :],
        -math.sqrt(2.0 / count) * jnp.sin(angles),
    )
    return jnp.stack([cosine, sine_part]).astype(jnp.bfloat16)


def shot_table(count):
    positions = jnp.arange(count)
    angles = (
        2.0
        * math.pi
        / count
        * (positions[:, None] * positions[None, :] % count).astype(jnp.float32)
    )
    scaling = 1.0 / math.sqrt(count)
    cosine = scaling * jnp.cos(angles)
    sine_part = scaling * jnp.sin(angles)
    upper_half = jnp.stack([cosine, sine_part], axis=1)
    lower_half = jnp.stack([-sine_part, cosine], axis=1)
    return jnp.stack([upper_half, lower_half]).astype(jnp.bfloat16)


def toeplitz_kernel(adjoint, taps_ref, out_ref):
    tap_count = taps_ref.shape[1]
    row_index = lax.broadcasted_iota(jnp.int32, (tap_count, tap_count), 0)
    col_index = lax.broadcasted_iota(jnp.int32, (tap_count, tap_count), 1)
    taps = taps_ref[...].astype(jnp.float32)
    for index in range(taps_ref.shape[0]):
        row = jnp.broadcast_to(taps[index : index + 1, :], (tap_count, tap_count))
        turned = pltpu.roll(row, 0, 1, stride=1, stride_axis=0)
        zeros = jnp.zeros_like(turned)
        near = jnp.where(col_index >= row_index, turned, zeros)
        far = jnp.where(col_index < row_index, turned, zeros)
        near, far = (near.T, far.T) if adjoint else (near, far)
        out_ref[index, :tap_count, :] = near.astype(jnp.bfloat16)
        out_ref[index, tap_count:, :] = far.astype(jnp.bfloat16)


def toeplitz_table(signatures, adjoint):
    count, tap_count = signatures.shape
    return pl.pallas_call(
        functools.partial(toeplitz_kernel, adjoint),
        out_shape=jax.ShapeDtypeStruct((count, 2 * tap_count, tap_count), jnp.bfloat16),
        in_specs=[pl.BlockSpec(memory_space=pltpu.VMEM)],
        out_specs=pl.BlockSpec(memory_space=pltpu.VMEM),
    )(signatures)


def apply_filter(traces, table, adjoint):
    empty = jnp.zeros_like(traces[:, :1])
    if adjoint:
        other = jnp.concatenate([traces[:, 1:], empty], axis=1)
    else:
        other = jnp.concatenate([empty, traces[:, :-1]], axis=1)
    return jnp.einsum(
        "sbrp,spq->sbrq",
        jnp.concatenate([traces, other], axis=3),
        table,
        preferred_element_type=jnp.float32,
    )


def rank_in_row(owners):
    shot_count = owners.shape[1]
    same_owner = owners[:, :, None] == owners[:, None, :]
    earlier = jnp.arange(shot_count)[None, :] < jnp.arange(shot_count)[:, None]
    return jnp.sum(same_owner & earlier[None], axis=2)


def to_slabs(payload):
    return lax.all_to_all(payload, ("shot", "rep"), split_axis=0, concat_axis=0, tiled=True)


def to_shots(payload):
    return lax.all_to_all(payload, ("shot", "rep"), split_axis=0, concat_axis=0, tiled=True)


def soft_limit(coefficients, threshold_row):
    magnitude = jnp.sqrt(coefficients[0] * coefficients[0] + coefficients[1] * coefficients[1])
    threshold_view = threshold_row[None, :, None, None]
    factor = 1.0 - threshold_view / jnp.maximum(magnitude, threshold_view)
    return (coefficients * factor[None]).astype(jnp.bfloat16)


def shrink(field_data, threshold_row, tables):
    table_time, table_x, table_y, table_r = tables
    rows_here, local_rcv, shot_count, sample_count = field_data.shape
    spectrum = jnp.einsum(
        "ckt,xryt->xckry",
        table_time,
        field_data.astype(jnp.bfloat16),
        preferred_element_type=jnp.float32,
    ).astype(jnp.bfloat16)
    bin_count = spectrum.shape[2]
    spectrum = spectrum.reshape(rows_here, 2, bin_count, local_rcv * shot_count)
    section_data = jnp.einsum(
        "akbx,xbfz->akfz",
        table_x,
        lax.all_to_all(spectrum, ("shot", "rep"), split_axis=2, concat_axis=0, tiled=True),
        preferred_element_type=jnp.float32,
    ).astype(jnp.bfloat16)
    all_rows, row_bins = (section_data.shape[1], section_data.shape[2])
    section_data = section_data.reshape(2, all_rows, row_bins, local_rcv, shot_count)
    section_data = lax.all_to_all(section_data, "rcv", split_axis=2, concat_axis=3, tiled=True)
    section_data = jnp.einsum(
        "ajby,bkfry->akfrj", table_y, section_data, preferred_element_type=jnp.float32
    ).astype(jnp.bfloat16)
    coefficients = jnp.einsum(
        "aqbr,bkfrj->akfqj", table_r, section_data, preferred_element_type=jnp.float32
    )
    shrunk = soft_limit(coefficients, threshold_row)
    section_data = jnp.einsum(
        "aqbr,akfqj->bkfrj", table_r, shrunk, preferred_element_type=jnp.float32
    ).astype(jnp.bfloat16)
    section_data = jnp.einsum(
        "ajby,akfrj->bkfry", table_y, section_data, preferred_element_type=jnp.float32
    ).astype(jnp.bfloat16)
    section_data = lax.all_to_all(section_data, "rcv", split_axis=3, concat_axis=2, tiled=True)
    section_data = section_data.reshape(2, all_rows, row_bins, local_rcv * shot_count)
    section_data = jnp.einsum(
        "akbx,akfz->bxfz", table_x, section_data, preferred_element_type=jnp.float32
    ).astype(jnp.bfloat16)
    result = jnp.einsum(
        "ckt,cxkz->xzt",
        table_time,
        lax.all_to_all(section_data, ("shot", "rep"), split_axis=1, concat_axis=2, tiled=True),
        preferred_element_type=jnp.float32,
    )
    return result.reshape(rows_here, local_rcv, shot_count, sample_count)


def body_by_rows(records, offsets, filter_index, signatures, thresholds):
    rows_here, shot_count = offsets.shape
    local_rcv, slab_len = records.shape
    slab_count = lax.axis_size(("shot", "rep"))
    rcv_count = lax.axis_size("rcv")
    tap_count = signatures.shape[1]
    sample_count = NT
    slab_blocks = slab_len // tap_count
    trace_blocks = sample_count // tap_count
    capacity = max(2, 2 * shot_count // slab_count)
    slot_count = slab_count * rows_here * capacity
    forward_tables = toeplitz_table(signatures, False)
    adjoint_tables = toeplitz_table(signatures, True)
    flat_index = filter_index.reshape(-1)
    forward_table = forward_tables[flat_index]
    adjoint_table = adjoint_tables[flat_index]
    owners = offsets // slab_len
    row_ids = jnp.arange(rows_here, dtype=jnp.int32)[:, None]
    slot_index = (
        owners * (rows_here * capacity) + row_ids * capacity + rank_in_row(owners)
    ).reshape(-1)
    every_offset = lax.all_gather(offsets, ("shot", "rep"), axis=0, tiled=True)
    every_owner = every_offset // slab_len
    every_start = every_offset // tap_count % slab_blocks
    every_rank = rank_in_row(every_owner)
    mine_mask = every_owner == lax.axis_index(("shot", "rep"))
    levels = jnp.arange(capacity, dtype=jnp.int32)
    picked = mine_mask[:, :, None] & (every_rank[:, :, None] == levels[None, None, :])
    table_in = jnp.sum(jnp.where(picked, every_start[:, :, None] + 1, 0), axis=1).reshape(-1)
    filled = table_in > 0
    block_steps = jnp.arange(trace_blocks, dtype=jnp.int32)
    target = jnp.where(
        filled[:, None],
        table_in[:, None] - 1 + block_steps[None, :],
        slab_blocks + trace_blocks - 1,
    )

    def correlate(record_field):
        record_low = (
            record_field.astype(jnp.bfloat16)
            .reshape(local_rcv, slab_blocks, tap_count)
            .transpose(1, 0, 2)
        )
        rim_blocks = from_behind(record_low[: trace_blocks - 1], ("shot", "rep"), -1)
        extended = jnp.concatenate(
            [record_low, rim_blocks, jnp.zeros((1, local_rcv, tap_count), jnp.bfloat16)], axis=0
        )
        windows = extended[target.reshape(-1)].reshape(
            slot_count, trace_blocks, local_rcv, tap_count
        )
        returned = to_shots(windows)
        traces = returned[slot_index]
        terms = apply_filter(traces, adjoint_table, True)
        terms = terms.reshape(rows_here, shot_count, trace_blocks, local_rcv, tap_count).transpose(
            0, 3, 1, 2, 4
        )
        return terms.reshape(rows_here, local_rcv, shot_count, sample_count)

    tables = (
        time_table(sample_count),
        shot_table(slab_count * rows_here),
        shot_table(shot_count),
        shot_table(local_rcv * rcv_count),
    )
    row_bins = sample_count // 2 // slab_count
    rcv_bins = row_bins // rcv_count
    bin_start = lax.axis_index(("shot", "rep")) * row_bins + lax.axis_index("rcv") * rcv_bins

    def threshold_for(level_index):
        return lax.dynamic_slice_in_dim(thresholds[level_index], bin_start, rcv_bins)

    model_field = shrink(correlate(records), threshold_for(0), tables)
    level_index = 1
    traces = model_field.astype(jnp.bfloat16).reshape(
        rows_here, local_rcv, shot_count, trace_blocks, tap_count
    )
    traces = traces.transpose(0, 2, 3, 1, 4).reshape(
        rows_here * shot_count, trace_blocks, local_rcv, tap_count
    )
    shots = apply_filter(traces, forward_table, False).astype(jnp.bfloat16)
    outgoing = (
        jnp.zeros((slot_count, trace_blocks, local_rcv, tap_count), jnp.bfloat16)
        .at[slot_index]
        .set(shots)
    )
    arrived = to_slabs(outgoing)
    slab_total = jnp.zeros((slab_blocks + trace_blocks, local_rcv, tap_count), jnp.float32)
    for block_step in range(trace_blocks):
        slab_total = slab_total.at[target[:, block_step]].add(
            arrived[:, block_step].astype(jnp.float32)
        )
    spill_over = slab_total[slab_blocks : slab_blocks + trace_blocks - 1]
    carried = from_behind(spill_over, ("shot", "rep"), 1)
    blended = slab_total[:slab_blocks].at[: trace_blocks - 1].add(carried)
    residual = records - blended.transpose(1, 0, 2).reshape(local_rcv, slab_len)
    model_field = shrink(model_field + correlate(residual), threshold_for(level_index), tables)
    return (model_field, residual)


def dot(left, right, left_dim=1, right_dim=0):
    return lax.dot_general(
        left, right, (((left_dim,), (right_dim,)), ((), ())), preferred_element_type=jnp.float32
    )


def fixed_time_table(count):
    samples = np.arange(count)
    bins = np.arange(count // 2)[:, None]
    angles = 2.0 * np.pi / count * (bins * samples[None, :] % count)
    scale = math.sqrt(2.0 / count)
    cosine = scale * np.cos(angles)
    sine = -scale * np.sin(angles)
    cosine[0] = math.sqrt(1.0 / count)
    sine[0] = math.sqrt(1.0 / count) * np.where(samples % 2 == 0, 1.0, -1.0)
    return np.stack([cosine, sine]).astype(jnp.bfloat16)


def fixed_shot_table(count):
    positions = np.arange(count)
    angles = 2.0 * np.pi / count * (positions[:, None] * positions[None, :] % count)
    cosine = np.cos(angles) / math.sqrt(count)
    sine = np.sin(angles) / math.sqrt(count)
    table = np.stack([np.stack([cosine, sine], 1), np.stack([-sine, cosine], 1)])
    return table.astype(jnp.bfloat16).astype(np.float32)


MESH = pl.DeviceIdType.MESH
AXES = ("shot", "rcv", "rep")


def neighbours(sizes):
    every = [(a, b, c) for a in range(sizes[0]) for b in range(sizes[1]) for c in range(sizes[2])]
    far = sizes[0] // 2
    return sorted(every[1:], key=lambda step: (abs(step[0] - far), -step[1], -step[2]))


def device_at(sizes, step):
    spot = [lax.rem(lax.axis_index(axis) + hop, size) for axis, hop, size in zip(AXES, step, sizes)]
    index = (spot[0] * sizes[1] + spot[1]) * sizes[2] + spot[2]
    return dict(zip(AXES, spot)), index


def build_taps(signature_ref, adjoint, out_ref):
    count, taps = signature_ref.shape
    row_index = lax.broadcasted_iota(jnp.int32, (taps, taps), 0)
    col_index = lax.broadcasted_iota(jnp.int32, (taps, taps), 1)
    values = signature_ref[...].astype(jnp.float32)
    for index in range(count):
        row = jnp.broadcast_to(values[index : index + 1, :], (taps, taps))
        turned = pltpu.roll(row, 0, 1, stride=1, stride_axis=0)
        zeros = jnp.zeros_like(turned)
        near = jnp.where(col_index >= row_index, turned, zeros)
        far = jnp.where(col_index < row_index, turned, zeros)
        near, far = (near.T, far.T) if adjoint else (near, far)
        where = slice(index * taps, (index + 1) * taps)
        out_ref[:taps, where] = near.astype(jnp.bfloat16)
        out_ref[taps:, where] = far.astype(jnp.bfloat16)


def pick_signature(every, picks_ref):
    slots, width = picks_ref.shape
    picks = jnp.concatenate([picks_ref[...]] * (every.shape[0] // slots), axis=0)
    chosen = every[:, :width]
    for index in range(1, every.shape[1] // width):
        chosen = jnp.where(picks == index, every[:, index * width : (index + 1) * width], chosen)
    return chosen


def correlate_line(line, padded, select_ref, blocks_ref, taps_ref, picks_ref, field_ref, traces_ref):
    slots, width = picks_ref.shape
    blocks = blocks_ref[pl.ds(pl.multiple_of(line * padded, 8), padded)].astype(jnp.bfloat16)
    window = dot(select_ref[...], blocks).astype(jnp.bfloat16)
    later = jnp.concatenate([window[slots:], jnp.zeros((slots, width), window.dtype)], axis=0)
    terms = pick_signature(dot(jnp.concatenate([window, later], axis=1), taps_ref[...]), picks_ref)
    steps = terms.shape[0] // slots
    terms = jnp.concatenate(
        [terms[step * slots : (step + 1) * slots] for step in range(steps)], axis=1
    )
    where = pl.ds(pl.multiple_of(line * slots, slots), slots)
    if field_ref is not None:
        terms = terms + field_ref[where]
    traces_ref[where] = terms.astype(jnp.bfloat16)


def blend_line(line, place_ref, field_ref, taps_ref, picks_ref):
    slots, width = picks_ref.shape
    trace = field_ref[pl.ds(pl.multiple_of(line * slots, slots), slots)].astype(jnp.bfloat16)
    steps = trace.shape[1] // width
    stacked = jnp.concatenate(
        [trace[:, step * width : (step + 1) * width] for step in range(steps)], axis=0
    )
    earlier = jnp.concatenate([jnp.zeros((slots, width), trace.dtype), stacked[:-slots]], axis=0)
    shots = pick_signature(dot(jnp.concatenate([stacked, earlier], axis=1), taps_ref[...]), picks_ref)
    return dot(place_ref[...], shots.astype(jnp.bfloat16))


def spectra_chunk(table, traces_ref, out_ref, lines, rcv, slots):
    parts, rows, lanes = out_ref.shape
    bins = rows // rcv
    half = parts * bins
    pack = max(1, 16 // bins)
    together = math.gcd(len(lines), 4)
    for first in range(lines[0], lines[-1] + 1, together):
        both = dot(table, traces_ref[first * slots : (first + together) * slots], 1, 1)
        for low in range(0, together, pack):
            pieces = []
            for line in range(low, low + pack):
                piece = both[:, line * slots : (line + 1) * slots]
                joined = jnp.concatenate([piece[:half], piece[half:]], axis=1)
                pieces.append(joined.reshape(parts, bins, lanes))
            out_ref[:, (first + low) * bins : (first + low + pack) * bins] = jnp.concatenate(
                pieces, axis=1
            ).astype(jnp.bfloat16)


def bins_chunk(place, halves, spectra_ref, go_ref, back_ref, cosine, sine, level, out_ref):
    _, rows, _ = spectra_ref.shape
    rcv_count, slab_count = place.shape
    joined = jnp.concatenate(
        [
            jnp.concatenate([spectra_ref[int(index)] for index in line], axis=1)
            for line in place
        ],
        axis=0,
    )
    section = dot(joined, go_ref[...]).astype(jnp.bfloat16)
    half = section.shape[1] // 2
    near = dot(cosine, section)
    far = dot(sine, section)
    real = near[:, :half] + far[:, half:]
    imag = near[:, half:] - far[:, :half]
    factor = 1.0 - level / jnp.maximum(jnp.sqrt(real * real + imag * imag), level)
    shrunk = jnp.concatenate([real * factor, imag * factor], axis=1).astype(jnp.bfloat16)
    near = dot(cosine, shrunk)
    far = dot(sine, shrunk)
    section = jnp.concatenate(
        [near[:, :half] - far[:, half:], far[:, :half] + near[:, half:]], axis=1
    ).astype(jnp.bfloat16)
    result = dot(section, back_ref[...], 1, 1).astype(jnp.bfloat16)
    width = result.shape[1] // slab_count
    for line in range(rcv_count):
        for slab in range(slab_count):
            piece = result[line * rows : (line + 1) * rows, slab * width : (slab + 1) * width]
            if halves == 2:
                piece = jnp.concatenate([piece[: rows // 2], piece[rows // 2 :]], axis=1)
            out_ref[int(place[line, slab])] = piece


def level_of(levels_ref, index, first, bins, copies_of):
    width = levels_ref.shape[1]
    lane = lax.broadcasted_iota(jnp.int32, (bins, width), 1)
    row = lax.broadcasted_iota(jnp.int32, (bins, width), 0)
    values = jnp.broadcast_to(levels_ref[index : index + 1, :], (bins, width))
    column = jnp.sum(jnp.where(lane == row + first, values, 0.0), axis=1, keepdims=True)
    return jnp.concatenate([column] * copies_of, axis=0)


def upright(spectra_ref, chunk, lines, bins, group_lanes):
    parts = spectra_ref.shape[1]
    pack = max(1, 16 // bins)
    count = group_lanes // 2
    pieces = []
    for low_line in range(lines[0], lines[-1] + 1, pack):
        block = spectra_ref[chunk, :, low_line * bins : (low_line + pack) * bins].astype(jnp.float32)
        for line in range(pack):
            turned = block[:, line * bins : (line + 1) * bins].reshape(parts * bins, -1).T
            turned = turned.astype(jnp.bfloat16)
            for low in range(0, turned.shape[0], group_lanes):
                pieces.append(
                    jnp.concatenate(
                        [turned[low : low + count], turned[low + count : low + 2 * count]], axis=1
                    )
                )
    return jnp.concatenate(pieces, axis=0)


CHUNKS = 2
SPANS = 2
UNROLL = 4


def whole_kernel(
    sizes,
    place,
    offsets_ref,
    filters_ref,
    signatures_ref,
    levels_ref,
    records_hbm,
    table_hbm,
    grid_hbm,
    cosine_hbm,
    sine_hbm,
    final_ref,
    left_ref,
    records_ref,
    table_ref,
    grid_ref,
    cosine_ref,
    sine_ref,
    row_ref,
    rows_ref,
    rim_ref,
    picks_ref,
    slot_table_ref,
    row_table_ref,
    adjoint_ref,
    forward_ref,
    select_ref,
    place_ref,
    traces_ref,
    field_ref,
    blocks_ref,
    rest_ref,
    head_ref,
    spill_ref,
    carried_ref,
    ahead_ref,
    sent_ref,
    got_ref,
    answer_ref,
    home_ref,
    reply_ref,
    raw_ref,
    other_raw_ref,
    other_rim_ref,
    other_blocks_ref,
    other_picks_ref,
    other_select_ref,
    other_traces_ref,
    other_sent_ref,
    load_sems,
    row_sends,
    row_recvs,
    go_sends,
    go_recvs,
    back_sends,
    back_recvs,
    rim_sends,
    rim_recvs,
    near_sends,
    near_recvs,
    raw_sems,
):
    slots, width = picks_ref.shape
    rcv, slab_len = records_ref.shape
    blocks = slab_len // width
    padded = blocks_ref.shape[0] // rcv
    chunks, _, samples = table_ref.shape
    steps = samples // width
    parts = place.size
    slab_count = place.shape[1]
    few = samples // 2 // parts // chunks
    quarter = rcv // 4
    early_spans = ((quarter, 2 * quarter), (2 * quarter, rcv))
    late_halves = ((0, 2 * quarter), (2 * quarter, rcv))
    late_spans = late_halves
    edge = head_ref.shape[1]
    all_rcv = rcv * place.shape[0]
    shot_count = offsets_ref.shape[1]
    row_count = slab_count
    capacity = slots // row_count
    wide = jnp.float32

    loads = [
        pltpu.make_async_copy(source, target, load_sems.at[number])
        for number, (source, target) in enumerate(
            (
                (records_hbm, records_ref),
                (table_hbm, table_ref),
                (grid_hbm, grid_ref),
                (cosine_hbm, cosine_ref),
                (sine_hbm, sine_ref),
            )
        )
    ]
    for load in loads:
        load.start()
    barrier = pltpu.get_barrier_semaphore()
    hops = neighbours(sizes)
    for hop in hops:
        pl.semaphore_signal(barrier, inc=1, device_id=device_at(sizes, hop)[0], device_id_type=MESH)
    mine = device_at(sizes, (0, 0, 0))[1]
    slab = lax.axis_index("shot") * sizes[2] + lax.axis_index("rep")
    last_slab = slab_count - 1

    def slab_device(shift):
        other = lax.rem(slab + shift + slab_count, slab_count)
        return {
            "shot": other // sizes[2],
            "rcv": lax.axis_index("rcv"),
            "rep": lax.rem(other, sizes[2]),
        }

    row_ref[...] = jnp.zeros_like(row_ref)
    row_ref[0:1, :shot_count] = offsets_ref[...]
    row_ref[1:2, :shot_count] = filters_ref[...]
    pl.semaphore_wait(barrier, len(hops))

    tile = row_ref.shape[0]
    here = pl.ds(pl.multiple_of(slab * tile, tile), tile)
    row_copies = []
    for hop in hops:
        if hop[1] == 0:
            number = len(row_copies)
            copy = pltpu.make_async_remote_copy(
                src_ref=row_ref,
                dst_ref=rows_ref.at[here],
                send_sem=row_sends.at[number],
                recv_sem=row_recvs.at[number],
                device_id=device_at(sizes, hop)[0],
                device_id_type=MESH,
            )
            copy.start()
            row_copies.append(copy)
    rows_ref[here] = row_ref[...]
    loads[0].wait()
    apart = slab_count // 2
    partner_slab = lax.rem(slab + apart, slab_count)
    partner = device_at(sizes, (sizes[0] // 2, 0, 0))[1]
    first_rim = pltpu.make_async_remote_copy(
        src_ref=records_ref.at[:, pl.ds(0, rim_ref.shape[1])],
        dst_ref=rim_ref,
        send_sem=rim_sends.at[SPANS, 0],
        recv_sem=rim_recvs.at[SPANS, 0],
        device_id=slab_device(-1),
        device_id_type=MESH,
    )
    partner_rim = pltpu.make_async_remote_copy(
        src_ref=records_ref.at[pl.ds(0, tile), pl.ds(0, rim_ref.shape[1])],
        dst_ref=other_rim_ref,
        send_sem=rim_sends.at[SPANS, 1],
        recv_sem=rim_recvs.at[SPANS, 1],
        device_id=slab_device(apart - 1),
        device_id_type=MESH,
    )

    @pl.when(slab > 0)
    def _():
        first_rim.start()
        partner_rim.start()

    for line in range(rcv):
        blocks_ref[line * padded + blocks : (line + 1) * padded] = jnp.zeros(
            (padded - blocks, width), wide
        )
    for block in range(blocks):
        blocks_ref[pl.ds(block, rcv, stride=padded), :] = records_ref[
            :, block * width : (block + 1) * width
        ]
    for line in range(quarter):
        raw_ref[line] = blocks_ref[line * padded : line * padded + blocks].astype(jnp.bfloat16)
    raw = pltpu.make_async_remote_copy(
        src_ref=raw_ref,
        dst_ref=other_raw_ref,
        send_sem=raw_sems.at[0],
        recv_sem=raw_sems.at[1],
        device_id=slab_device(apart),
        device_id_type=MESH,
    )
    raw.start()
    build_taps(signatures_ref, True, adjoint_ref)
    for copy in row_copies:
        copy.wait_recv()

    lane = lax.broadcasted_iota(jnp.int32, (row_count, width), 1)
    valid = lane < shot_count
    zero = jnp.zeros((row_count, width), jnp.int32)
    start_sample = jnp.where(valid, rows_ref[pl.ds(0, row_count, stride=tile), :], zero)
    signature = jnp.where(valid, rows_ref[pl.ds(1, row_count, stride=tile), :], zero)
    block_bits = width.bit_length() - 1
    slab_bits = slab_len.bit_length() - 1
    owner = lax.shift_right_logical(start_sample, slab_bits)
    rank = zero
    for step in range(1, shot_count):
        same = (pltpu.roll(owner, step, 1) == owner) & (lane >= step)
        rank = rank + same.astype(jnp.int32)
    key = jnp.where(valid, owner * capacity + rank + 1, zero)
    first_block = (lax.shift_right_logical(start_sample, block_bits) & (blocks - 1)).astype(wide)
    signature = signature.astype(wide)
    block_index = lax.broadcasted_iota(jnp.int32, (slots, padded), 1).astype(wide)

    def choose(owner_slab, into_picks_ref, into_select_ref):
        firsts, picks = [], []
        for level in range(capacity):
            taken = key == owner_slab * capacity + level + 1
            empty = jnp.zeros_like(first_block)
            firsts.append(
                jnp.sum(jnp.where(taken, first_block + 1.0, empty), axis=1, keepdims=True)
            )
            picks.append(jnp.sum(jnp.where(taken, signature, empty), axis=1, keepdims=True))
        firsts = jnp.broadcast_to(jnp.concatenate(firsts, axis=0), (slots, padded))
        firsts = jnp.where(firsts > 0.5, firsts - 1.0, -float(samples))
        into_picks_ref[...] = jnp.broadcast_to(jnp.concatenate(picks, axis=0), (slots, width))
        select = jnp.concatenate(
            [(block_index == firsts + float(step)).astype(wide) for step in range(steps)], axis=0
        )
        into_select_ref[...] = select.astype(jnp.bfloat16)
        return select

    select = choose(slab, picks_ref, select_ref)

    @pl.when(slab < last_slab)
    def _():
        first_rim.wait_recv()
        for step in range(rim_ref.shape[1] // width):
            blocks_ref[pl.ds(blocks + step, rcv, stride=padded), :] = rim_ref[
                :, step * width : (step + 1) * width
            ]

    loads[1].wait()

    def exchange(source, target, send_sems, recv_sems, low, rows):
        made = []
        where = pl.ds(low, rows)
        for number, hop in enumerate(hops):
            device, index = device_at(sizes, hop)
            copy = pltpu.make_async_remote_copy(
                src_ref=source.at[index, where],
                dst_ref=target.at[mine, where],
                send_sem=send_sems.at[number],
                recv_sem=recv_sems.at[number],
                device_id=device,
                device_id_type=MESH,
            )
            copy.start()
            made.append(copy)
        target[mine, where] = source[mine, where]
        return made

    def correlate_span(span, from_ref, model, one_select_ref, one_picks_ref, into_ref):
        def one(line, carry):
            correlate_line(
                line, padded, one_select_ref, from_ref, adjoint_ref, one_picks_ref, model, into_ref
            )
            return carry

        lax.fori_loop(span[0], span[1], one, 0, unroll=UNROLL)

    def span_spectra(span, chunk):
        spectra_chunk(table_ref[chunk], traces_ref, sent_ref.at[chunk], range(*span), rcv, slots)

    def span_exchange(number, span, chunk):
        return exchange(
            sent_ref.at[chunk],
            got_ref.at[chunk],
            go_sends.at[number, chunk],
            go_recvs.at[number, chunk],
            span[0] * few,
            (span[1] - span[0]) * few,
        )

    def send_span(number, span):
        made = []
        for chunk in range(chunks):
            span_spectra(span, chunk)
            made.append(span_exchange(number, span, chunk))
        return made

    def send_near(number, from_ref, one_select_ref, one_picks_ref, into_ref, out_ref, owner):
        span = (0, quarter)
        correlate_span(span, from_ref, None, one_select_ref, one_picks_ref, into_ref)
        where = pl.ds(0, quarter * few)
        depth, place_x, core = (lax.axis_index(axis) for axis in AXES)
        made = []
        for chunk in range(chunks):
            spectra_chunk(
                table_ref[chunk], into_ref, out_ref.at[chunk], range(*span), rcv, slots
            )
            copies = []
            for hop in range(1, 8):
                spot = (
                    depth + (hop // 4) * (1 - 2 * lax.rem(depth, 2)),
                    lax.rem(place_x + hop // 2 % 2, sizes[1]),
                    lax.rem(core + hop % 2, sizes[2]),
                )
                index = (spot[0] * sizes[1] + spot[1]) * sizes[2] + spot[2]
                copy = pltpu.make_async_remote_copy(
                    src_ref=out_ref.at[chunk, index, where],
                    dst_ref=got_ref.at[chunk, owner, where],
                    send_sem=near_sends.at[number, chunk, hop - 1],
                    recv_sem=near_recvs.at[number, chunk, hop - 1],
                    device_id=dict(zip(AXES, spot)),
                    device_id_type=MESH,
                )
                copy.start()
                copies.append(copy)
            got_ref[chunk, owner, where] = out_ref[chunk, mine, where]
            made.append(copies)
        return made

    def level_at(index, chunk):
        return level_of(levels_ref, index, (mine * chunks + chunk) * few, few, all_rcv)

    first_span, second_span = early_spans
    correlate_span(first_span, blocks_ref, None, select_ref, picks_ref, traces_ref)
    going = [send_span(0, first_span), []]
    going.append(send_near(0, blocks_ref, select_ref, picks_ref, traces_ref, sent_ref, mine))
    correlate_span(second_span, blocks_ref, None, select_ref, picks_ref, traces_ref)
    for chunk in range(chunks):
        span_spectra(second_span, chunk)
        if chunk == 0:
            going[1].append(span_exchange(1, second_span, chunk))

    choose(partner_slab, other_picks_ref, other_select_ref)
    raw.wait_recv()
    for line in range(quarter):
        other_blocks_ref[line * padded : line * padded + blocks] = other_raw_ref[line].astype(wide)
        other_blocks_ref[line * padded + blocks : (line + 1) * padded] = jnp.zeros(
            (padded - blocks, width), wide
        )

    @pl.when(partner_slab < last_slab)
    def _():
        partner_rim.wait_recv()
        for step in range(rim_ref.shape[1] // width):
            other_blocks_ref[pl.ds(blocks + step, quarter, stride=padded), :] = other_rim_ref[
                :quarter, step * width : (step + 1) * width
            ]

    going.append(
        send_near(
            1, other_blocks_ref, other_select_ref, other_picks_ref, other_traces_ref, other_sent_ref, partner
        )
    )
    for chunk in range(1, chunks):
        going[1].append(span_exchange(1, second_span, chunk))
    place_ref[...] = select.T.astype(jnp.bfloat16)
    build_taps(signatures_ref, False, forward_ref)
    repeated = key
    for shift in range(shot_count, width, shot_count):
        repeated = repeated + pltpu.roll(key, shift, 1)
    points = row_count * shot_count
    repeated = jnp.concatenate([repeated] * (points // width), axis=1)
    point = lax.broadcasted_iota(jnp.int32, (row_count, points), 1)
    row = lax.broadcasted_iota(jnp.int32, (row_count, points), 0)
    shot_bits = shot_count.bit_length() - 1
    repeated = jnp.where(lax.shift_right_logical(point, shot_bits) == row, repeated, 0)
    chosen = jnp.concatenate(
        [(repeated == number + 1).astype(wide) for number in range(slab_count * capacity)], axis=0
    ).astype(jnp.bfloat16)
    for load in loads[2:]:
        load.wait()
    for half in range(2):
        for number in range(row_count):
            low = (2 * number + half) * shot_count
            source = half * points + number * shot_count
            row_table_ref[low : low + shot_count] = grid_ref[source : source + shot_count]
        part = dot(chosen, grid_ref[half * points : (half + 1) * points]).astype(jnp.bfloat16)
        for number in range(slab_count):
            low = (2 * number + half) * slots
            slot_table_ref[low : low + slots] = part[number * slots : (number + 1) * slots]

    coming = {}

    def send_back(number, chunk):
        span = late_halves[number]
        coming[number, chunk] = exchange(
            answer_ref.at[chunk],
            home_ref.at[chunk],
            back_sends.at[number, chunk],
            back_recvs.at[number, chunk],
            span[0] * few,
            (span[1] - span[0]) * few,
        )

    for chunk in range(chunks):
        for made in going:
            for copy in made[chunk]:
                copy.wait_recv()
        bins_chunk(
            place, 1, got_ref.at[chunk], slot_table_ref, slot_table_ref, cosine_ref[...], sine_ref[...], level_at(0, chunk), answer_ref.at[chunk]
        )
        send_back(0, chunk)
    send_back(1, 0)
    for copy in row_copies:
        copy.wait_send()

    raw.wait_send()

    @pl.when(slab > 0)
    def _():
        first_rim.wait_send()
        partner_rim.wait_send()

    for made in going:
        for chunk in made:
            for copy in chunk:
                copy.wait_send()

    def halo(number):
        low, high = late_spans[number]
        where = pl.ds(low, high - low)
        onward = pltpu.make_async_remote_copy(
            src_ref=spill_ref.at[where],
            dst_ref=carried_ref.at[where],
            send_sem=rim_sends.at[number, 0],
            recv_sem=rim_recvs.at[number, 0],
            device_id=slab_device(1),
            device_id_type=MESH,
        )
        backward = pltpu.make_async_remote_copy(
            src_ref=head_ref.at[where],
            dst_ref=ahead_ref.at[where],
            send_sem=rim_sends.at[number, 1],
            recv_sem=rim_recvs.at[number, 1],
            device_id=slab_device(-1),
            device_id_type=MESH,
        )
        return onward, backward

    def subtract(number):
        low, high = late_spans[number]
        together = math.gcd(high - low, 4)
        for chunk in range(chunks):
            for copy in coming[number, chunk]:
                copy.wait_recv()
            for first in range(low, high, together):
                where = slice(first * slots, (first + together) * slots)
                lines = range(first, first + together)
                field = dot(upright(home_ref, chunk, lines, few, 2 * slots), table_ref[chunk])
                if chunk:
                    field = field + field_ref[where]
                field_ref[where] = field

        def one(line, carry):
            blended = blend_line(line, place_ref, field_ref, forward_ref, picks_ref)
            start = pl.multiple_of(line * padded, 8)
            left = blocks_ref[pl.ds(start, blocks)] - blended[:blocks]
            rest_ref[pl.ds(start, blocks)] = left
            rest_ref[pl.ds(start + blocks, padded - blocks)] = jnp.zeros(
                (padded - blocks, width), wide
            )
            head_ref[line] = left[:edge]
            spill_ref[line] = blended[blocks : blocks + edge]
            return carry

        lax.fori_loop(low, high, one, 0, unroll=UNROLL)
        onward, backward = halo(number)

        @pl.when(slab < last_slab)
        def _():
            onward.start()

        @pl.when(slab > 0)
        def _():
            backward.start()

    def correlate_rest(number):
        low, high = late_spans[number]
        onward, backward = halo(number)

        @pl.when(slab > 0)
        def _():
            onward.wait_recv()
            for line in range(low, high):
                here = pl.ds(line * padded, edge)
                rest_ref[here] = rest_ref[here] - carried_ref[line]

        @pl.when(slab < last_slab)
        def _():
            backward.wait_recv()
            for line in range(low, high):
                rest_ref[pl.ds(line * padded + blocks, edge)] = ahead_ref[line] - spill_ref[line]
            onward.wait_send()

        @pl.when(slab > 0)
        def _():
            backward.wait_send()

        correlate_span((low, high), rest_ref, field_ref, select_ref, picks_ref, traces_ref)

    again = [[], []]
    subtract(0)
    for chunk in range(1, chunks):
        send_back(1, chunk)
    correlate_rest(0)
    span_spectra(late_halves[0], 0)
    again[0].append(span_exchange(0, late_halves[0], 0))
    for chunk in range(1, chunks):
        span_spectra(late_halves[0], chunk)
    subtract(1)
    for chunk in range(1, chunks):
        again[0].append(span_exchange(0, late_halves[0], chunk))
    correlate_rest(1)
    again[1] = send_span(1, late_halves[1])

    for block in range(blocks):
        left_ref[:, block * width : (block + 1) * width] = rest_ref[
            pl.ds(block, rcv, stride=padded), :
        ]
    for made in coming.values():
        for copy in made:
            copy.wait_send()
    final = []
    for chunk in range(chunks):
        for made in again:
            for copy in made[chunk]:
                copy.wait_recv()
        bins_chunk(
            place, 2, got_ref.at[chunk], slot_table_ref, row_table_ref, cosine_ref[...], sine_ref[...], level_at(1, chunk), reply_ref.at[chunk]
        )
        final.append(
            exchange(
                reply_ref.at[chunk], final_ref.at[chunk], back_sends.at[0, chunk], back_recvs.at[0, chunk], 0, reply_ref.shape[2]
            )
        )
    for made in again:
        for chunk in made:
            for copy in chunk:
                copy.wait_send()
    for made in final:
        for copy in made:
            copy.wait()


def finish_kernel(bins, spectra_ref, left_ref, table_ref, model_ref, out_ref, sem):
    chunks = spectra_ref.shape[0]
    groups, together, count, _ = model_ref.shape
    step = pl.program_id(0)
    copy = pltpu.make_async_copy(left_ref, out_ref, sem)

    @pl.when(step == 0)
    def _():
        copy.start()

    fields = sum(
        dot(upright(spectra_ref, chunk, range(together), bins, 2 * count), table_ref[chunk])
        for chunk in range(chunks)
    )
    for line in range(together):
        for group in range(groups):
            low = (line * groups + group) * count
            model_ref[group, line] = fields[low : low + count]

    @pl.when(step == pl.num_programs(0) - 1)
    def _():
        copy.wait()


def finish(spectra, left, table, groups, rcv):
    chunks, parts, rows, lanes = spectra.shape
    samples = table.shape[2]
    bins = rows // rcv
    count = lanes // 2 // groups
    together = math.gcd(rcv, 4)
    whole = pl.BlockSpec(memory_space=pltpu.VMEM)
    return pl.pallas_call(
        functools.partial(finish_kernel, bins),
        grid=(rcv // together,),
        out_shape=(
            jax.ShapeDtypeStruct((groups, rcv, count, samples), jnp.float32),
            jax.ShapeDtypeStruct(left.shape, jnp.float32),
        ),
        in_specs=[
            pl.BlockSpec((chunks, parts, together * bins, lanes), lambda i: (0, 0, i, 0)),
            whole,
            whole,
        ],
        out_specs=(
            pl.BlockSpec((groups, together, count, samples), lambda i: (0, i, 0, 0)),
            pl.BlockSpec(memory_space=pl.ANY),
        ),
        scratch_shapes=[pltpu.SemaphoreType.DMA],
        compiler_params=pltpu.CompilerParams(vmem_limit_bytes=16 * 2**20),
    )(spectra, left, table)


def body_by_slots(records, offsets, filter_index, signatures, thresholds):
    rows_here, shot_count = offsets.shape
    local_rcv, slab_len = records.shape
    slab_count = lax.axis_size(("shot", "rep"))
    rep_count = lax.axis_size("rep")
    rcv_count = lax.axis_size("rcv")
    sizes = tuple(lax.axis_size(axis) for axis in AXES)
    parts = slab_count * rcv_count
    tap_count = signatures.shape[1]
    slab_blocks = slab_len // tap_count
    steps = NT // tap_count
    capacity = max(2, 2 * shot_count // slab_count)
    row_count = rows_here * slab_count
    slots = row_count * capacity
    bins = NT // 2 // parts
    chunks = CHUNKS
    few = bins // chunks
    place = np.array(
        [
            [((slab // rep_count) * rcv_count + line) * rep_count + slab % rep_count for slab in range(slab_count)]
            for line in range(rcv_count)
        ]
    )

    time_table_fixed = fixed_time_table(NT).reshape(2, parts, chunks, few, NT)
    time_table_fixed = jnp.asarray(
        np.ascontiguousarray(time_table_fixed.transpose(2, 0, 1, 3, 4)).reshape(chunks, NT // chunks, NT)
    )
    table_x, table_y, table_r = (
        fixed_shot_table(count) for count in (row_count, shot_count, local_rcv * rcv_count)
    )
    grid_table = np.einsum("ajby,bkcx->cxyakj", table_y, table_x).astype(jnp.bfloat16)
    points = 2 * row_count * shot_count
    grid_table = jnp.asarray(grid_table.reshape(points, points))
    same = np.eye(few, dtype=np.float32)
    cosine = jnp.asarray(np.kron(table_r[0, :, 0], same).astype(jnp.bfloat16))
    sine = jnp.asarray(np.kron(table_r[0, :, 1], same).astype(jnp.bfloat16))

    edge = 8
    padded = slab_blocks + 2 * edge
    vmem = pl.BlockSpec(memory_space=pltpu.VMEM)
    anywhere = pl.BlockSpec(memory_space=pl.ANY)
    rows = local_rcv * few
    table_width = tap_count * signatures.shape[0]
    low, wide = jnp.bfloat16, jnp.float32
    big = (records, time_table_fixed, grid_table, cosine, sine)
    spectra, residual = pl.pallas_call(
        functools.partial(whole_kernel, sizes, place),
        out_shape=(
            pltpu.VMEM((chunks, parts, rows // 2, 4 * shot_count), low),
            pltpu.VMEM(records.shape, wide),
        ),
        in_specs=[vmem] * 4 + [anywhere] * len(big),
        out_specs=(vmem, vmem),
        scratch_shapes=[pltpu.VMEM(array.shape, array.dtype) for array in big]
        + [
            pltpu.VMEM((edge, tap_count), jnp.int32),
            pltpu.VMEM((slab_count * edge, tap_count), jnp.int32),
            pltpu.VMEM((local_rcv, (steps - 1) * tap_count), wide),
            pltpu.VMEM((slots, tap_count), wide),
            pltpu.VMEM((slab_count * 2 * slots, points), low),
            pltpu.VMEM((points, points), low),
            pltpu.VMEM((2 * tap_count, table_width), low),
            pltpu.VMEM((2 * tap_count, table_width), low),
            pltpu.VMEM((slots * steps, padded), low),
            pltpu.VMEM((padded, slots * steps), low),
            pltpu.VMEM((local_rcv * slots, NT), low),
            pltpu.VMEM((local_rcv * slots, NT), wide),
            pltpu.VMEM((local_rcv * padded, tap_count), wide),
            pltpu.VMEM((local_rcv * padded, tap_count), wide),
        ]
        + [pltpu.VMEM((local_rcv, edge, tap_count), wide)] * 4
        + [pltpu.VMEM((chunks, parts, rows, 2 * slots), low)] * 4
        + [
            pltpu.VMEM((chunks, parts, rows // 2, 4 * shot_count), low),
            pltpu.VMEM((local_rcv // 4, slab_blocks, tap_count), low),
            pltpu.VMEM((local_rcv // 4, slab_blocks, tap_count), low),
            pltpu.VMEM((edge, (steps - 1) * tap_count), wide),
            pltpu.VMEM((local_rcv // 4 * padded, tap_count), wide),
            pltpu.VMEM((slots, tap_count), wide),
            pltpu.VMEM((slots * steps, padded), low),
            pltpu.VMEM((local_rcv // 4 * slots, NT), low),
            pltpu.VMEM((chunks, parts, rows, 2 * slots), low),
        ]
        + [pltpu.SemaphoreType.DMA((len(big),))]
        + [pltpu.SemaphoreType.DMA((slab_count - 1,))] * 2
        + [pltpu.SemaphoreType.DMA((2, chunks, parts - 1))] * 4
        + [pltpu.SemaphoreType.DMA((SPANS + 1, 2))] * 2
        + [pltpu.SemaphoreType.DMA((2, chunks, parts // 2 - 1))] * 2
        + [pltpu.SemaphoreType.DMA((2,))],
        compiler_params=pltpu.CompilerParams(
            collective_id=0, has_side_effects=True, vmem_limit_bytes=60 * 2**20
        ),
    )(offsets, filter_index, signatures, thresholds, *big)
    model, residual = finish(spectra, residual, time_table_fixed, 2, local_rcv // 2)
    return (model.reshape(rows_here, local_rcv, shot_count, NT), residual)


def body(records, offsets, filter_index, signatures, thresholds):
    rows_here, shot_count = offsets.shape
    slab_count = lax.axis_size(("shot", "rep"))
    parts = slab_count * lax.axis_size("rcv")
    slots = rows_here * slab_count * max(2, 2 * shot_count // slab_count)
    table_rows = 2 * rows_here * slab_count * shot_count
    fits = table_rows <= 1024 and rows_here == 1 and slots == 64 and 4 * shot_count == 128
    fits = fits and records.shape[0] == 16 and NT // 2 // parts == 16
    slab_len, tap_count = records.shape[1], signatures.shape[1]
    fits = fits and tap_count == 128 and slab_len & (slab_len - 1) == 0
    fits = fits and tuple(lax.axis_size(axis) for axis in AXES) == (4, 2, 2)
    run = body_by_slots if fits else body_by_rows
    return run(records, offsets, filter_index, signatures, thresholds)


def solution(mesh):
    in_specs = (
        P(("groups", "rcv"), ("shot", "rep")),
        P(("groups", "shot", "rep"), None),
        P(("groups", "shot", "rep"), None),
        P(),
        P(),
    )
    out_specs = (
        P(("groups", "shot", "rep"), "rcv", None, None),
        P(("groups", "rcv"), ("shot", "rep")),
    )
    return jax.shard_map(body, mesh=mesh, in_specs=in_specs, out_specs=out_specs, check_vma=False)
```
